32 devices in a mesh: fsdp: 8 (over z, y), dp: 4 (over x, core).
Axes of the slice: x: 2, y: 2, z: 4, core: 2. Of those that a mesh axis runs over, the one named last changes fastest.
Arguments:
- inputs: float32 [32768, 768], P(('fsdp', 'dp')), may hold values from -6 to 6
- cotangent: float32 [32768, 768], P(('fsdp', 'dp')), may hold values from -6 to 6
- timesteps: int32 [256], P(('fsdp', 'dp')), may hold values from 0 to 999
- layouts: int32 [128], P(('fsdp', 'dp')), may hold values 0 or 1
- step_table: float32 [1000, 768], P(None, 'fsdp'), may hold values from -6 to 6
- first_gain: float32 [768], P('fsdp'), may hold values from 0.25 to 1.75
- first_shift: float32 [768], P('fsdp'), may hold values from -3 to 3
- query_matrix: float32 [768, 768], P('fsdp'), may hold values from -0.21875 to 0.21875
- query_bias: float32 [768], P('fsdp'), may hold values from -3 to 3
- key_matrix: float32 [768, 768], P('fsdp'), may hold values from -0.21875 to 0.21875
- value_matrix: float32 [768, 768], P('fsdp'), may hold values from -0.21875 to 0.21875
- value_bias: float32 [768], P('fsdp'), may hold values from -3 to 3
- out_matrix: float32 [768, 768], P('fsdp'), may hold values from -1.25 to 1.25
- out_bias: float32 [768], P('fsdp'), may hold values from -3 to 3
- second_gain: float32 [768], P('fsdp'), may hold values from 0.25 to 1.75
- second_shift: float32 [768], P('fsdp'), may hold values from -3 to 3
- up_matrix: float32 [768, 3072], P(None, 'fsdp'), may hold values from -0.21875 to 0.21875
- up_bias: float32 [3072], P('fsdp'), may hold values from -3 to 3
- down_matrix: float32 [3072, 768], P('fsdp'), may hold values from -0.109375 to 0.109375
- down_bias: float32 [768], P('fsdp'), may hold values from -3 to 3
Outputs:
- block_output: float32 [32768, 768], P(('fsdp', 'dp'))
- input_grad: float32 [32768, 768], P(('fsdp', 'dp'))
- table_grad: float32 [1000, 768], P(None, 'fsdp')
- first_gain_grad: float32 [768], P('fsdp')
- first_shift_grad: float32 [768], P('fsdp')
- query_matrix_grad: float32 [768, 768], P('fsdp')
- query_bias_grad: float32 [768], P('fsdp')
- key_matrix_grad: float32 [768, 768], P('fsdp')
- value_matrix_grad: float32 [768, 768], P('fsdp')
- value_bias_grad: float32 [768], P('fsdp')
- out_matrix_grad: float32 [768, 768], P('fsdp')
- out_bias_grad: float32 [768], P('fsdp')
- second_gain_grad: float32 [768], P('fsdp')
- second_shift_grad: float32 [768], P('fsdp')
- up_matrix_grad: float32 [768, 3072], P(None, 'fsdp')
- up_bias_grad: float32 [3072], P('fsdp')
- down_matrix_grad: float32 [3072, 768], P('fsdp')
- down_bias_grad: float32 [768], P('fsdp')
The draws below stay inside these ranges and needn't reach their ends.
Inputs may be any that keep to these rules, and one draw needn't show every extreme that they name: A window with layouts 1 holds one sequence of 256 tokens that takes the timestep of its first slot; a window with layouts 0 holds two sequences of 128 tokens, one a slot.
All inputs are finite; a program needn't handle non-finite values. No bound on the sum of `layouts` on one device may be relied on, other than what follows from the above.
Results may differ from the reference program's by a relative error of at most 0.015.
The reference program's roundings to bfloat16 on the way count: a program that leaves them out, or rounds other values in their place, can miss the bound.
Values may be sent and summed in bfloat16 or wider, within the bound.
No kernel may reach another device: no remote copies, remote signals or barrier semaphores. Data moves between devices by JAX's collectives and lax.ppermute only.
A program may use at most 192 MiB of HBM per device.

```python
import math
import jax
import jax.numpy as jnp
from jax import lax

D = 768
HEADS = 12
HEAD = 64
FF = 3072
TSTEPS = 1000
WINDOW = 256
SHORT = 128
WINDOWS = 128
SLOTS = 256
TOKENS = 32768


def set_ends(drawn, rng, least, largest):
    longest = drawn.shape.index(max(drawn.shape))
    spots = []
    for shift in (0, 1):
        where = [jax.random.randint(jax.random.fold_in(rng, axis), (), 0, length) for axis, length in enumerate(drawn.shape)]
        where[longest] = (where[longest] + shift) % drawn.shape[longest]
        spots.append(tuple(where))
    return drawn.at[spots[0]].set(least).at[spots[1]].set(largest)


def level_of(own_key, extent, pieces, smallest, largest):
    def one(axis_at, shards_of):
        heights = jax.random.uniform(jax.random.fold_in(jax.random.fold_in(own_key, 6), axis_at), (shards_of,), jnp.float32, smallest / len(pieces), largest / len(pieces))
        return jnp.repeat(jnp.exp(heights), extent[axis_at] // shards_of).reshape((-1,) + (1,) * (len(extent) - axis_at - 1))

    level = one(*pieces[0])
    for cut in pieces[1:]:
        level = level * one(*cut)
    return level


def scatter_about(stream_key, dims, deviation, most, pieces=(), kind=jnp.bfloat16):
    values = jax.random.normal(stream_key, dims, jnp.float32) * deviation
    if len(pieces) > 0:
        values = level_of(stream_key, dims, pieces, -0.22, 0.18) * values
    return jnp.clip(values, min=-most, max=most).astype(kind)


def setup_inputs(seed: int = 0) -> dict:
    key_list = jax.random.split(jax.random.key(seed), 21)
    return {
        "inputs": scatter_about(key_list[0], (TOKENS, D), 1.0, 6.0, ((0, 32),), jnp.float32),
        "cotangent": scatter_about(key_list[1], (TOKENS, D), 1.0, 6.0, ((0, 32),), jnp.float32),
        "timesteps": set_ends(jax.random.randint(key_list[2], (SLOTS,), 0, TSTEPS), jax.random.fold_in(key_list[2], 1), 0, TSTEPS - 1).astype(jnp.int32),
        "layouts": set_ends((jax.random.randint(key_list[3], (WINDOWS,), 0, 2) < 1).astype(jnp.int32), jax.random.fold_in(key_list[3], 1), 0, 1),
        "step_table": scatter_about(key_list[4], (TSTEPS, D), 1.0, 6.0, ((1, 8),), jnp.float32),
        "first_gain": jnp.clip(1.0 + 0.15 * jax.random.normal(key_list[5], (D,), jnp.float32), 0.25, 1.75),
        "first_shift": scatter_about(key_list[6], (D,), 0.5, 3.0, ((0, 8),), jnp.float32),
        "query_matrix": scatter_about(key_list[7], (D, D), D ** -0.5, 0.21875, ((0, 8),), jnp.float32),
        "query_bias": scatter_about(key_list[8], (D,), 0.5, 3.0, ((0, 8),), jnp.float32),
        "key_matrix": scatter_about(key_list[9], (D, D), D ** -0.5, 0.21875, ((0, 8),), jnp.float32),
        "value_matrix": scatter_about(key_list[10], (D, D), D ** -0.5, 0.21875, ((0, 8),), jnp.float32),
        "value_bias": scatter_about(key_list[11], (D,), 0.5, 3.0, ((0, 8),), jnp.float32),
        "out_matrix": scatter_about(key_list[12], (D, D), (D // 32) ** -0.5, 1.25, ((0, 8),), jnp.float32),
        "out_bias": scatter_about(key_list[13], (D,), 0.5, 3.0, ((0, 8),), jnp.float32),
        "second_gain": jnp.clip(1.0 + 0.15 * jax.random.normal(key_list[14], (D,), jnp.float32), 0.25, 1.75),
        "second_shift": scatter_about(key_list[15], (D,), 0.5, 3.0, ((0, 8),), jnp.float32),
        "up_matrix": scatter_about(key_list[16], (D, FF), D ** -0.5, 0.21875, ((1, 8),), jnp.float32),
        "up_bias": scatter_about(key_list[17], (FF,), 0.5, 3.0, ((0, 8),), jnp.float32),
        "down_matrix": scatter_about(key_list[18], (FF, D), FF ** -0.5, 0.109375, ((0, 8),), jnp.float32),
        "down_bias": scatter_about(key_list[19], (D,), 0.5, 3.0, ((0, 8),), jnp.float32),
    }


@jax.custom_vjp
def low(v):
    return lax.optimization_barrier(v.astype(jnp.bfloat16)).astype(jnp.float32)

@jax.custom_vjp
def low_back(v):
    return v

def low_keep(v):
    return (low(v), None)

def low_pass(kept, grad):
    return (grad,)

def back_keep(v):
    return (v, None)

def back_low(kept, grad):
    return (low(grad),)
low.defvjp(low_keep, low_pass)
low_back.defvjp(back_keep, back_low)

def product(left_side, right_side):
    return jnp.dot(left_side, right_side, precision=lax.Precision.HIGHEST, preferred_element_type=jnp.float32)

def norm_rows(values, gain_row, shift_row):
    centred = values - lax.optimization_barrier(jnp.mean(values, axis=-1, keepdims=True))
    spread = lax.optimization_barrier(jnp.mean(centred * centred, axis=-1, keepdims=True))
    return centred * lax.rsqrt(spread + 1e-05) * gain_row + shift_row

def attend_windows(bundle):
    query_rows, key_rows, value_rows, layout = bundle
    scores = jnp.einsum('gqhe,gkhe->ghqk', query_rows, key_rows, precision=lax.Precision.HIGHEST) * (1.0 / math.sqrt(HEAD))
    scores = low_back(scores)
    places = jnp.arange(WINDOW) // SHORT
    same_half = places[:, None] == places[None, :]
    allowed = same_half[None, :, :] | (layout[:, None, None] == 1)
    scores = jnp.where(allowed[:, None, :, :], scores, -1e+30)
    weights = low(jax.nn.softmax(scores, axis=-1))
    mixture = jnp.einsum('ghqk,gkhe->gqhe', weights, value_rows, precision=lax.Precision.HIGHEST)
    return low(low_back(mixture))

def forward(layer_in, timesteps, layouts, params):
    lowered = [low(member) for member in params]
    full_table, gain_one, shift_one, query_full, query_add, key_full, value_full, value_add, out_full, out_add, gain_two, shift_two, up_full, up_add, down_full, down_add = lowered
    row_index = jnp.arange(TOKENS).astype(jnp.int32)
    window_index = row_index // WINDOW
    slot_index = jnp.where(layouts[window_index] == 1, 2 * window_index, row_index // SHORT)
    stamped = layer_in + full_table[timesteps[slot_index]]
    normed = low(norm_rows(stamped, gain_one, shift_one))
    query_low = low(low_back(product(normed, query_full) + query_add))
    key_low = low(low_back(product(normed, key_full)))
    value_low = low(low_back(product(normed, value_full) + value_add))
    group_size = math.gcd(WINDOWS, max(1, 4096 // WINDOW))
    groups = WINDOWS // group_size
    shaped = (groups, group_size, WINDOW, HEADS, HEAD)
    mixture = lax.map(jax.checkpoint(attend_windows), (query_low.reshape(shaped), key_low.reshape(shaped), value_low.reshape(shaped), layouts.reshape(groups, group_size)))
    mixture = mixture.reshape(TOKENS, D)
    attended = stamped + low_back(product(mixture, out_full)) + out_add
    normed_two = low(norm_rows(attended, gain_two, shift_two))
    hidden_pre = low_back(product(normed_two, up_full) + up_add)
    hidden = low(jax.nn.gelu(hidden_pre, approximate=False))
    return attended + low_back(product(hidden, down_full)) + down_add

def reference(inputs, cotangent, timesteps, layouts, step_table, first_gain, first_shift, query_matrix, query_bias, key_matrix, value_matrix, value_bias, out_matrix, out_bias, second_gain, second_shift, up_matrix, up_bias, down_matrix, down_bias):
    params = (step_table, first_gain, first_shift, query_matrix, query_bias, key_matrix, value_matrix, value_bias, out_matrix, out_bias, second_gain, second_shift, up_matrix, up_bias, down_matrix, down_bias)

    def apply_layer(layer_in, param_list):
        return forward(layer_in, timesteps, layouts, param_list)
    output, pullback = jax.vjp(apply_layer, inputs, params)
    input_grad, grads = pullback(cotangent)
    return (output, input_grad, grads[0], grads[1], grads[2], grads[3], grads[4], grads[5], grads[6], grads[7], grads[8], grads[9], grads[10], grads[11], grads[12], grads[13], grads[14], grads[15])
```

```python
import functools
import math

import jax
import jax.numpy as jnp
from jax import lax
from jax.experimental import pallas as pl
from jax.experimental.pallas import tpu as pltpu
from jax.sharding import PartitionSpec as P

HEADS = 12
HEAD = 64
D = HEADS * HEAD
F32 = jnp.float32
BF16 = jnp.bfloat16
ANY = pl.BlockSpec(memory_space=pl.ANY)
SMEM = pl.BlockSpec(memory_space=pltpu.SMEM)
PARAMS = pltpu.CompilerParams(vmem_limit_bytes=60 * 1024 * 1024)

TAIL_P = 0.21
TAIL = (
    0.08371157580586816,
    0.08506885523539415,
    0.06919219089790565,
    0.12487264009661635,
    -0.09392498913162721,
    0.349400678909721,
    -0.33025308461653297,
    0.2835884168453487,
    -0.07165627723466013,
)

GAIN1, SHIFT1, QADD, VADD, OADD, GAIN2, SHIFT2, DADD, UADD = range(9)


def whole(shape):
    return pl.BlockSpec(shape, lambda *_: (0,) * len(shape))


def sds(shape, dtype):
    return jax.ShapeDtypeStruct(shape, dtype)


def mm(a, b, ca=1, cb=0):
    return lax.dot_general(a, b, (((ca,), (cb,)), ((), ())), preferred_element_type=F32)


def place(scal, buf, other, k):
    f, p = scal[0], scal[1]
    y, z, c, x = f & 1, f >> 1, p & 1, p >> 1
    core = c ^ other
    by_y = 1 - core if buf == 1 else core if buf == 2 else buf // 3
    by_x = core if buf == 1 else 1 - core if buf == 2 else buf // 3
    return ((z ^ k) << 1) | (y ^ by_y), ((x ^ by_x) << 1) | core


def fetch(scal, refs, dst, sem, row=0, rows=0, columns=False):
    if len(refs) == 1:
        pltpu.make_async_copy(refs[0], dst, sem).start()
        return
    for other in range(2):
        for buf in range(4):
            for k in range(4):
                f, p = place(scal, buf, other, k)
                src = refs[other * 4 + buf].at[k]
                if columns:
                    half = D // 2
                    for part in range(2):
                        r = pl.multiple_of(p * 2 * rows + part * rows, 8)
                        pltpu.make_async_copy(
                            src.at[pl.ds(row, rows), pl.ds(part * half, half)],
                            dst.at[pl.ds(r, rows), pl.ds(pl.multiple_of(f * half, 128), half)],
                            sem,
                        ).start()
                else:
                    r = pl.multiple_of((f * 4 + p) * rows, 8)
                    pltpu.make_async_copy(
                        src.at[pl.ds(row, rows), :], dst.at[pl.ds(r, rows), :], sem
                    ).start()


def arrive(dst, sem):
    pltpu.make_async_copy(dst, dst, sem).wait()


def prep_body(scal, *refs):
    vecs, (q, k, v, o, up, down), (one, two, three) = refs[:9], refs[9:15], refs[15:]
    up_add = vecs[8][...]
    left = jnp.concatenate([r[...] for r in vecs[:8]], axis=0)
    left = jnp.concatenate([left, jnp.zeros((8, D // 2 - left.shape[1]), F32)], axis=1)
    right = jnp.concatenate([up_add, jnp.zeros((7, D // 2), F32)], axis=0)
    one[0:8, :] = jnp.concatenate([left, right], axis=1).astype(BF16)
    r = q.shape[0]
    for i, m in enumerate((q, k, v)):
        one[8 + i * r : 8 + (i + 1) * r, :] = m[...].astype(BF16)
    two[0:r, :] = o[...].astype(BF16)
    u = up.shape[0] // 2
    two[r : r + u, 0 : D // 2] = up[0:u, :].astype(BF16)
    two[r : r + u, D // 2 : D] = up[u : 2 * u, :].astype(BF16)
    three[...] = down[...].astype(BF16)


def prep(scal, vecs, mats):
    q, up, down = mats[0], mats[4], mats[5]
    r, u, d = q.shape[0] // 4, up.shape[0] // 4, down.shape[0] // 4
    half = up.shape[1]
    mine = lambda rows, cols: pl.BlockSpec((rows, cols), lambda i, s: (s[1], 0))
    vecs = [v.reshape(1, -1) for v in vecs]
    return pl.pallas_call(
        prep_body,
        grid_spec=pltpu.PrefetchScalarGridSpec(
            num_scalar_prefetch=1,
            grid=(1,),
            in_specs=[pl.BlockSpec(v.shape, lambda i, s: (0, 0)) for v in vecs]
            + [mine(r, D)] * 4
            + [mine(u, half), mine(d, D)],
            out_specs=[
                pl.BlockSpec(s, lambda i, s_: (0, 0))
                for s in ((8 + 3 * r, D), (r + u // 2, D), (d, D))
            ],
        ),
        out_shape=(sds((8 + 3 * r, D), BF16), sds((r + u // 2, D), BF16), sds((d, D), BF16)),
        compiler_params=PARAMS,
    )(scal, *vecs, *mats)


def normal_rows(v):
    c = v - jnp.mean(v, axis=-1, keepdims=True)
    r = lax.rsqrt(jnp.mean(c * c, axis=-1, keepdims=True) + 1e-05)
    return c * r, r


def stamp(x, slots, i):
    half = x.shape[0] // 2
    return jnp.concatenate(
        [x[:half] + slots[pl.ds(2 * i, 1), :], x[half:] + slots[pl.ds(2 * i + 1, 1), :]], axis=0
    )


def qkv_body(n, shape, scal, x, rel, *refs):
    weights, refs = refs[:n], refs[n:]
    if n != 8:
        vec_in, refs = refs[0], refs[1:]
    normed, q, k, v, slots_out, vec_out, wq, wk, wv, small, sems = refs
    i = pl.program_id(0)

    @pl.when(i == 0)
    def _():
        if n == 8:
            rows = shape
            for j, w in enumerate((wq, wk, wv)):
                fetch(scal, weights, w, sems.at[j], 8 + j * rows, rows)
            for buf in range(4):
                for z in range(4):
                    f, _ = place(scal, buf, 0, z)
                    if buf in (0, 1, 2):
                        pass
                    pltpu.make_async_copy(
                        weights[buf].at[z, pl.ds(0, 8), :], small.at[buf * 4 + z], sems.at[3]
                    ).start()
            f0 = scal[0]
            slots_out[...] = jnp.concatenate([rel[f0 ^ f] for f in range(8)], axis=1)
            arrive(small, sems.at[3])
            core = scal[1] & 1
            flip = jnp.where(core == 0, 1, 2)
            parts = []
            for f in range(8):
                zz = (f >> 1) ^ (f0 >> 1)
                yy = (f & 1) ^ (f0 & 1)
                parts.append(small[yy * flip * 4 + zz].astype(F32))
            vec_out[0:8, :] = jnp.concatenate([t[:, : D // 8] for t in parts], axis=1)
            for j in range(4):
                vec_out[8 + j : 9 + j, :] = jnp.concatenate(
                    [parts[2 * j][0:1, D // 2 :], parts[2 * j + 1][0:1, D // 2 :]], axis=1
                )
        else:
            for j, w in enumerate((wq, wk, wv)):
                fetch(scal, weights[j : j + 1], w, sems.at[j])
            slots_out[...] = rel[...]
            vec_out[...] = vec_in[...]
        for j, w in enumerate((wq, wk, wv)):
            arrive(w, sems.at[j])

    n1, _ = normal_rows(stamp(x[...], slots_out, i))
    low = (n1 * vec_out[GAIN1 : GAIN1 + 1, :] + vec_out[SHIFT1 : SHIFT1 + 1, :]).astype(BF16)
    normed[...] = low
    q[...] = (mm(low, wq[...]) + vec_out[QADD : QADD + 1, :]).astype(BF16)
    k[...] = mm(low, wk[...]).astype(BF16)
    v[...] = (mm(low, wv[...]) + vec_out[VADD : VADD + 1, :]).astype(BF16)


def qkv(scal, x, rel, weights, vec, win):
    rows = x.shape[0]
    slots = 2 * (rows // win)
    n = len(weights)
    blk = pl.BlockSpec((win, D), lambda i: (i, 0))
    ins = [SMEM, blk, whole(rel.shape)] + [ANY] * n
    args = [scal, x, rel, *weights]
    if n != 8:
        ins.append(whole(vec.shape))
        args.append(vec)
    return pl.pallas_call(
        functools.partial(qkv_body, n, D // 32),
        grid=(rows // win,),
        in_specs=ins,
        out_specs=[blk] * 4 + [whole((slots, D)), whole((12, D))],
        out_shape=[sds((rows, D), BF16)] * 4 + [sds((slots, D), F32), sds((12, D), F32)],
        scratch_shapes=[pltpu.VMEM((D, D), BF16)] * 3
        + [pltpu.VMEM((16, 8, D), BF16), pltpu.SemaphoreType.DMA((4,))],
        compiler_params=PARAMS,
    )(*args)


def lane_mask(half):
    lane = lax.broadcasted_iota(jnp.int32, (1, 2 * HEAD), 1)
    return (lane >= HEAD) if half else (lane < HEAD)


def permitted(win, layout):
    a = lax.broadcasted_iota(jnp.int32, (win, win), 0) // (win // 2)
    b = lax.broadcasted_iota(jnp.int32, (win, win), 1) // (win // 2)
    return (a == b) | (layout == 1)


def attend_body(n, rows, scal, lay, q, k, v, x, slots, vec, *refs):
    weights, refs = refs[:n], refs[n:]
    mixture, attended, second, wo, sems = refs
    i = pl.program_id(0)

    @pl.when(i == 0)
    def _():
        fetch(scal, weights, wo, sems, 0, rows)

    win = q.shape[0]
    allowed = permitted(win, lay[i])

    def pair(j, _):
        at = pl.ds(pl.multiple_of(j * 2 * HEAD, 2 * HEAD), 2 * HEAD)
        qp, kp, vp = q[:, at] * 0.125, k[:, at], v[:, at]
        got = []
        for half in range(2):
            s = mm(jnp.where(lane_mask(half), qp, 0), kp, 1, 1)
            s = jnp.where(allowed, s, -1e30)
            e = jnp.exp(s - jnp.max(s, axis=-1, keepdims=True))
            a = e * (1.0 / jnp.sum(e, axis=-1, keepdims=True))
            got.append(mm(a.astype(BF16), vp))
        mixture[:, at] = jnp.where(lane_mask(0), got[0], got[1]).astype(BF16)
        return 0

    lax.fori_loop(0, HEADS // 2, pair, 0)

    @pl.when(i == 0)
    def _():
        arrive(wo, sems)

    att = stamp(x[...], slots, i) + mm(mixture[...], wo[...]) + vec[OADD : OADD + 1, :]
    attended[...] = att
    n2, _ = normal_rows(att)
    second[...] = (n2 * vec[GAIN2 : GAIN2 + 1, :] + vec[SHIFT2 : SHIFT2 + 1, :]).astype(BF16)


def attend(scal, lay, q, k, v, x, slots, vec, weights):
    rows = x.shape[0]
    win = rows // lay.shape[0]
    n = len(weights)
    blk = pl.BlockSpec((win, D), lambda i: (i, 0))
    return pl.pallas_call(
        functools.partial(attend_body, n, D // 32),
        grid=(rows // win,),
        in_specs=[SMEM, SMEM] + [blk] * 4 + [whole(slots.shape), whole(vec.shape)] + [ANY] * n,
        out_specs=[blk] * 3,
        out_shape=[sds((rows, D), BF16), sds((rows, D), F32), sds((rows, D), BF16)],
        scratch_shapes=[pltpu.VMEM((D, D), BF16), pltpu.SemaphoreType.DMA],
        compiler_params=PARAMS,
    )(scal, lay, q, k, v, x, slots, vec, *weights)


CHUNK = 64


def up_body(n, row, rows, scal, second, vec, *refs):
    weights, refs = refs[:n], refs[n:]
    hidden, slope, wu, pre, sems = refs
    i = pl.program_id(0)

    @pl.when(i == 0)
    def _():
        fetch(scal, weights, wu, sems, row, rows, True)
        arrive(wu, sems)

    at = pl.ds(pl.multiple_of(i * D, D), D)
    pre[...] = mm(second[...], wu[:, at])
    add = vec[pl.ds(8 + i, 1), :]

    def step(j, _):
        rr = pl.ds(pl.multiple_of(j * CHUNK, CHUNK), CHUNK)
        u = pre[rr, :] + add
        a = jnp.abs(u)
        t = 1.0 / (1.0 + TAIL_P * a)
        e = jnp.exp(-0.5 * (u * u))
        acc = jnp.full_like(t, TAIL[-1])
        for c in TAIL[-2::-1]:
            acc = acc * t + c
        tail = e * (t * acc)
        cdf = jnp.where(u >= 0, 1.0 - tail, tail)
        hidden[rr, :] = (u * cdf).astype(BF16)
        slope[rr, :] = cdf + u * (e * (1.0 / math.sqrt(2.0 * math.pi)))
        return 0

    lax.fori_loop(0, pre.shape[0] // CHUNK, step, 0)


def up_gelu(scal, second, vec, weights, ff, row=0, rows=0):
    n = len(weights)
    m = second.shape[0]
    blk = pl.BlockSpec((m, D), lambda i: (0, i))
    return pl.pallas_call(
        functools.partial(up_body, n, row, rows),
        grid=(ff // D,),
        in_specs=[SMEM, whole(second.shape), whole(vec.shape)] + [ANY] * n,
        out_specs=[blk] * 2,
        out_shape=[sds((m, ff), BF16), sds((m, ff), F32)],
        scratch_shapes=[
            pltpu.VMEM((D, ff), BF16),
            pltpu.VMEM((m, D), F32),
            pltpu.SemaphoreType.DMA,
        ],
        compiler_params=PARAMS,
    )(scal, second, vec, *weights)


def pre_body(n, rows, scal, cot, slope, *refs):
    weights, refs = refs[:n], refs[n:]
    low, add, wd, sems = refs
    i = pl.program_id(0)

    @pl.when(i == 0)
    def _():
        fetch(scal, weights, wd, sems, 0, rows)
        arrive(wd, sems)

    grad = mm(cot[...], wd[pl.ds(pl.multiple_of(i * D, D), D), :], 1, 1)
    g = (grad * slope[...]).astype(BF16)
    low[...] = g
    add[...] = jnp.sum(g.astype(F32), axis=0, keepdims=True)


def pre_grad(scal, cot, slope, weights, rows=0):
    n = len(weights)
    m, ff = slope.shape
    blk = pl.BlockSpec((m, D), lambda i: (0, i))
    return pl.pallas_call(
        functools.partial(pre_body, n, rows),
        grid=(ff // D,),
        in_specs=[SMEM, whole(cot.shape), blk] + [ANY] * n,
        out_specs=[blk, pl.BlockSpec((1, D), lambda i: (0, i))],
        out_shape=[sds((m, ff), BF16), sds((1, ff), F32)],
        scratch_shapes=[pltpu.VMEM((ff, D), BF16), pltpu.SemaphoreType.DMA],
        compiler_params=PARAMS,
    )(scal, cot, slope, *weights)


def norm_back(e, n, r, gain):
    f = e * gain
    return r * (f - jnp.mean(f, -1, keepdims=True) - n * jnp.mean(f * n, -1, keepdims=True))


def total(v):
    return jnp.sum(v, axis=0, keepdims=True)


def accumulate(ref, i, rows):
    new = jnp.concatenate(rows + [jnp.zeros((8 - len(rows), D), F32)], axis=0)

    @pl.when(i == 0)
    def _():
        ref[...] = new

    @pl.when(i != 0)
    def _():
        ref[...] += new


def second_body(n, row, rows, scal, pre, attended, cot, vec, *refs):
    weights, refs = refs[:n], refs[n:]
    grad, low, sums, wu, sems = refs
    i = pl.program_id(0)

    @pl.when(i == 0)
    def _():
        fetch(scal, weights, wu, sems, row, rows, True)
        arrive(wu, sems)

    e = mm(pre[...], wu[...], 1, 1)
    n2, r = normal_rows(attended[...])
    c = cot[...]
    g = c + norm_back(e, n2, r, vec[GAIN2 : GAIN2 + 1, :])
    grad[...] = g
    low[...] = g.astype(BF16)
    accumulate(sums, i, [total(e * n2), total(e), total(g), total(c)])


def second_back(scal, pre, attended, cot, vec, weights, win, row=0, rows=0):
    n = len(weights)
    m, ff = pre.shape
    blk = pl.BlockSpec((win, D), lambda i: (i, 0))
    return pl.pallas_call(
        functools.partial(second_body, n, row, rows),
        grid=(m // win,),
        in_specs=[SMEM, pl.BlockSpec((win, ff), lambda i: (i, 0)), blk, blk, whole(vec.shape)]
        + [ANY] * n,
        out_specs=[blk, blk, whole((8, D))],
        out_shape=[sds((m, D), F32), sds((m, D), BF16), sds((8, D), F32)],
        scratch_shapes=[pltpu.VMEM((D, ff), BF16), pltpu.SemaphoreType.DMA],
        compiler_params=PARAMS,
    )(scal, pre, attended, cot, vec, *weights)


def attend_back_body(n, rows, scal, lay, low, q, k, v, *refs):
    weights, refs = refs[:n], refs[n:]
    dq, dk, dv, wo, mix, sems = refs
    i = pl.program_id(0)

    @pl.when(i == 0)
    def _():
        fetch(scal, weights, wo, sems, 0, rows)
        arrive(wo, sems)

    mix[...] = mm(low[...], wo[...], 1, 1).astype(BF16)
    win = q.shape[0]
    allowed = permitted(win, lay[i])

    def pair(j, _):
        at = pl.ds(pl.multiple_of(j * 2 * HEAD, 2 * HEAD), 2 * HEAD)
        qp, kp, vp, gp = q[:, at] * 0.125, k[:, at], v[:, at], mix[:, at]
        ks = kp * 0.125
        got = []
        for half in range(2):
            mask = lane_mask(half)
            s = mm(jnp.where(mask, kp, 0), qp, 1, 1)
            s = jnp.where(allowed, s, -1e30)
            e = jnp.exp(s - jnp.max(s, axis=0, keepdims=True))
            a = e * (1.0 / jnp.sum(e, axis=0, keepdims=True))
            t = a * mm(jnp.where(mask, vp, 0), gp, 1, 1)
            ds = (t - a * jnp.sum(t, axis=0, keepdims=True)).astype(BF16)
            got.append((mm(ds, ks, 0, 0), mm(ds, qp), mm(a.astype(BF16), gp)))
        for ref, first, last in zip((dq, dk, dv), got[0], got[1]):
            ref[:, at] = jnp.where(lane_mask(0), first, last).astype(BF16)
        return 0

    lax.fori_loop(0, HEADS // 2, pair, 0)


def attend_back(scal, lay, low, q, k, v, weights):
    n = len(weights)
    m = q.shape[0]
    win = m // lay.shape[0]
    blk = pl.BlockSpec((win, D), lambda i: (i, 0))
    return pl.pallas_call(
        functools.partial(attend_back_body, n, D // 32),
        grid=(m // win,),
        in_specs=[SMEM, SMEM] + [blk] * 4 + [ANY] * n,
        out_specs=[blk] * 3,
        out_shape=[sds((m, D), BF16)] * 3,
        scratch_shapes=[
            pltpu.VMEM((D, D), BF16),
            pltpu.VMEM((win, D), BF16),
            pltpu.SemaphoreType.DMA,
        ],
        compiler_params=PARAMS,
    )(scal, lay, low, q, k, v, *weights)


def first_body(n, rows, scal, dq, dk, dv, x, upper, slots, vec, *refs):
    weights, refs = refs[:n], refs[n:]
    out, slot_sums, sums, wq, wk, wv, sems = refs
    i = pl.program_id(0)

    @pl.when(i == 0)
    def _():
        for j, w in enumerate((wq, wk, wv)):
            src = weights if n == 8 else weights[j : j + 1]
            fetch(scal, src, w, sems.at[j], 8 + j * rows, rows)
        for j, w in enumerate((wq, wk, wv)):
            arrive(w, sems.at[j])

    e = mm(dq[...], wq[...], 1, 1) + mm(dk[...], wk[...], 1, 1) + mm(dv[...], wv[...], 1, 1)
    n1, r = normal_rows(stamp(x[...], slots, i))
    g = upper[...] + norm_back(e, n1, r, vec[GAIN1 : GAIN1 + 1, :])
    out[...] = g
    half = g.shape[0] // 2
    slot_sums[pl.ds(2 * i, 1), :] = total(g[:half])
    slot_sums[pl.ds(2 * i + 1, 1), :] = total(g[half:])
    accumulate(
        sums,
        i,
        [total(e * n1), total(e), total(dq[...].astype(F32)), total(dv[...].astype(F32))],
    )


def first_back(scal, dq, dk, dv, x, upper, slots, vec, weights, win):
    n = len(weights)
    m = x.shape[0]
    blk = pl.BlockSpec((win, D), lambda i: (i, 0))
    return pl.pallas_call(
        functools.partial(first_body, n, D // 32),
        grid=(m // win,),
        in_specs=[SMEM] + [blk] * 5 + [whole(slots.shape), whole(vec.shape)] + [ANY] * n,
        out_specs=[blk, whole(slots.shape), whole((8, D))],
        out_shape=[sds((m, D), F32), sds(slots.shape, F32), sds((8, D), F32)],
        scratch_shapes=[pltpu.VMEM((D, D), BF16)] * 3 + [pltpu.SemaphoreType.DMA((3,))],
        compiler_params=PARAMS,
    )(scal, dq, dk, dv, x, upper, slots, vec, *weights)


def down_body(n, rows, scal, hidden, attended, vec, *refs):
    weights, refs = refs[:n], refs[n:]
    out, wd, sems = refs
    i = pl.program_id(0)

    @pl.when(i == 0)
    def _():
        fetch(scal, weights, wd, sems, 0, rows)
        arrive(wd, sems)

    out[...] = attended[...] + mm(hidden[...], wd[...]) + vec[DADD : DADD + 1, :]


def down_out(scal, hidden, attended, vec, weights, win, rows=0):
    n = len(weights)
    m, ff = hidden.shape
    blk = pl.BlockSpec((win, D), lambda i: (i, 0))
    return pl.pallas_call(
        functools.partial(down_body, n, rows),
        grid=(m // win,),
        in_specs=[SMEM, pl.BlockSpec((win, ff), lambda i: (i, 0)), blk, whole(vec.shape)]
        + [ANY] * n,
        out_specs=blk,
        out_shape=sds((m, D), F32),
        scratch_shapes=[pltpu.VMEM((ff, D), BF16), pltpu.SemaphoreType.DMA],
        compiler_params=PARAMS,
    )(scal, hidden, attended, vec, *weights)


def scatter_tile(scal, stage, keep, send, sem, blocks, rows, row, columns=False):
    f0, p0 = scal[0], scal[1]
    y, z, c, x = f0 & 1, f0 >> 1, p0 & 1, p0 >> 1
    for at, f in enumerate(blocks):
        dy, k = (f & 1) ^ y, (f >> 1) ^ z
        for px in range(2):
            dx = px ^ x
            for other, out in enumerate((keep, send)):
                core = c ^ other
                one = jnp.where(core == 0, dx, dy)
                two = jnp.where(core == 0, dy, dx)
                dst = out.at[one, two, k]
                piece = px * 2 + core
                if columns:
                    half = D // 2
                    for part in range(2):
                        pltpu.make_async_copy(
                            stage.at[pl.ds(pl.multiple_of((piece * 2 + part) * rows, 8), rows), :],
                            dst.at[pl.ds(row, rows), pl.ds(part * half, half)],
                            sem,
                        ).start()
                else:
                    src = pl.multiple_of((at * 4 + piece) * rows, 8)
                    pltpu.make_async_copy(
                        stage.at[pl.ds(src, rows), :], dst.at[pl.ds(row, rows), :], sem
                    ).start()


def wide_body(columns, scal, a, b, keep, send, stage, sems):
    i = pl.program_id(0)
    last = pl.num_programs(0) - 1
    slot = i & 1

    @pl.when(i >= 2)
    def _():
        arrive(stage.at[slot], sems.at[slot])

    tile = mm(a[...], b[...], 0, 0).astype(BF16)
    stage[slot] = tile
    rows = D // 8
    scatter_tile(scal, stage.at[slot], keep, send, sems.at[slot], [i], rows, 0, columns)

    @pl.when(i == last)
    def _():
        arrive(stage.at[1 - slot], sems.at[1 - slot])
        arrive(stage.at[slot], sems.at[slot])


def wide_grad(scal, a, b, columns):
    m = a.shape[0]
    half = D // 2
    full = pl.BlockSpec((m, D), lambda i: (0, 0))
    part = pl.BlockSpec((m, half), lambda i: (0, i))
    shape = sds((2, 2, 4, D // 8, D), BF16)
    return pl.pallas_call(
        functools.partial(wide_body, columns),
        grid=(8,),
        in_specs=[SMEM, full if columns else part, part if columns else full],
        out_specs=[ANY, ANY],
        out_shape=[shape, shape],
        scratch_shapes=[
            pltpu.VMEM((2, D, half) if columns else (2, half, D), BF16),
            pltpu.SemaphoreType.DMA((2,)),
        ],
        compiler_params=PARAMS,
    )(scal, a, b)


def square_body(scal, mixture, normed, low, dq, dk, dv, keep, send, stage, sems):
    rows = D // 32
    half = D // 2
    for j in range(8):
        m, part = j // 2, j % 2
        slot = j % 2
        if j >= 2:
            arrive(stage.at[slot], sems.at[slot])
        left = mixture if m == 0 else normed
        right = (low, dq, dk, dv)[m]
        stage[slot] = mm(left[:, part * half : (part + 1) * half], right[...], 0, 0).astype(BF16)
        blocks = [part * 4 + n for n in range(4)]
        scatter_tile(scal, stage.at[slot], keep, send, sems.at[slot], blocks, rows, m * rows)
    for slot in range(2):
        arrive(stage.at[slot], sems.at[slot])


def square_grads(scal, *args):
    shape = sds((2, 2, 4, D // 8, D), BF16)
    return pl.pallas_call(
        square_body,
        in_specs=[SMEM] + [pl.BlockSpec(memory_space=pltpu.VMEM)] * 6,
        out_specs=[ANY, ANY],
        out_shape=[shape, shape],
        scratch_shapes=[pltpu.VMEM((2, D // 2, D), BF16), pltpu.SemaphoreType.DMA((2,))],
        compiler_params=PARAMS,
    )(scal, *args)


BOTH = ("fsdp", "dp")


def flip(v, f_of=0, p_of=0):
    pairs = [
        (f * 4 + p, (f ^ f_of) * 4 + (p ^ p_of)) for f in range(8) for p in range(4)
    ]
    return lax.ppermute(v, BOTH, pairs)


def flip_by_core(v, first, second):
    pairs = []
    for f in range(8):
        for p in range(4):
            df, dp = second if p & 1 else first
            pairs.append((f * 4 + p, (f ^ df) * 4 + (p ^ dp)))
    return lax.ppermute(v, BOTH, pairs)


Y_OF, X_OF = (1, 0), (0, 2)


def gather_pieces(piece):
    held = jnp.stack([piece] + [flip(piece, 2 * k) for k in (1, 2, 3)])
    one = flip_by_core(held, Y_OF, X_OF)
    two = flip_by_core(held, X_OF, Y_OF)
    three = flip_by_core(one, X_OF, Y_OF)
    mine = [held, one, two, three]
    return mine + [flip(v, 0, 1) for v in mine]


def up32(*vs):
    out = vs[0].astype(F32)
    for v in vs[1:]:
        out = out + v.astype(F32)
    return out


def sum_pieces(keep, send):
    r = flip(send, 0, 1)
    s1 = up32(keep[1], r[1]).astype(BF16)
    r1 = flip_by_core(s1, X_OF, Y_OF)
    s2 = up32(keep[0, 1], r[0, 1], r1[1]).astype(BF16)
    r2 = flip_by_core(s2, Y_OF, X_OF)
    rz = []
    for k in (1, 2, 3):
        t = up32(keep[0, 0, k], r[0, 0, k], r1[0, k], r2[k]).astype(BF16)
        rz.append(flip(t, 2 * k))
    done = up32(keep[0, 0, 0], r[0, 0, 0], r1[0, 0], r2[0], *rz).astype(BF16)
    return spread_dp(done)


def order_dp(parts):
    p = lax.axis_index("dp")
    low, high = (p & 1) == 1, (p >> 1) == 1
    a, b, c, d = parts
    a, b, c, d = (
        jnp.where(low, b, a),
        jnp.where(low, a, b),
        jnp.where(low, d, c),
        jnp.where(low, c, d),
    )
    return (
        jnp.where(high, c, a),
        jnp.where(high, d, b),
        jnp.where(high, a, c),
        jnp.where(high, b, d),
    )


def spread_dp(done):
    over = flip(done, 0, 2)
    return order_dp((done, flip(done, 0, 1), over, flip(over, 0, 1)))


def sum_all(v):
    v = v + sum_in_order([flip(v, 2 * k) for k in (1, 2, 3)])
    v = v + flip(v, 1)
    v = v + flip(v, 0, 2)
    return v + flip(v, 0, 1)


def sum_in_order(vs):
    out = vs[0]
    for v in vs[1:]:
        out = out + v
    return out


def on_device(
    sizes,
    inputs,
    cotangent,
    timesteps,
    layouts,
    step_table,
    first_gain,
    first_shift,
    query_matrix,
    query_bias,
    key_matrix,
    value_matrix,
    value_bias,
    out_matrix,
    out_bias,
    second_gain,
    second_shift,
    up_matrix,
    up_bias,
    down_matrix,
    down_bias,
):
    n_fsdp, n_dp = sizes
    fast = (n_fsdp, n_dp) == (8, 4)
    f, p = lax.axis_index("fsdp"), lax.axis_index("dp")
    scal = jnp.stack([f, p]).astype(jnp.int32)
    row_count = inputs.shape[0]
    win = row_count // layouts.shape[0]
    ff = up_matrix.shape[1] * n_fsdp
    steps = step_table.shape[0]
    pairs = timesteps.reshape(-1, 2)
    first_steps = pairs[:, 0]
    second_steps = jnp.where(layouts == 1, first_steps, pairs[:, 1])
    slot_steps = jnp.stack([first_steps, second_steps], axis=1).reshape(-1)
    vecs = (
        first_gain,
        first_shift,
        query_bias,
        value_bias,
        out_bias,
        second_gain,
        second_shift,
        down_bias,
        up_bias,
    )
    mats = (query_matrix, key_matrix, value_matrix, out_matrix, up_matrix, down_matrix)
    cot_low = cotangent.astype(BF16)
    r = D // 32
    if fast:
        pieces = prep(scal, vecs, mats)
        y_steps = jnp.stack([slot_steps, flip(slot_steps, 1)])
        all_steps = jnp.stack([y_steps] + [flip(y_steps, 2 * k) for k in (1, 2, 3)])
        asked = jnp.take(step_table, all_steps, axis=0).astype(BF16)
        back = jnp.stack([asked[0]] + [flip(asked[k], 2 * k) for k in (1, 2, 3)])
        given = jnp.stack([back[:, 0], flip(back[:, 1], 1)], axis=1)
        rel = given.reshape(8, given.shape[2], given.shape[3]).astype(F32)
        one = gather_pieces(pieces[0])
        two = gather_pieces(pieces[1])
        three = gather_pieces(pieces[2])
        w_qkv, w_out, w_up, w_down, vec = one, two, two, three, None
        at_up = dict(row=r, rows=D // 8)
        at_down = dict(rows=D // 8)
    else:
        low = [m.astype(BF16) for m in vecs + mats]
        full = [lax.all_gather(m, "fsdp", axis=0, tiled=True) for m in low[:9]]
        vec = jnp.concatenate(full).reshape(12, D).astype(F32)
        w_qkv = [lax.all_gather(m, "fsdp", axis=0, tiled=True) for m in low[9:12]]
        w_out = [lax.all_gather(low[12], "fsdp", axis=0, tiled=True)]
        w_up = [lax.all_gather(low[13], "fsdp", axis=1, tiled=True)]
        w_down = [lax.all_gather(low[14], "fsdp", axis=0, tiled=True)]
        table = lax.all_gather(step_table.astype(BF16), "fsdp", axis=1, tiled=True)
        rel = jnp.take(table, slot_steps, axis=0).astype(F32)
        at_up = at_down = {}

    normed, q, k, v, slots, vec = qkv(scal, inputs, rel, w_qkv, vec, win)
    mixture, attended, second = attend(scal, layouts, q, k, v, inputs, slots, vec, w_out)
    hidden, slope = up_gelu(scal, second, vec, w_up, ff, **at_up)
    pre, up_add = pre_grad(scal, cot_low, slope, w_down, **at_down)
    grad, low, sums2 = second_back(scal, pre, attended, cotangent, vec, w_up, win, **at_up)
    dq, dk, dv = attend_back(scal, layouts, low, q, k, v, w_out)
    input_grad, slot_sums, sums1 = first_back(
        scal, dq, dk, dv, inputs, grad, slots, vec, w_qkv, win
    )
    block_output = down_out(scal, hidden, attended, vec, w_down, win, **at_down)

    small = jnp.concatenate(
        [sums1[:4], sums2[2:3], sums2[:2], sums2[3:4], up_add.reshape(-1, D)], axis=0
    )
    if fast:
        down_sum = sum_pieces(*wide_grad(scal, hidden, cot_low, False))
        up_sum = sum_pieces(*wide_grad(scal, second, pre, True))
        square = sum_pieces(*square_grads(scal, mixture, normed, low, dq, dk, dv))
        down_grad = jnp.concatenate(down_sum, axis=0).astype(F32)
        half = D // 2
        up_grad = jnp.concatenate(
            [t for m in up_sum for t in (m[:, :half], m[:, half:])], axis=0
        ).astype(F32)
        out_grad, query_grad, key_grad, value_grad = (
            jnp.concatenate([m[j * r : (j + 1) * r] for m in square], axis=0).astype(F32)
            for j in range(4)
        )
        small = sum_all(small)
        own = slot_sums.reshape(-1, 8, D // 8)
        rel_sums = jnp.stack([lax.dynamic_index_in_dim(own, f ^ j, 1, False) for j in range(8)])
        rel_sums = rel_sums.reshape(4, 2, *rel_sums.shape[1:])
        half_sums = jnp.stack([rel_sums[:, 0], flip(rel_sums[:, 1], 1)], axis=1)
        fsdp_sums = jnp.stack(
            [half_sums[0]] + [flip(half_sums[k], 2 * k) for k in (1, 2, 3)]
        ).reshape(-1, D // 8)
        fsdp_steps = all_steps.reshape(-1)
        every_sum = jnp.concatenate(spread_dp(fsdp_sums))
        every_step = jnp.concatenate(spread_dp(fsdp_steps))
        table_grad = jnp.zeros((steps, D // 8), F32).at[every_step].add(every_sum)
    else:
        total_of = lambda v, dim: lax.psum(
            lax.psum_scatter(v, "fsdp", scatter_dimension=dim, tiled=True), "dp"
        )
        down_grad = total_of(mm(hidden, cot_low, 0, 0), 0)
        up_grad = total_of(mm(second, pre, 0, 0), 1)
        out_grad = total_of(mm(mixture, low, 0, 0), 0)
        query_grad = total_of(mm(normed, dq, 0, 0), 0)
        key_grad = total_of(mm(normed, dk, 0, 0), 0)
        value_grad = total_of(mm(normed, dv, 0, 0), 0)
        small = lax.psum(small, BOTH)
        table_grad = total_of(
            jnp.zeros((steps, D), F32).at[slot_steps].add(slot_sums), 1
        )
    width = D // n_fsdp
    mine = lax.dynamic_slice(small[:8], (0, f * width), (8, width))
    up_mine = lax.dynamic_slice(small[8:].reshape(-1), (f * (ff // n_fsdp),), (ff // n_fsdp,))
    return (
        block_output,
        input_grad,
        table_grad,
        mine[0],
        mine[1],
        query_grad,
        mine[2],
        key_grad,
        value_grad,
        mine[3],
        out_grad,
        mine[4],
        mine[5],
        mine[6],
        up_grad,
        up_mine,
        down_grad,
        mine[7],
    )


def solution(mesh):
    rows = P(("fsdp", "dp"), None)
    slots = P(("fsdp", "dp"))
    vector = P("fsdp")
    matrix = P("fsdp", None)
    wide = P(None, "fsdp")
    placed = (
        rows, rows, slots, slots, wide, vector, vector, matrix, vector, matrix,
        matrix, vector, matrix, vector, vector, vector, wide, vector, matrix, vector,
    )
    results = (
        rows, rows, wide, vector, vector, matrix, vector, matrix, matrix, vector,
        matrix, vector, vector, vector, wide, vector, matrix, vector,
    )
    return jax.shard_map(
        functools.partial(on_device, (mesh.shape["fsdp"], mesh.shape["dp"])),
        mesh=mesh,
        in_specs=placed,
        out_specs=results,
        check_vma=False,
    )
```

```python
import functools
import math

import jax
import jax.numpy as jnp
from jax import lax
from jax.experimental import pallas as pl
from jax.experimental.pallas import tpu as pltpu
from jax.sharding import PartitionSpec as P

HEADS = 12
HEAD = 64
D = HEADS * HEAD
F32 = jnp.float32
BF16 = jnp.bfloat16
ANY = pl.BlockSpec(memory_space=pl.ANY)
SMEM = pl.BlockSpec(memory_space=pltpu.SMEM)
PARAMS = pltpu.CompilerParams(vmem_limit_bytes=60 * 1024 * 1024)

TAIL_P = 0.21
TAIL = (
    0.08371157580586816,
    0.08506885523539415,
    0.06919219089790565,
    0.12487264009661635,
    -0.09392498913162721,
    0.349400678909721,
    -0.33025308461653297,
    0.2835884168453487,
    -0.07165627723466013,
)

GAIN1, SHIFT1, QADD, VADD, OADD, GAIN2, SHIFT2, DADD, UADD = range(9)


def whole(shape):
    return pl.BlockSpec(shape, lambda *_: (0,) * len(shape))


def sds(shape, dtype):
    return jax.ShapeDtypeStruct(shape, dtype)


def mm(a, b, ca=1, cb=0):
    return lax.dot_general(a, b, (((ca,), (cb,)), ((), ())), preferred_element_type=F32)


def place(scal, buf, other, k):
    f, p = scal[0], scal[1]
    y, z, c, x = f & 1, f >> 1, p & 1, p >> 1
    core = c ^ other
    by_y = 1 - core if buf == 1 else core if buf == 2 else buf // 3
    by_x = core if buf == 1 else 1 - core if buf == 2 else buf // 3
    return ((z ^ k) << 1) | (y ^ by_y), ((x ^ by_x) << 1) | core


def fetch(scal, refs, dst, sem, row=0, rows=0, columns=False):
    if len(refs) == 1:
        pltpu.make_async_copy(refs[0], dst, sem).start()
        return
    for other in range(2):
        for buf in range(4):
            for k in range(4):
                f, p = place(scal, buf, other, k)
                src = refs[other * 4 + buf].at[k]
                if columns:
                    half = D // 2
                    for part in range(2):
                        r = pl.multiple_of(p * 2 * rows + part * rows, 8)
                        pltpu.make_async_copy(
                            src.at[pl.ds(row, rows), pl.ds(part * half, half)],
                            dst.at[pl.ds(r, rows), pl.ds(pl.multiple_of(f * half, 128), half)],
                            sem,
                        ).start()
                else:
                    r = pl.multiple_of((f * 4 + p) * rows, 8)
                    pltpu.make_async_copy(
                        src.at[pl.ds(row, rows), :], dst.at[pl.ds(r, rows), :], sem
                    ).start()


def arrive(dst, sem):
    pltpu.make_async_copy(dst, dst, sem).wait()


def prep_body(scal, *refs):
    vecs, (q, k, v, o, up, down), (one, two, three) = refs[:9], refs[9:15], refs[15:]
    up_add = vecs[8][...]
    left = jnp.concatenate([r[...] for r in vecs[:8]], axis=0)
    left = jnp.concatenate([left, jnp.zeros((8, D // 2 - left.shape[1]), F32)], axis=1)
    right = jnp.concatenate([up_add, jnp.zeros((7, D // 2), F32)], axis=0)
    one[0:8, :] = jnp.concatenate([left, right], axis=1).astype(BF16)
    r = q.shape[0]
    for i, m in enumerate((q, k, v)):
        one[8 + i * r : 8 + (i + 1) * r, :] = m[...].astype(BF16)
    two[0:r, :] = o[...].astype(BF16)
    u = up.shape[0] // 2
    two[r : r + u, 0 : D // 2] = up[0:u, :].astype(BF16)
    two[r : r + u, D // 2 : D] = up[u : 2 * u, :].astype(BF16)
    three[...] = down[...].astype(BF16)


def prep(scal, vecs, mats):
    q, up, down = mats[0], mats[4], mats[5]
    r, u, d = q.shape[0] // 4, up.shape[0] // 4, down.shape[0] // 4
    half = up.shape[1]
    mine = lambda rows, cols: pl.BlockSpec((rows, cols), lambda i, s: (s[1], 0))
    vecs = [v.reshape(1, -1) for v in vecs]
    return pl.pallas_call(
        prep_body,
        grid_spec=pltpu.PrefetchScalarGridSpec(
            num_scalar_prefetch=1,
            grid=(1,),
            in_specs=[pl.BlockSpec(v.shape, lambda i, s: (0, 0)) for v in vecs]
            + [mine(r, D)] * 4
            + [mine(u, half), mine(d, D)],
            out_specs=[
                pl.BlockSpec(s, lambda i, s_: (0, 0))
                for s in ((8 + 3 * r, D), (r + u // 2, D), (d, D))
            ],
        ),
        out_shape=(sds((8 + 3 * r, D), BF16), sds((r + u // 2, D), BF16), sds((d, D), BF16)),
        compiler_params=PARAMS,
    )(scal, *vecs, *mats)


def normal_rows(v):
    c = v - jnp.mean(v, axis=-1, keepdims=True)
    r = lax.rsqrt(jnp.mean(c * c, axis=-1, keepdims=True) + 1e-05)
    return c * r, r


def stamp(x, slots, i):
    half = x.shape[0] // 2
    return jnp.concatenate(
        [x[:half] + slots[pl.ds(2 * i, 1), :], x[half:] + slots[pl.ds(2 * i + 1, 1), :]], axis=0
    )


def qkv_body(n, shape, scal, x, rel, *refs):
    weights, refs = refs[:n], refs[n:]
    if n != 8:
        vec_in, refs = refs[0], refs[1:]
    normed, q, k, v, slots_out, vec_out, wq, wk, wv, small, sems = refs
    i = pl.program_id(0)

    @pl.when(i == 0)
    def _():
        if n == 8:
            rows = shape
            for j, w in enumerate((wq, wk, wv)):
                fetch(scal, weights, w, sems.at[j], 8 + j * rows, rows)
            for buf in range(4):
                for z in range(4):
                    f, _ = place(scal, buf, 0, z)
                    if buf in (0, 1, 2):
                        pass
                    pltpu.make_async_copy(
                        weights[buf].at[z, pl.ds(0, 8), :], small.at[buf * 4 + z], sems.at[3]
                    ).start()
            f0 = scal[0]
            slots_out[...] = jnp.concatenate([rel[f0 ^ f] for f in range(8)], axis=1)
            arrive(small, sems.at[3])
            core = scal[1] & 1
            flip = jnp.where(core == 0, 1, 2)
            parts = []
            for f in range(8):
                zz = (f >> 1) ^ (f0 >> 1)
                yy = (f & 1) ^ (f0 & 1)
                parts.append(small[yy * flip * 4 + zz].astype(F32))
            vec_out[0:8, :] = jnp.concatenate([t[:, : D // 8] for t in parts], axis=1)
            for j in range(4):
                vec_out[8 + j : 9 + j, :] = jnp.concatenate(
                    [parts[2 * j][0:1, D // 2 :], parts[2 * j + 1][0:1, D // 2 :]], axis=1
                )
        else:
            for j, w in enumerate((wq, wk, wv)):
                fetch(scal, weights[j : j + 1], w, sems.at[j])
            slots_out[...] = rel[...]
            vec_out[...] = vec_in[...]
        for j, w in enumerate((wq, wk, wv)):
            arrive(w, sems.at[j])

    n1, _ = normal_rows(stamp(x[...], slots_out, i))
    low = (n1 * vec_out[GAIN1 : GAIN1 + 1, :] + vec_out[SHIFT1 : SHIFT1 + 1, :]).astype(BF16)
    normed[...] = low
    q[...] = (mm(low, wq[...]) + vec_out[QADD : QADD + 1, :]).astype(BF16)
    k[...] = mm(low, wk[...]).astype(BF16)
    v[...] = (mm(low, wv[...]) + vec_out[VADD : VADD + 1, :]).astype(BF16)


def qkv(scal, x, rel, weights, vec, win):
    rows = x.shape[0]
    slots = 2 * (rows // win)
    n = len(weights)
    blk = pl.BlockSpec((win, D), lambda i: (i, 0))
    ins = [SMEM, blk, whole(rel.shape)] + [ANY] * n
    args = [scal, x, rel, *weights]
    if n != 8:
        ins.append(whole(vec.shape))
        args.append(vec)
    return pl.pallas_call(
        functools.partial(qkv_body, n, D // 32),
        grid=(rows // win,),
        in_specs=ins,
        out_specs=[blk] * 4 + [whole((slots, D)), whole((12, D))],
        out_shape=[sds((rows, D), BF16)] * 4 + [sds((slots, D), F32), sds((12, D), F32)],
        scratch_shapes=[pltpu.VMEM((D, D), BF16)] * 3
        + [pltpu.VMEM((16, 8, D), BF16), pltpu.SemaphoreType.DMA((4,))],
        compiler_params=PARAMS,
    )(*args)


def lane_mask(half):
    lane = lax.broadcasted_iota(jnp.int32, (1, 2 * HEAD), 1)
    return (lane >= HEAD) if half else (lane < HEAD)


def permitted(win, layout):
    a = lax.broadcasted_iota(jnp.int32, (win, win), 0) // (win // 2)
    b = lax.broadcasted_iota(jnp.int32, (win, win), 1) // (win // 2)
    return (a == b) | (layout == 1)


def attend_body(scal, lay, q, k, v, mixture):
    allowed = permitted(q.shape[0], lay[pl.program_id(0)])

    def pair(j, _):
        at = pl.ds(pl.multiple_of(j * 2 * HEAD, 2 * HEAD), 2 * HEAD)
        qp, kp, vp = q[:, at] * 0.125, k[:, at], v[:, at]
        got = []
        for half in range(2):
            s = mm(jnp.where(lane_mask(half), qp, 0), kp, 1, 1)
            s = jnp.where(allowed, s, -1e30)
            e = jnp.exp(s - jnp.max(s, axis=-1, keepdims=True))
            a = e * (1.0 / jnp.sum(e, axis=-1, keepdims=True))
            got.append(mm(a.astype(BF16), vp))
        mixture[:, at] = jnp.where(lane_mask(0), got[0], got[1]).astype(BF16)
        return 0

    lax.fori_loop(0, HEADS // 2, pair, 0, unroll=True)


def attend(scal, lay, q, k, v):
    rows = q.shape[0]
    win = rows // lay.shape[0]
    blk = pl.BlockSpec((win, D), lambda i: (i, 0))
    return pl.pallas_call(
        attend_body,
        grid=(rows // win,),
        in_specs=[SMEM, SMEM] + [blk] * 3,
        out_specs=blk,
        out_shape=sds((rows, D), BF16),
        compiler_params=PARAMS,
    )(scal, lay, q, k, v)


def mix_body(n, rows, scal, mixture, x, slots, vec, *refs):
    weights, refs = refs[:n], refs[n:]
    attended, second, wo, sems = refs
    i = pl.program_id(0)

    @pl.when(i == 0)
    def _():
        fetch(scal, weights, wo, sems, 0, rows)
        arrive(wo, sems)

    att = stamp(x[...], slots, i) + mm(mixture[...], wo[...]) + vec[OADD : OADD + 1, :]
    attended[...] = att
    n2, _ = normal_rows(att)
    second[...] = (n2 * vec[GAIN2 : GAIN2 + 1, :] + vec[SHIFT2 : SHIFT2 + 1, :]).astype(BF16)


def mix(scal, mixture, x, slots, vec, weights, win):
    rows = x.shape[0]
    n = len(weights)
    blk = pl.BlockSpec((win, D), lambda i: (i, 0))
    return pl.pallas_call(
        functools.partial(mix_body, n, D // 32),
        grid=(rows // win,),
        in_specs=[SMEM, blk, blk, whole(slots.shape), whole(vec.shape)] + [ANY] * n,
        out_specs=[blk] * 2,
        out_shape=[sds((rows, D), F32), sds((rows, D), BF16)],
        scratch_shapes=[pltpu.VMEM((D, D), BF16), pltpu.SemaphoreType.DMA],
        compiler_params=PARAMS,
    )(scal, mixture, x, slots, vec, *weights)


CHUNK = 64


def up_body(n, row, rows, scal, second, vec, *refs):
    weights, refs = refs[:n], refs[n:]
    hidden, slope, wu, pre, sems = refs
    i = pl.program_id(0)

    @pl.when(i == 0)
    def _():
        fetch(scal, weights, wu, sems, row, rows, True)
        arrive(wu, sems)

    at = pl.ds(pl.multiple_of(i * D, D), D)
    pre[...] = mm(second[...], wu[:, at])
    add = vec[pl.ds(8 + i, 1), :]

    def step(j, _):
        rr = pl.ds(pl.multiple_of(j * CHUNK, CHUNK), CHUNK)
        u = pre[rr, :] + add
        a = jnp.abs(u)
        t = 1.0 / (1.0 + TAIL_P * a)
        e = jnp.exp(-0.5 * (u * u))
        acc = jnp.full_like(t, TAIL[-1])
        for c in TAIL[-2::-1]:
            acc = acc * t + c
        tail = e * (t * acc)
        cdf = jnp.where(u >= 0, 1.0 - tail, tail)
        hidden[rr, :] = (u * cdf).astype(BF16)
        slope[rr, :] = cdf + u * (e * (1.0 / math.sqrt(2.0 * math.pi)))
        return 0

    lax.fori_loop(0, pre.shape[0] // CHUNK, step, 0)


def up_gelu(scal, second, vec, weights, ff, row=0, rows=0):
    n = len(weights)
    m = second.shape[0]
    blk = pl.BlockSpec((m, D), lambda i: (0, i))
    return pl.pallas_call(
        functools.partial(up_body, n, row, rows),
        grid=(ff // D,),
        in_specs=[SMEM, whole(second.shape), whole(vec.shape)] + [ANY] * n,
        out_specs=[blk] * 2,
        out_shape=[sds((m, ff), BF16), sds((m, ff), F32)],
        scratch_shapes=[
            pltpu.VMEM((D, ff), BF16),
            pltpu.VMEM((m, D), F32),
            pltpu.SemaphoreType.DMA,
        ],
        compiler_params=PARAMS,
    )(scal, second, vec, *weights)


def pre_body(n, rows, scal, cot, slope, *refs):
    weights, refs = refs[:n], refs[n:]
    low, add, wd, sems = refs
    i = pl.program_id(0)

    @pl.when(i == 0)
    def _():
        fetch(scal, weights, wd, sems, 0, rows)
        arrive(wd, sems)

    grad = mm(cot[...], wd[pl.ds(pl.multiple_of(i * D, D), D), :], 1, 1)
    g = (grad * slope[...]).astype(BF16)
    low[...] = g
    add[...] = jnp.sum(g.astype(F32), axis=0, keepdims=True)


def pre_grad(scal, cot, slope, weights, rows=0):
    n = len(weights)
    m, ff = slope.shape
    blk = pl.BlockSpec((m, D), lambda i: (0, i))
    return pl.pallas_call(
        functools.partial(pre_body, n, rows),
        grid=(ff // D,),
        in_specs=[SMEM, whole(cot.shape), blk] + [ANY] * n,
        out_specs=[blk, pl.BlockSpec((1, D), lambda i: (0, i))],
        out_shape=[sds((m, ff), BF16), sds((1, ff), F32)],
        scratch_shapes=[pltpu.VMEM((ff, D), BF16), pltpu.SemaphoreType.DMA],
        compiler_params=PARAMS,
    )(scal, cot, slope, *weights)


def norm_back(e, n, r, gain):
    f = e * gain
    return r * (f - jnp.mean(f, -1, keepdims=True) - n * jnp.mean(f * n, -1, keepdims=True))


def total(v):
    return jnp.sum(v, axis=0, keepdims=True)


def accumulate(ref, i, rows):
    new = jnp.concatenate(rows + [jnp.zeros((8 - len(rows), D), F32)], axis=0)

    @pl.when(i == 0)
    def _():
        ref[...] = new

    @pl.when(i != 0)
    def _():
        ref[...] += new


def second_body(n, row, rows, scal, pre, attended, cot, vec, *refs):
    weights, refs = refs[:n], refs[n:]
    grad, low, sums, wu, sems = refs
    i = pl.program_id(0)

    @pl.when(i == 0)
    def _():
        fetch(scal, weights, wu, sems, row, rows, True)
        arrive(wu, sems)

    e = mm(pre[...], wu[...], 1, 1)
    n2, r = normal_rows(attended[...])
    c = cot[...]
    g = c + norm_back(e, n2, r, vec[GAIN2 : GAIN2 + 1, :])
    grad[...] = g
    low[...] = g.astype(BF16)
    accumulate(sums, i, [total(e * n2), total(e), total(g), total(c)])


def second_back(scal, pre, attended, cot, vec, weights, win, row=0, rows=0):
    n = len(weights)
    m, ff = pre.shape
    blk = pl.BlockSpec((win, D), lambda i: (i, 0))
    return pl.pallas_call(
        functools.partial(second_body, n, row, rows),
        grid=(m // win,),
        in_specs=[SMEM, pl.BlockSpec((win, ff), lambda i: (i, 0)), blk, blk, whole(vec.shape)]
        + [ANY] * n,
        out_specs=[blk, blk, whole((8, D))],
        out_shape=[sds((m, D), F32), sds((m, D), BF16), sds((8, D), F32)],
        scratch_shapes=[pltpu.VMEM((D, ff), BF16), pltpu.SemaphoreType.DMA],
        compiler_params=PARAMS,
    )(scal, pre, attended, cot, vec, *weights)


def attend_back_body(n, rows, start, filled, scal, lay, low, q, k, v, *refs):
    weights, refs = refs[:n], refs[n + filled :]
    dq, dk, dv, wo, mix, sems = refs
    i = pl.program_id(0)

    @pl.when(i == 0)
    def _():
        fetch(scal, weights, wo, sems, 0, rows)
        arrive(wo, sems)

    mix[...] = mm(low[...], wo[...], 1, 1).astype(BF16)
    win = q.shape[0]
    allowed = permitted(win, lay[i + start])

    def pair(j, _):
        at = pl.ds(pl.multiple_of(j * 2 * HEAD, 2 * HEAD), 2 * HEAD)
        qp, kp, vp, gp = q[:, at] * 0.125, k[:, at], v[:, at], mix[:, at]
        ks = kp * 0.125
        got = []
        for half in range(2):
            mask = lane_mask(half)
            s = mm(jnp.where(mask, kp, 0), qp, 1, 1)
            s = jnp.where(allowed, s, -1e30)
            e = jnp.exp(s - jnp.max(s, axis=0, keepdims=True))
            a = e * (1.0 / jnp.sum(e, axis=0, keepdims=True))
            t = a * mm(jnp.where(mask, vp, 0), gp, 1, 1)
            ds = (t - a * jnp.sum(t, axis=0, keepdims=True)).astype(BF16)
            got.append((mm(ds, ks, 0, 0), mm(ds, qp), mm(a.astype(BF16), gp)))
        for ref, first, last in zip((dq, dk, dv), got[0], got[1]):
            ref[:, at] = jnp.where(lane_mask(0), first, last).astype(BF16)
        return 0

    lax.fori_loop(0, HEADS // 2, pair, 0, unroll=True)


def attend_back(scal, lay, low, q, k, v, weights, start, count, so_far=()):
    n = len(weights)
    m = q.shape[0]
    win = m // lay.shape[0]
    blk = pl.BlockSpec((win, D), lambda i: (i + start, 0))
    return pl.pallas_call(
        functools.partial(attend_back_body, n, D // 32, start, len(so_far)),
        grid=(count,),
        in_specs=[SMEM, SMEM] + [blk] * 4 + [ANY] * (n + len(so_far)),
        out_specs=[blk] * 3,
        out_shape=[sds((m, D), BF16)] * 3,
        scratch_shapes=[
            pltpu.VMEM((D, D), BF16),
            pltpu.VMEM((win, D), BF16),
            pltpu.SemaphoreType.DMA,
        ],
        input_output_aliases={6 + n + j: j for j in range(len(so_far))},
        compiler_params=PARAMS,
    )(scal, lay, low, q, k, v, *weights, *so_far)


def first_body(n, rows, scal, dq, dk, dv, x, upper, slots, vec, *refs):
    weights, refs = refs[:n], refs[n:]
    out, slot_sums, sums, wq, wk, wv, sems = refs
    i = pl.program_id(0)

    @pl.when(i == 0)
    def _():
        for j, w in enumerate((wq, wk, wv)):
            src = weights if n == 8 else weights[j : j + 1]
            fetch(scal, src, w, sems.at[j], 8 + j * rows, rows)
        for j, w in enumerate((wq, wk, wv)):
            arrive(w, sems.at[j])

    e = mm(dq[...], wq[...], 1, 1) + mm(dk[...], wk[...], 1, 1) + mm(dv[...], wv[...], 1, 1)
    n1, r = normal_rows(stamp(x[...], slots, i))
    g = upper[...] + norm_back(e, n1, r, vec[GAIN1 : GAIN1 + 1, :])
    out[...] = g
    half = g.shape[0] // 2
    slot_sums[pl.ds(2 * i, 1), :] = total(g[:half])
    slot_sums[pl.ds(2 * i + 1, 1), :] = total(g[half:])
    accumulate(
        sums,
        i,
        [total(e * n1), total(e), total(dq[...].astype(F32)), total(dv[...].astype(F32))],
    )


def first_back(scal, dq, dk, dv, x, upper, slots, vec, weights, win):
    n = len(weights)
    m = x.shape[0]
    blk = pl.BlockSpec((win, D), lambda i: (i, 0))
    return pl.pallas_call(
        functools.partial(first_body, n, D // 32),
        grid=(m // win,),
        in_specs=[SMEM] + [blk] * 5 + [whole(slots.shape), whole(vec.shape)] + [ANY] * n,
        out_specs=[blk, whole(slots.shape), whole((8, D))],
        out_shape=[sds((m, D), F32), sds(slots.shape, F32), sds((8, D), F32)],
        scratch_shapes=[pltpu.VMEM((D, D), BF16)] * 3 + [pltpu.SemaphoreType.DMA((3,))],
        compiler_params=PARAMS,
    )(scal, dq, dk, dv, x, upper, slots, vec, *weights)


def down_body(n, rows, filled, scal, hidden, attended, vec, *refs):
    weights, refs = refs[:n], refs[n + filled :]
    out, wd, sems = refs
    i = pl.program_id(0)

    @pl.when(i == 0)
    def _():
        fetch(scal, weights, wd, sems, 0, rows)
        arrive(wd, sems)

    out[...] = attended[...] + mm(hidden[...], wd[...]) + vec[DADD : DADD + 1, :]


def down_out(scal, hidden, attended, vec, weights, win, start, count, rows=0, so_far=()):
    n = len(weights)
    m, ff = hidden.shape
    blk = pl.BlockSpec((win, D), lambda i: (i + start, 0))
    return pl.pallas_call(
        functools.partial(down_body, n, rows, len(so_far)),
        grid=(count,),
        in_specs=[SMEM, pl.BlockSpec((win, ff), lambda i: (i + start, 0)), blk, whole(vec.shape)]
        + [ANY] * (n + len(so_far)),
        out_specs=blk,
        out_shape=sds((m, D), F32),
        scratch_shapes=[pltpu.VMEM((ff, D), BF16), pltpu.SemaphoreType.DMA],
        input_output_aliases={4 + n: 0} if so_far else {},
        compiler_params=PARAMS,
    )(scal, hidden, attended, vec, *weights, *so_far)


def scatter_tile(scal, stage, keep, send, sem, blocks, rows, row, columns=False):
    f0, p0 = scal[0], scal[1]
    y, z, c, x = f0 & 1, f0 >> 1, p0 & 1, p0 >> 1
    for at, f in enumerate(blocks):
        dy, k = (f & 1) ^ y, (f >> 1) ^ z
        for px in range(2):
            dx = px ^ x
            for other, out in enumerate((keep, send)):
                core = c ^ other
                one = jnp.where(core == 0, dx, dy)
                two = jnp.where(core == 0, dy, dx)
                dst = out.at[one, two, k]
                piece = px * 2 + core
                if columns:
                    half = D // 2
                    for part in range(2):
                        pltpu.make_async_copy(
                            stage.at[pl.ds(pl.multiple_of((piece * 2 + part) * rows, 8), rows), :],
                            dst.at[pl.ds(row, rows), pl.ds(part * half, half)],
                            sem,
                        ).start()
                else:
                    src = pl.multiple_of((at * 4 + piece) * rows, 8)
                    pltpu.make_async_copy(
                        stage.at[pl.ds(src, rows), :], dst.at[pl.ds(row, rows), :], sem
                    ).start()


def wide_body(columns, scal, a, b, keep, send, stage, sems):
    i = pl.program_id(0)
    last = pl.num_programs(0) - 1
    slot = i & 1

    @pl.when(i >= 2)
    def _():
        arrive(stage.at[slot], sems.at[slot])

    tile = mm(a[...], b[...], 0, 0).astype(BF16)
    stage[slot] = tile
    rows = D // 8
    scatter_tile(scal, stage.at[slot], keep, send, sems.at[slot], [i], rows, 0, columns)

    @pl.when(i == last)
    def _():
        arrive(stage.at[1 - slot], sems.at[1 - slot])
        arrive(stage.at[slot], sems.at[slot])


def wide_grad(scal, a, b, columns):
    m = a.shape[0]
    half = D // 2
    full = pl.BlockSpec((m, D), lambda i: (0, 0))
    part = pl.BlockSpec((m, half), lambda i: (0, i))
    shape = sds((2, 2, 4, D // 8, D), BF16)
    return pl.pallas_call(
        functools.partial(wide_body, columns),
        grid=(8,),
        in_specs=[SMEM, full if columns else part, part if columns else full],
        out_specs=[ANY, ANY],
        out_shape=[shape, shape],
        scratch_shapes=[
            pltpu.VMEM((2, D, half) if columns else (2, half, D), BF16),
            pltpu.SemaphoreType.DMA((2,)),
        ],
        compiler_params=PARAMS,
    )(scal, a, b)


def square_body(scal, mixture, normed, low, dq, dk, dv, keep, send, stage, sems):
    rows = D // 32
    half = D // 2
    for j in range(8):
        m, part = j // 2, j % 2
        slot = j % 2
        if j >= 2:
            arrive(stage.at[slot], sems.at[slot])
        left = mixture if m == 0 else normed
        right = (low, dq, dk, dv)[m]
        stage[slot] = mm(left[:, part * half : (part + 1) * half], right[...], 0, 0).astype(BF16)
        blocks = [part * 4 + n for n in range(4)]
        scatter_tile(scal, stage.at[slot], keep, send, sems.at[slot], blocks, rows, m * rows)
    for slot in range(2):
        arrive(stage.at[slot], sems.at[slot])


def square_grads(scal, *args):
    shape = sds((2, 2, 4, D // 8, D), BF16)
    return pl.pallas_call(
        square_body,
        in_specs=[SMEM] + [pl.BlockSpec(memory_space=pltpu.VMEM)] * 6,
        out_specs=[ANY, ANY],
        out_shape=[shape, shape],
        scratch_shapes=[pltpu.VMEM((2, D // 2, D), BF16), pltpu.SemaphoreType.DMA((2,))],
        compiler_params=PARAMS,
    )(scal, *args)


BOTH = ("fsdp", "dp")


def flip(v, f_of=0, p_of=0):
    pairs = [
        (f * 4 + p, (f ^ f_of) * 4 + (p ^ p_of)) for f in range(8) for p in range(4)
    ]
    return lax.ppermute(v, BOTH, pairs)


def flip_by_core(v, first, second):
    pairs = []
    for f in range(8):
        for p in range(4):
            df, dp = second if p & 1 else first
            pairs.append((f * 4 + p, (f ^ df) * 4 + (p ^ dp)))
    return lax.ppermute(v, BOTH, pairs)


Y_OF, X_OF = (1, 0), (0, 2)


def up32(*vs):
    out = vs[0].astype(F32)
    for v in vs[1:]:
        out = out + v.astype(F32)
    return out


def together(*groups):
    flat, tree = jax.tree.flatten(groups)
    return jax.tree.unflatten(tree, lax.optimization_barrier(tuple(flat)))


def flips_z(v):
    return [flip(v[k], 2 * k) for k in (1, 2, 3)]


class Gather:
    def along_z(self, piece):
        self.now = [piece] + flips_z([piece] * 4)

    def along_xy(self):
        self.held = jnp.stack(self.now)
        self.now = [flip_by_core(self.held, Y_OF, X_OF), flip_by_core(self.held, X_OF, Y_OF)]

    def along_rest(self):
        one, two = self.now
        self.mine = [self.held, one, two]
        self.now = [flip_by_core(one, X_OF, Y_OF)] + [flip(v, 0, 1) for v in self.mine]

    def along_core(self):
        three, *others = self.now
        self.all = self.mine + [three] + others
        self.now = flip(three, 0, 1)

    def done(self):
        return self.all + [self.now]


class Sum:
    def along_core(self, keep, send):
        self.keep = keep
        self.now = flip(send, 0, 1)

    def along_first(self):
        self.r = self.now
        part = up32(self.keep[1], self.r[1]).astype(BF16)
        self.now = flip_by_core(part, X_OF, Y_OF)

    def along_second(self):
        self.r1 = self.now
        part = up32(self.keep[0, 1], self.r[0, 1], self.r1[1]).astype(BF16)
        self.now = flip_by_core(part, Y_OF, X_OF)

    def along_z(self):
        self.r2 = self.now
        parts = [
            up32(self.keep[0, 0, k], self.r[0, 0, k], self.r1[0, k], self.r2[k]) for k in range(4)
        ]
        self.own = parts[0]
        self.now = flips_z([t.astype(BF16) for t in parts])

    def back_x(self):
        self.own = up32(self.own, *self.now).astype(BF16)
        self.now = flip(self.own, 0, 2)

    def back_core(self):
        self.over = self.now
        self.now = [flip(self.own, 0, 1), flip(self.over, 0, 1)]

    def done(self):
        return order_dp((self.own, self.now[0], self.over, self.now[1]))


def order_dp(parts):
    p = lax.axis_index("dp")
    low, high = (p & 1) == 1, (p >> 1) == 1
    a, b, c, d = parts
    a, b, c, d = (
        jnp.where(low, b, a),
        jnp.where(low, a, b),
        jnp.where(low, d, c),
        jnp.where(low, c, d),
    )
    return (
        jnp.where(high, c, a),
        jnp.where(high, d, b),
        jnp.where(high, a, c),
        jnp.where(high, b, d),
    )


def spread_dp(done):
    over = flip(done, 0, 2)
    return order_dp((done, flip(done, 0, 1), over, flip(over, 0, 1)))


def on_device(
    sizes,
    inputs,
    cotangent,
    timesteps,
    layouts,
    step_table,
    first_gain,
    first_shift,
    query_matrix,
    query_bias,
    key_matrix,
    value_matrix,
    value_bias,
    out_matrix,
    out_bias,
    second_gain,
    second_shift,
    up_matrix,
    up_bias,
    down_matrix,
    down_bias,
):
    n_fsdp, n_dp = sizes
    fast = (n_fsdp, n_dp) == (8, 4)
    f, p = lax.axis_index("fsdp"), lax.axis_index("dp")
    scal = jnp.stack([f, p]).astype(jnp.int32)
    row_count = inputs.shape[0]
    win = row_count // layouts.shape[0]
    ff = up_matrix.shape[1] * n_fsdp
    steps = step_table.shape[0]
    pairs = timesteps.reshape(-1, 2)
    first_steps = pairs[:, 0]
    second_steps = jnp.where(layouts == 1, first_steps, pairs[:, 1])
    slot_steps = jnp.stack([first_steps, second_steps], axis=1).reshape(-1)
    vecs = (
        first_gain,
        first_shift,
        query_bias,
        value_bias,
        out_bias,
        second_gain,
        second_shift,
        down_bias,
        up_bias,
    )
    mats = (query_matrix, key_matrix, value_matrix, out_matrix, up_matrix, down_matrix)
    r = D // 32
    if fast:
        return exchange_and_run(
            scal, inputs, cotangent, layouts, step_table, slot_steps, vecs, mats, win, ff, f
        )
    cot_low = cotangent.astype(BF16)
    low = [m.astype(BF16) for m in vecs + mats]
    full = [lax.all_gather(m, "fsdp", axis=0, tiled=True) for m in low[:9]]
    vec = jnp.concatenate(full).reshape(12, D).astype(F32)
    w_qkv = [lax.all_gather(m, "fsdp", axis=0, tiled=True) for m in low[9:12]]
    w_out = [lax.all_gather(low[12], "fsdp", axis=0, tiled=True)]
    w_up = [lax.all_gather(low[13], "fsdp", axis=1, tiled=True)]
    w_down = [lax.all_gather(low[14], "fsdp", axis=0, tiled=True)]
    table = lax.all_gather(step_table.astype(BF16), "fsdp", axis=1, tiled=True)
    rel = jnp.take(table, slot_steps, axis=0).astype(F32)
    count = layouts.shape[0]

    normed, q, k, v, slots, vec = qkv(scal, inputs, rel, w_qkv, vec, win)
    mixture = attend(scal, layouts, q, k, v)
    attended, second = mix(scal, mixture, inputs, slots, vec, w_out, win)
    hidden, slope = up_gelu(scal, second, vec, w_up, ff)
    pre, up_add = pre_grad(scal, cot_low, slope, w_down)
    grad, low, sums2 = second_back(scal, pre, attended, cotangent, vec, w_up, win)
    dq, dk, dv = attend_back(scal, layouts, low, q, k, v, w_out, 0, count)
    input_grad, slot_sums, sums1 = first_back(
        scal, dq, dk, dv, inputs, grad, slots, vec, w_qkv, win
    )
    block_output = down_out(scal, hidden, attended, vec, w_down, win, 0, count)

    total_of = lambda v, dim: lax.psum(
        lax.psum_scatter(v, "fsdp", scatter_dimension=dim, tiled=True), "dp"
    )
    down_grad = total_of(mm(hidden, cot_low, 0, 0), 0)
    up_grad = total_of(mm(second, pre, 0, 0), 1)
    out_grad = total_of(mm(mixture, low, 0, 0), 0)
    query_grad = total_of(mm(normed, dq, 0, 0), 0)
    key_grad = total_of(mm(normed, dk, 0, 0), 0)
    value_grad = total_of(mm(normed, dv, 0, 0), 0)
    small = lax.psum(vector_sums(sums1, sums2, up_add), BOTH)
    table_grad = total_of(jnp.zeros((steps, D), F32).at[slot_steps].add(slot_sums), 1)
    return results(
        block_output, input_grad, table_grad, small, f, n_fsdp, ff,
        query_grad, key_grad, value_grad, out_grad, up_grad, down_grad,
    )


def vector_sums(sums1, sums2, up_add):
    return jnp.concatenate(
        [sums1[:4], sums2[2:3], sums2[:2], sums2[3:4], up_add.reshape(-1, D)], axis=0
    )


def results(
    block_output, input_grad, table_grad, small, f, n_fsdp, ff,
    query_grad, key_grad, value_grad, out_grad, up_grad, down_grad,
):
    width = D // n_fsdp
    mine = lax.dynamic_slice(small[:8], (0, f * width), (8, width))
    up_mine = lax.dynamic_slice(small[8:].reshape(-1), (f * (ff // n_fsdp),), (ff // n_fsdp,))
    return (
        block_output,
        input_grad,
        table_grad,
        mine[0],
        mine[1],
        query_grad,
        mine[2],
        key_grad,
        value_grad,
        mine[3],
        out_grad,
        mine[4],
        mine[5],
        mine[6],
        up_grad,
        up_mine,
        down_grad,
        mine[7],
    )


def exchange_and_run(
    scal, inputs, cotangent, layouts, step_table, slot_steps, vecs, mats, win, ff, f
):
    r = D // 32
    at_up = dict(row=r, rows=D // 8)
    at_down = dict(rows=D // 8)
    one, two, three = Gather(), Gather(), Gather()

    pieces = prep(scal, vecs, mats)
    y_steps = jnp.stack([slot_steps, flip(slot_steps, 1)])
    pieces, y_steps = together(pieces, y_steps)

    one.along_z(pieces[0])
    z_steps = flips_z([y_steps] * 4)
    cot_low = cotangent.astype(BF16)
    one.now, z_steps, cot_low, pieces = together(one.now, z_steps, cot_low, pieces)

    one.along_xy()
    all_steps = jnp.stack([y_steps] + z_steps)
    asked = jnp.take(step_table, all_steps, axis=0).astype(BF16)
    back = jnp.stack([asked[0]] + flips_z(asked))
    two.along_z(pieces[1])
    one.now, back = together(one.now, back)

    one.along_rest()
    given = jnp.stack([back[:, 0], flip(back[:, 1], 1)], axis=1)
    one.now, given, two.now, pieces = together(one.now, given, two.now, pieces)

    one.along_core()
    rel = given.reshape(8, given.shape[2], given.shape[3]).astype(F32)
    two.along_xy()
    three.along_z(pieces[2])
    one.now, rel = together(one.now, rel)

    w_qkv = one.done()
    normed, q, k, v, slots, vec = qkv(scal, inputs, rel, w_qkv, None, win)
    q, k, v, two.now, three.now = together(q, k, v, two.now, three.now)

    two.along_rest()
    three.along_xy()
    mixture = attend(scal, layouts, q, k, v)
    mixture, two.now, three.now = together(mixture, two.now, three.now)

    two.along_core()
    three.along_rest()
    mixture, two.now = together(mixture, two.now)

    w_two = two.done()
    attended, second = mix(scal, mixture, inputs, slots, vec, w_two, win)
    attended, second, three.now = together(attended, second, three.now)

    three.along_core()
    hidden, slope = up_gelu(scal, second, vec, w_two, ff, **at_up)
    hidden, slope, three.now = together(hidden, slope, three.now)

    w_down = three.done()
    down = Sum()
    kept = wide_grad(scal, hidden, cot_low, False)
    kept, slope = together(kept, slope)

    down.along_core(*kept)
    pre, up_add = pre_grad(scal, cot_low, slope, w_down, **at_down)
    pre, down.now = together(pre, down.now)

    down.along_first()
    grad, low, sums2 = second_back(scal, pre, attended, cotangent, vec, w_two, win, **at_up)
    grad, low, pre, down.now = together(grad, low, pre, down.now)

    down.along_second()
    up = Sum()
    kept = wide_grad(scal, second, pre, True)
    kept, low, down.now = together(kept, low, down.now)

    down.along_z()
    up.along_core(*kept)
    halves = layouts.shape[0] // 2
    back1 = attend_back(scal, layouts, low, q, k, v, w_two, 0, halves)
    back1, down.now, up.now = together(back1, down.now, up.now)

    down.back_x()
    up.along_first()
    dq, dk, dv = attend_back(scal, layouts, low, q, k, v, w_two, halves, halves, back1)
    dq, dk, dv, down.now, up.now = together(dq, dk, dv, down.now, up.now)

    down.back_core()
    up.along_second()
    square = Sum()
    kept = square_grads(scal, mixture, normed, low, dq, dk, dv)
    kept, dq, dk, dv, down.now, up.now = together(kept, dq, dk, dv, down.now, up.now)

    up.along_z()
    square.along_core(*kept)
    input_grad, slot_sums, sums1 = first_back(
        scal, dq, dk, dv, inputs, grad, slots, vec, w_qkv, win
    )
    small = vector_sums(sums1, sums2, up_add)
    own = slot_sums.reshape(-1, 8, D // 8)
    sums = jnp.stack([lax.dynamic_index_in_dim(own, f ^ j, 1, False) for j in range(8)])
    sums = sums.reshape(4, 2, *sums.shape[1:])
    small, sums, hidden, square.now, up.now = together(small, sums, hidden, square.now, up.now)

    up.back_x()
    square.along_first()
    small_z = flips_z([small] * 4)
    sums_y = flip(sums[:, 1], 1)
    part = down_out(scal, hidden, attended, vec, w_down, win, 0, halves, **at_down)
    part, small_z, sums_y, up.now, square.now = together(part, small_z, sums_y, up.now, square.now)

    up.back_core()
    square.along_second()
    small = small + (small_z[0] + small_z[1] + small_z[2])
    small_y = flip(small, 1)
    sums = jnp.stack([sums[:, 0], sums_y], axis=1)
    sums_z = flips_z(sums)
    block_output = down_out(
        scal, hidden, attended, vec, w_down, win, halves, halves, so_far=(part,), **at_down
    )
    block_output, small_y, sums_z, up.now, square.now = together(
        block_output, small_y, sums_z, up.now, square.now
    )

    square.along_z()
    small = small + small_y
    small_x = flip(small, 0, 2)
    fsdp_sums = jnp.stack([sums[0]] + sums_z).reshape(-1, D // 8)
    fsdp_steps = all_steps.reshape(-1)
    x_sums, x_steps = flip(fsdp_sums, 0, 2), flip(fsdp_steps, 0, 2)
    square.now, small_x, x_sums, x_steps = together(square.now, small_x, x_sums, x_steps)

    square.back_x()
    small = small + small_x
    small = small + flip(small, 0, 1)
    every = [
        jnp.concatenate(order_dp((a, flip(a, 0, 1), b, flip(b, 0, 1))))
        for a, b in ((fsdp_sums, x_sums), (fsdp_steps, x_steps))
    ]
    table_grad = jnp.zeros((step_table.shape[0], D // 8), F32).at[every[1]].add(every[0])
    half = D // 2
    down_grad = jnp.concatenate(down.done(), axis=0).astype(F32)
    up_grad = jnp.concatenate(
        [t for m in up.done() for t in (m[:, :half], m[:, half:])], axis=0
    ).astype(F32)
    square.now, small, table_grad, down_grad, up_grad = together(
        square.now, small, table_grad, down_grad, up_grad
    )

    square.back_core()
    out_grad, query_grad, key_grad, value_grad = (
        jnp.concatenate([m[j * r : (j + 1) * r] for m in square.done()], axis=0).astype(F32)
        for j in range(4)
    )
    return results(
        block_output, input_grad, table_grad, small, f, 8, ff,
        query_grad, key_grad, value_grad, out_grad, up_grad, down_grad,
    )


def solution(mesh):
    rows = P(("fsdp", "dp"), None)
    slots = P(("fsdp", "dp"))
    vector = P("fsdp")
    matrix = P("fsdp", None)
    wide = P(None, "fsdp")
    placed = (
        rows, rows, slots, slots, wide, vector, vector, matrix, vector, matrix,
        matrix, vector, matrix, vector, vector, vector, wide, vector, matrix, vector,
    )
    returned = (
        rows, rows, wide, vector, vector, matrix, vector, matrix, matrix, vector,
        matrix, vector, vector, vector, wide, vector, matrix, vector,
    )
    return jax.shard_map(
        functools.partial(on_device, (mesh.shape["fsdp"], mesh.shape["dp"])),
        mesh=mesh,
        in_specs=placed,
        out_specs=returned,
        check_vma=False,
    )
```

```python
import functools
import math

import jax
import jax.numpy as jnp
from jax import lax
from jax.experimental import pallas as pl
from jax.experimental.pallas import tpu as pltpu
from jax.sharding import PartitionSpec as P

HEADS = 12
HEAD = 64
D = HEADS * HEAD
F32 = jnp.float32
BF16 = jnp.bfloat16
ANY = pl.BlockSpec(memory_space=pl.ANY)
SMEM = pl.BlockSpec(memory_space=pltpu.SMEM)
PARAMS = pltpu.CompilerParams(vmem_limit_bytes=60 * 1024 * 1024)

TAIL_P = 0.21
TAIL = (
    0.08371157580586816,
    0.08506885523539415,
    0.06919219089790565,
    0.12487264009661635,
    -0.09392498913162721,
    0.349400678909721,
    -0.33025308461653297,
    0.2835884168453487,
    -0.07165627723466013,
)

GAIN1, SHIFT1, QADD, VADD, OADD, GAIN2, SHIFT2, DADD, UADD = range(9)


def whole(shape):
    return pl.BlockSpec(shape, lambda *_: (0,) * len(shape))


def sds(shape, dtype):
    return jax.ShapeDtypeStruct(shape, dtype)


def mm(a, b, ca=1, cb=0):
    return lax.dot_general(a, b, (((ca,), (cb,)), ((), ())), preferred_element_type=F32)


def place(scal, buf, other, k):
    f, p = scal[0], scal[1]
    y, z, c, x = f & 1, f >> 1, p & 1, p >> 1
    core = c ^ other
    by_y = 1 - core if buf == 1 else core if buf == 2 else buf // 3
    by_x = core if buf == 1 else 1 - core if buf == 2 else buf // 3
    return ((z ^ k) << 1) | (y ^ by_y), ((x ^ by_x) << 1) | core


def fetch(scal, refs, dst, sem, row=0, rows=0, columns=False, parts=range(4)):
    if len(refs) == 1 and len(parts) == 4:
        pltpu.make_async_copy(refs[0], dst, sem).start()
        return
    if len(refs) == 1:
        size = dst.shape[columns] // 4
        at = pl.ds(pl.multiple_of((parts[0] ^ (scal[0] >> 1)) * size, size), size)
        at = (slice(None), at) if columns else (at, slice(None))
        pltpu.make_async_copy(refs[0].at[at], dst.at[at], sem).start()
        return
    for other in range(2):
        for buf in range(4):
            for k in parts:
                f, p = place(scal, buf, other, k)
                src = refs[other * 4 + buf].at[k]
                if columns:
                    half = D // 2
                    for part in range(2):
                        r = pl.multiple_of(p * 2 * rows + part * rows, 8)
                        pltpu.make_async_copy(
                            src.at[pl.ds(row, rows), pl.ds(part * half, half)],
                            dst.at[pl.ds(r, rows), pl.ds(pl.multiple_of(f * half, 128), half)],
                            sem,
                        ).start()
                else:
                    r = pl.multiple_of((f * 4 + p) * rows, 8)
                    pltpu.make_async_copy(
                        src.at[pl.ds(row, rows), :], dst.at[pl.ds(r, rows), :], sem
                    ).start()


def arrive(dst, sem):
    pltpu.make_async_copy(dst, dst, sem).wait()


def prep_body(scal, *refs):
    vecs, (q, k, v, o, up, down), (one, two, three) = refs[:9], refs[9:15], refs[15:]
    up_add = vecs[8][...]
    left = jnp.concatenate([r[...] for r in vecs[:8]], axis=0)
    left = jnp.concatenate([left, jnp.zeros((8, D // 2 - left.shape[1]), F32)], axis=1)
    right = jnp.concatenate([up_add, jnp.zeros((7, D // 2), F32)], axis=0)
    one[0:8, :] = jnp.concatenate([left, right], axis=1).astype(BF16)
    r = q.shape[0]
    for i, m in enumerate((q, k, v)):
        one[8 + i * r : 8 + (i + 1) * r, :] = m[...].astype(BF16)
    two[0:r, :] = o[...].astype(BF16)
    u = up.shape[0] // 2
    two[r : r + u, 0 : D // 2] = up[0:u, :].astype(BF16)
    two[r : r + u, D // 2 : D] = up[u : 2 * u, :].astype(BF16)
    three[...] = down[...].astype(BF16)


def prep(scal, vecs, mats):
    q, up, down = mats[0], mats[4], mats[5]
    r, u, d = q.shape[0] // 4, up.shape[0] // 4, down.shape[0] // 4
    half = up.shape[1]
    mine = lambda rows, cols: pl.BlockSpec((rows, cols), lambda i, s: (s[1], 0))
    vecs = [v.reshape(1, -1) for v in vecs]
    return pl.pallas_call(
        prep_body,
        grid_spec=pltpu.PrefetchScalarGridSpec(
            num_scalar_prefetch=1,
            grid=(1,),
            in_specs=[pl.BlockSpec(v.shape, lambda i, s: (0, 0)) for v in vecs]
            + [mine(r, D)] * 4
            + [mine(u, half), mine(d, D)],
            out_specs=[
                pl.BlockSpec(s, lambda i, s_: (0, 0))
                for s in ((8 + 3 * r, D), (r + u // 2, D), (d, D))
            ],
        ),
        out_shape=(sds((8 + 3 * r, D), BF16), sds((r + u // 2, D), BF16), sds((d, D), BF16)),
        compiler_params=PARAMS,
    )(scal, *vecs, *mats)


def normal_rows(v):
    c = v - jnp.mean(v, axis=-1, keepdims=True)
    r = lax.rsqrt(jnp.mean(c * c, axis=-1, keepdims=True) + 1e-05)
    return c * r, r


def stamp(x, slots, i):
    half = x.shape[0] // 2
    return jnp.concatenate(
        [x[:half] + slots[pl.ds(2 * i, 1), :], x[half:] + slots[pl.ds(2 * i + 1, 1), :]], axis=0
    )


def qkv_body(n, shape, scal, x, rel, *refs):
    weights, refs = refs[:n], refs[n:]
    if n != 8:
        vec_in, refs = refs[0], refs[1:]
    normed, q, k, v, slots_out, vec_out, wq, wk, wv, small, sems = refs
    i = pl.program_id(0)

    @pl.when(i == 0)
    def _():
        if n == 8:
            rows = shape
            for j, w in enumerate((wq, wk, wv)):
                fetch(scal, weights, w, sems.at[j], 8 + j * rows, rows)
            for buf in range(4):
                for z in range(4):
                    f, _ = place(scal, buf, 0, z)
                    if buf in (0, 1, 2):
                        pass
                    pltpu.make_async_copy(
                        weights[buf].at[z, pl.ds(0, 8), :], small.at[buf * 4 + z], sems.at[3]
                    ).start()
            f0 = scal[0]
            slots_out[...] = jnp.concatenate([rel[f0 ^ f] for f in range(8)], axis=1)
            arrive(small, sems.at[3])
            core = scal[1] & 1
            flip = jnp.where(core == 0, 1, 2)
            parts = []
            for f in range(8):
                zz = (f >> 1) ^ (f0 >> 1)
                yy = (f & 1) ^ (f0 & 1)
                parts.append(small[yy * flip * 4 + zz].astype(F32))
            vec_out[0:8, :] = jnp.concatenate([t[:, : D // 8] for t in parts], axis=1)
            for j in range(4):
                vec_out[8 + j : 9 + j, :] = jnp.concatenate(
                    [parts[2 * j][0:1, D // 2 :], parts[2 * j + 1][0:1, D // 2 :]], axis=1
                )
        else:
            for j, w in enumerate((wq, wk, wv)):
                fetch(scal, weights[j : j + 1], w, sems.at[j])
            slots_out[...] = rel[...]
            vec_out[...] = vec_in[...]
        for j, w in enumerate((wq, wk, wv)):
            arrive(w, sems.at[j])

    n1, _ = normal_rows(stamp(x[...], slots_out, i))
    low = (n1 * vec_out[GAIN1 : GAIN1 + 1, :] + vec_out[SHIFT1 : SHIFT1 + 1, :]).astype(BF16)
    normed[...] = low
    q[...] = (mm(low, wq[...]) + vec_out[QADD : QADD + 1, :]).astype(BF16)
    k[...] = mm(low, wk[...]).astype(BF16)
    v[...] = (mm(low, wv[...]) + vec_out[VADD : VADD + 1, :]).astype(BF16)


def qkv(scal, x, rel, weights, vec, win):
    rows = x.shape[0]
    slots = 2 * (rows // win)
    n = len(weights)
    blk = pl.BlockSpec((win, D), lambda i: (i, 0))
    ins = [SMEM, blk, whole(rel.shape)] + [ANY] * n
    args = [scal, x, rel, *weights]
    if n != 8:
        ins.append(whole(vec.shape))
        args.append(vec)
    return pl.pallas_call(
        functools.partial(qkv_body, n, D // 32),
        grid=(rows // win,),
        in_specs=ins,
        out_specs=[blk] * 4 + [whole((slots, D)), whole((12, D))],
        out_shape=[sds((rows, D), BF16)] * 4 + [sds((slots, D), F32), sds((12, D), F32)],
        scratch_shapes=[pltpu.VMEM((D, D), BF16)] * 3
        + [pltpu.VMEM((16, 8, D), BF16), pltpu.SemaphoreType.DMA((4,))],
        compiler_params=PARAMS,
    )(*args)


def lane_mask(half):
    lane = lax.broadcasted_iota(jnp.int32, (1, 2 * HEAD), 1)
    return (lane >= HEAD) if half else (lane < HEAD)


def permitted(win, layout):
    a = lax.broadcasted_iota(jnp.int32, (win, win), 0) // (win // 2)
    b = lax.broadcasted_iota(jnp.int32, (win, win), 1) // (win // 2)
    return (a == b) | (layout == 1)


def attend_body(scal, lay, q, k, v, mixture):
    allowed = permitted(q.shape[0], lay[pl.program_id(0)])

    def pair(j, _):
        at = pl.ds(pl.multiple_of(j * 2 * HEAD, 2 * HEAD), 2 * HEAD)
        qp, kp, vp = q[:, at] * 0.125, k[:, at], v[:, at]
        got = []
        for half in range(2):
            s = mm(jnp.where(lane_mask(half), qp, 0), kp, 1, 1)
            s = jnp.where(allowed, s, -1e30)
            e = jnp.exp(s - jnp.max(s, axis=-1, keepdims=True))
            a = e * (1.0 / jnp.sum(e, axis=-1, keepdims=True))
            got.append(mm(a.astype(BF16), vp))
        mixture[:, at] = jnp.where(lane_mask(0), got[0], got[1]).astype(BF16)
        return 0

    lax.fori_loop(0, HEADS // 2, pair, 0, unroll=True)


def attend(scal, lay, q, k, v):
    rows = q.shape[0]
    win = rows // lay.shape[0]
    blk = pl.BlockSpec((win, D), lambda i: (i, 0))
    return pl.pallas_call(
        attend_body,
        grid=(rows // win,),
        in_specs=[SMEM, SMEM] + [blk] * 3,
        out_specs=blk,
        out_shape=sds((rows, D), BF16),
        compiler_params=PARAMS,
    )(scal, lay, q, k, v)


def mix_body(n, rows, scal, mixture, x, slots, vec, *refs):
    weights, refs = refs[:n], refs[n:]
    attended, second, wo, sems = refs
    i = pl.program_id(0)

    @pl.when(i == 0)
    def _():
        fetch(scal, weights, wo, sems, 0, rows)
        arrive(wo, sems)

    att = stamp(x[...], slots, i) + mm(mixture[...], wo[...]) + vec[OADD : OADD + 1, :]
    attended[...] = att
    n2, _ = normal_rows(att)
    second[...] = (n2 * vec[GAIN2 : GAIN2 + 1, :] + vec[SHIFT2 : SHIFT2 + 1, :]).astype(BF16)


def mix(scal, mixture, x, slots, vec, weights, win):
    rows = x.shape[0]
    n = len(weights)
    blk = pl.BlockSpec((win, D), lambda i: (i, 0))
    return pl.pallas_call(
        functools.partial(mix_body, n, D // 32),
        grid=(rows // win,),
        in_specs=[SMEM, blk, blk, whole(slots.shape), whole(vec.shape)] + [ANY] * n,
        out_specs=[blk] * 2,
        out_shape=[sds((rows, D), F32), sds((rows, D), BF16)],
        scratch_shapes=[pltpu.VMEM((D, D), BF16), pltpu.SemaphoreType.DMA],
        compiler_params=PARAMS,
    )(scal, mixture, x, slots, vec, *weights)


TILE = 256


def mlp_body(n, row_up, rows, scal, second, cot, vec, *refs):
    w_up, w_down, refs = refs[:n], refs[n : 2 * n], refs[2 * n :]
    hidden, low, add, wu, wd, pre_a, pre_b, grad_a, grad_b, sems = refs
    i = pl.program_id(0)
    last = pl.num_programs(0) - 1
    across = D // TILE
    units = (second.shape[0] // TILE) * across
    own = scal[0] >> 1

    def wait(g):
        arrive(wu.at[:, pl.ds(0, D)], sems.at[0, g])
        arrive(wd.at[pl.ds(0, D), :], sems.at[1, g])

    def tile(u):
        r = pl.multiple_of((u // across) * TILE, TILE)
        return pl.ds(r, TILE), (u % across) * TILE

    def multiply(step, u, pre, grad):
        at, col = tile(u)
        cols = pl.ds(pl.multiple_of((step ^ own) * D + col, TILE), TILE)
        pre[...] = mm(second[at, :], wu[:, cols])
        grad[...] = mm(cot[at, :], wd[cols, :], 1, 1)

    def finish(n, pre, grad):
        at, col = tile(n)
        cols = pl.ds(pl.multiple_of(col, TILE), TILE)
        u = pre[...] + vec[pl.ds(8 + (i ^ own), 1), cols]
        a = jnp.abs(u)
        t = 1.0 / (1.0 + TAIL_P * a)
        e = jnp.exp(-0.5 * (u * u))
        acc = jnp.full_like(t, TAIL[-1])
        for c in TAIL[-2::-1]:
            acc = acc * t + c
        tail = e * (t * acc)
        cdf = jnp.where(u >= 0, 1.0 - tail, tail)
        hidden[at, cols] = (u * cdf).astype(BF16)
        slope = cdf + u * (e * (1.0 / math.sqrt(2.0 * math.pi)))
        g = (grad[...] * slope).astype(BF16)
        low[at, cols] = g
        add[:, cols] = jnp.where(n < across, 0.0, add[:, cols]) + total(g.astype(F32))

    @pl.when(i == 0)
    def _():
        for g in range(4):
            fetch(scal, w_up, wu, sems.at[0, g], row_up, rows, True, [g])
            fetch(scal, w_down, wd, sems.at[1, g], 0, rows, False, [g])
        wait(0)
        multiply(0, 0, pre_a, grad_a)

    @pl.when(i != last)
    def _():
        wait(i + 1)

    def two(p, _):
        n = 2 * p
        multiply(i, n + 1, pre_b, grad_b)
        finish(n, pre_a, grad_a)
        over = n + 2 == units
        multiply(jnp.where(over, jnp.minimum(i + 1, last), i), jnp.where(over, 0, n + 2), pre_a, grad_a)
        finish(n + 1, pre_b, grad_b)
        return 0

    lax.fori_loop(0, units // 2, two, 0)


def mlp(scal, second, cot, vec, w_up, w_down, ff, row_up=0, rows=0):
    n = len(w_up)
    m = second.shape[0]
    blk = lambda rows: pl.BlockSpec((rows, D), lambda i, s: (0, i ^ (s[0] >> 1)))
    tile = pltpu.VMEM((TILE, TILE), F32)
    return pl.pallas_call(
        functools.partial(mlp_body, n, row_up, rows),
        grid_spec=pltpu.PrefetchScalarGridSpec(
            num_scalar_prefetch=1,
            grid=(ff // D,),
            in_specs=[whole(second.shape), whole(cot.shape), whole(vec.shape)] + [ANY] * (2 * n),
            out_specs=[blk(m), blk(m), blk(1)],
            scratch_shapes=[pltpu.VMEM((D, ff), BF16), pltpu.VMEM((ff, D), BF16)]
            + [tile] * 4
            + [pltpu.SemaphoreType.DMA((2, 4))],
        ),
        out_shape=[sds((m, ff), BF16), sds((m, ff), BF16), sds((1, ff), F32)],
        compiler_params=PARAMS,
    )(scal, second, cot, vec, *w_up, *w_down)


def norm_back(e, n, r, gain):
    f = e * gain
    return r * (f - jnp.mean(f, -1, keepdims=True) - n * jnp.mean(f * n, -1, keepdims=True))


def total(v):
    return jnp.sum(v, axis=0, keepdims=True)


def accumulate(ref, i, rows):
    new = jnp.concatenate(rows + [jnp.zeros((8 - len(rows), D), F32)], axis=0)

    @pl.when(i == 0)
    def _():
        ref[...] = new

    @pl.when(i != 0)
    def _():
        ref[...] += new


def second_body(n, row, rows, scal, pre, attended, cot, vec, *refs):
    weights, refs = refs[:n], refs[n:]
    grad, low, sums, wu, sems = refs
    i = pl.program_id(0)

    @pl.when(i == 0)
    def _():
        fetch(scal, weights, wu, sems, row, rows, True)
        arrive(wu, sems)

    e = mm(pre[...], wu[...], 1, 1)
    n2, r = normal_rows(attended[...])
    c = cot[...]
    g = c + norm_back(e, n2, r, vec[GAIN2 : GAIN2 + 1, :])
    grad[...] = g
    low[...] = g.astype(BF16)
    accumulate(sums, i, [total(e * n2), total(e), total(g), total(c)])


def second_back(scal, pre, attended, cot, vec, weights, win, row=0, rows=0):
    n = len(weights)
    m, ff = pre.shape
    blk = pl.BlockSpec((win, D), lambda i: (i, 0))
    return pl.pallas_call(
        functools.partial(second_body, n, row, rows),
        grid=(m // win,),
        in_specs=[SMEM, pl.BlockSpec((win, ff), lambda i: (i, 0)), blk, blk, whole(vec.shape)]
        + [ANY] * n,
        out_specs=[blk, blk, whole((8, D))],
        out_shape=[sds((m, D), F32), sds((m, D), BF16), sds((8, D), F32)],
        scratch_shapes=[pltpu.VMEM((D, ff), BF16), pltpu.SemaphoreType.DMA],
        compiler_params=PARAMS,
    )(scal, pre, attended, cot, vec, *weights)


def attend_back_body(n, rows, start, filled, scal, lay, low, q, k, v, *refs):
    weights, refs = refs[:n], refs[n + filled :]
    dq, dk, dv, wo, mix, sems = refs
    i = pl.program_id(0)

    @pl.when(i == 0)
    def _():
        fetch(scal, weights, wo, sems, 0, rows)
        arrive(wo, sems)

    mix[...] = mm(low[...], wo[...], 1, 1).astype(BF16)
    win = q.shape[0]
    allowed = permitted(win, lay[i + start])

    def pair(j, _):
        at = pl.ds(pl.multiple_of(j * 2 * HEAD, 2 * HEAD), 2 * HEAD)
        qp, kp, vp, gp = q[:, at] * 0.125, k[:, at], v[:, at], mix[:, at]
        ks = kp * 0.125
        got = []
        for half in range(2):
            mask = lane_mask(half)
            s = mm(jnp.where(mask, kp, 0), qp, 1, 1)
            s = jnp.where(allowed, s, -1e30)
            e = jnp.exp(s - jnp.max(s, axis=0, keepdims=True))
            a = e * (1.0 / jnp.sum(e, axis=0, keepdims=True))
            t = a * mm(jnp.where(mask, vp, 0), gp, 1, 1)
            ds = (t - a * jnp.sum(t, axis=0, keepdims=True)).astype(BF16)
            got.append((mm(ds, ks, 0, 0), mm(ds, qp), mm(a.astype(BF16), gp)))
        for ref, first, last in zip((dq, dk, dv), got[0], got[1]):
            ref[:, at] = jnp.where(lane_mask(0), first, last).astype(BF16)
        return 0

    lax.fori_loop(0, HEADS // 2, pair, 0, unroll=True)


def attend_back(scal, lay, low, q, k, v, weights, start, count, so_far=()):
    n = len(weights)
    m = q.shape[0]
    win = m // lay.shape[0]
    blk = pl.BlockSpec((win, D), lambda i: (i + start, 0))
    return pl.pallas_call(
        functools.partial(attend_back_body, n, D // 32, start, len(so_far)),
        grid=(count,),
        in_specs=[SMEM, SMEM] + [blk] * 4 + [ANY] * (n + len(so_far)),
        out_specs=[blk] * 3,
        out_shape=[sds((m, D), BF16)] * 3,
        scratch_shapes=[
            pltpu.VMEM((D, D), BF16),
            pltpu.VMEM((win, D), BF16),
            pltpu.SemaphoreType.DMA,
        ],
        input_output_aliases={6 + n + j: j for j in range(len(so_far))},
        compiler_params=PARAMS,
    )(scal, lay, low, q, k, v, *weights, *so_far)


def first_body(n, rows, scal, dq, dk, dv, x, upper, slots, vec, *refs):
    weights, refs = refs[:n], refs[n:]
    out, slot_sums, sums, wq, wk, wv, sems = refs
    i = pl.program_id(0)

    @pl.when(i == 0)
    def _():
        for j, w in enumerate((wq, wk, wv)):
            src = weights if n == 8 else weights[j : j + 1]
            fetch(scal, src, w, sems.at[j], 8 + j * rows, rows)
        for j, w in enumerate((wq, wk, wv)):
            arrive(w, sems.at[j])

    e = mm(dq[...], wq[...], 1, 1) + mm(dk[...], wk[...], 1, 1) + mm(dv[...], wv[...], 1, 1)
    n1, r = normal_rows(stamp(x[...], slots, i))
    g = upper[...] + norm_back(e, n1, r, vec[GAIN1 : GAIN1 + 1, :])
    out[...] = g
    half = g.shape[0] // 2
    slot_sums[pl.ds(2 * i, 1), :] = total(g[:half])
    slot_sums[pl.ds(2 * i + 1, 1), :] = total(g[half:])
    accumulate(
        sums,
        i,
        [total(e * n1), total(e), total(dq[...].astype(F32)), total(dv[...].astype(F32))],
    )


def first_back(scal, dq, dk, dv, x, upper, slots, vec, weights, win):
    n = len(weights)
    m = x.shape[0]
    blk = pl.BlockSpec((win, D), lambda i: (i, 0))
    return pl.pallas_call(
        functools.partial(first_body, n, D // 32),
        grid=(m // win,),
        in_specs=[SMEM] + [blk] * 5 + [whole(slots.shape), whole(vec.shape)] + [ANY] * n,
        out_specs=[blk, whole(slots.shape), whole((8, D))],
        out_shape=[sds((m, D), F32), sds(slots.shape, F32), sds((8, D), F32)],
        scratch_shapes=[pltpu.VMEM((D, D), BF16)] * 3 + [pltpu.SemaphoreType.DMA((3,))],
        compiler_params=PARAMS,
    )(scal, dq, dk, dv, x, upper, slots, vec, *weights)


def down_body(n, rows, filled, scal, hidden, attended, vec, *refs):
    weights, refs = refs[:n], refs[n + filled :]
    out, wd, sems = refs
    i = pl.program_id(0)

    @pl.when(i == 0)
    def _():
        fetch(scal, weights, wd, sems, 0, rows)
        arrive(wd, sems)

    out[...] = attended[...] + mm(hidden[...], wd[...]) + vec[DADD : DADD + 1, :]


def down_out(scal, hidden, attended, vec, weights, win, start, count, rows=0, so_far=()):
    n = len(weights)
    m, ff = hidden.shape
    blk = pl.BlockSpec((win, D), lambda i: (i + start, 0))
    return pl.pallas_call(
        functools.partial(down_body, n, rows, len(so_far)),
        grid=(count,),
        in_specs=[SMEM, pl.BlockSpec((win, ff), lambda i: (i + start, 0)), blk, whole(vec.shape)]
        + [ANY] * (n + len(so_far)),
        out_specs=blk,
        out_shape=sds((m, D), F32),
        scratch_shapes=[pltpu.VMEM((ff, D), BF16), pltpu.SemaphoreType.DMA],
        input_output_aliases={4 + n: 0} if so_far else {},
        compiler_params=PARAMS,
    )(scal, hidden, attended, vec, *weights, *so_far)


def scatter_tile(scal, stage, keep, send, sem, blocks, rows, row, columns=False, across=None):
    f0, p0 = scal[0], scal[1]
    y, z, c, x = f0 & 1, f0 >> 1, p0 & 1, p0 >> 1
    for at, f in enumerate(blocks):
        dy, k = (f & 1) ^ y, (f >> 1) ^ z
        for px in range(2):
            dx = px ^ x
            for other, out in enumerate((keep, send)):
                core = c ^ other
                one = jnp.where(core == 0, dx, dy)
                two = jnp.where(core == 0, dy, dx)
                dst = out.at[one, two, k]
                piece = px * 2 + core
                if columns:
                    half = D // 2
                    for part in range(2):
                        pltpu.make_async_copy(
                            stage.at[pl.ds(pl.multiple_of((piece * 2 + part) * rows, 8), rows), :],
                            dst.at[pl.ds(row, rows), pl.ds(part * half, half)],
                            sem,
                        ).start()
                else:
                    src = pl.multiple_of((at * 4 + piece) * rows, 8)
                    cols = slice(None) if across is None else pl.ds(across * (D // 2), D // 2)
                    pltpu.make_async_copy(
                        stage.at[pl.ds(src, rows), :], dst.at[pl.ds(row, rows), cols], sem
                    ).start()


def wide_body(columns, scal, a, b, *refs):
    i = pl.program_id(0)
    last = pl.num_programs(0) - 1
    slot = i & 1
    rows, half = D // 8, D // 2
    if columns:
        mixture, low, keep, send, stage, sems = refs
    else:
        keep, send, stage, sems = refs

    @pl.when(i >= 2)
    def _():
        arrive(stage.at[slot], sems.at[slot])

    if columns:

        @pl.when(i < 8)
        def _():
            stage[slot] = mm(a[...], b[...], 0, 0).astype(BF16)
            scatter_tile(scal, stage.at[slot], keep, send, sems.at[slot], [i], rows, 0, True)

        for part in range(2):

            @pl.when(i == 8 + part)
            def _():
                left = mixture[:, part * half : (part + 1) * half]
                blocks = [part * 4 + n for n in range(4)]
                tile = mm(left, low[...], 0, 0).astype(BF16)
                for n in range(2):
                    stage[slot, n * half : (n + 1) * half, :] = tile[:, n * half : (n + 1) * half]
                for n in range(2):
                    scatter_tile(
                        scal, stage.at[slot, pl.ds(n * half, half)], keep, send, sems.at[slot],
                        blocks, rows // 4, rows, across=n,
                    )

    else:
        stage[slot] = mm(a[...], b[...], 0, 0).astype(BF16)
        scatter_tile(scal, stage.at[slot], keep, send, sems.at[slot], [i], rows, 0)

    @pl.when(i == last)
    def _():
        arrive(stage.at[1 - slot], sems.at[1 - slot])
        arrive(stage.at[slot], sems.at[slot])


def wide_grad(scal, a, b, columns, square=()):
    m = a.shape[0]
    half = D // 2
    full = pl.BlockSpec((m, D), lambda i: (0, 0))
    part = pl.BlockSpec((m, half), lambda i: (0, jnp.minimum(i, 7)))
    shape = sds((2, 2, 4, D // 8 + (D // 32 if columns else 0), D), BF16)
    return pl.pallas_call(
        functools.partial(wide_body, columns),
        grid=(10 if columns else 8,),
        in_specs=[SMEM] + ([full, part, full, full] if columns else [part, full]),
        out_specs=[ANY, ANY],
        out_shape=[shape, shape],
        scratch_shapes=[
            pltpu.VMEM((2, D, half) if columns else (2, half, D), BF16),
            pltpu.SemaphoreType.DMA((2,)),
        ],
        compiler_params=PARAMS,
    )(scal, a, b, *square)


def square_body(count, scal, left, *refs):
    rights, (keep, send, stage, sems) = refs[:count], refs[count:]
    rows = D // 32
    half = D // 2
    for j in range(2 * count):
        m, part = j // 2, j % 2
        slot = j % 2
        if j >= 2:
            arrive(stage.at[slot], sems.at[slot])
        right = rights[m]
        stage[slot] = mm(left[:, part * half : (part + 1) * half], right[...], 0, 0).astype(BF16)
        blocks = [part * 4 + n for n in range(4)]
        scatter_tile(scal, stage.at[slot], keep, send, sems.at[slot], blocks, rows, m * rows)
    for slot in range(2):
        arrive(stage.at[slot], sems.at[slot])


def square_grads(scal, left, *rights):
    shape = sds((2, 2, 4, len(rights) * D // 32, D), BF16)
    return pl.pallas_call(
        functools.partial(square_body, len(rights)),
        in_specs=[SMEM] + [pl.BlockSpec(memory_space=pltpu.VMEM)] * (1 + len(rights)),
        out_specs=[ANY, ANY],
        out_shape=[shape, shape],
        scratch_shapes=[pltpu.VMEM((2, D // 2, D), BF16), pltpu.SemaphoreType.DMA((2,))],
        compiler_params=PARAMS,
    )(scal, left, *rights)


BOTH = ("fsdp", "dp")


def flip(v, f_of=0, p_of=0):
    pairs = [
        (f * 4 + p, (f ^ f_of) * 4 + (p ^ p_of)) for f in range(8) for p in range(4)
    ]
    return lax.ppermute(v, BOTH, pairs)


def flip_by_core(v, first, second):
    pairs = []
    for f in range(8):
        for p in range(4):
            df, dp = second if p & 1 else first
            pairs.append((f * 4 + p, (f ^ df) * 4 + (p ^ dp)))
    return lax.ppermute(v, BOTH, pairs)


Y_OF, X_OF = (1, 0), (0, 2)


def up32(*vs):
    out = vs[0].astype(F32)
    for v in vs[1:]:
        out = out + v.astype(F32)
    return out


def together(*groups):
    flat, tree = jax.tree.flatten(groups)
    return jax.tree.unflatten(tree, lax.optimization_barrier(tuple(flat)))


def flips_z(v):
    return [flip(v[k], 2 * k) for k in (1, 2, 3)]


class Gather:
    def along_z(self, piece):
        self.now = [piece] + flips_z([piece] * 4)

    def along_xy(self):
        self.held = jnp.stack(self.now)
        self.now = [flip_by_core(self.held, Y_OF, X_OF), flip_by_core(self.held, X_OF, Y_OF)]

    def along_rest(self):
        one, two = self.now
        self.mine = [self.held, one, two]
        self.now = [flip_by_core(one, X_OF, Y_OF)] + [flip(v, 0, 1) for v in self.mine]

    def along_core(self):
        three, *others = self.now
        self.all = self.mine + [three] + others
        self.now = flip(three, 0, 1)

    def done(self):
        return self.all + [self.now]


class Sum:
    def along_core(self, keep, send):
        self.keep = keep
        self.now = flip(send, 0, 1)

    def along_first(self):
        self.r = self.now
        part = up32(self.keep[1], self.r[1]).astype(BF16)
        self.now = flip_by_core(part, X_OF, Y_OF)

    def along_second(self):
        self.r1 = self.now
        part = up32(self.keep[0, 1], self.r[0, 1], self.r1[1]).astype(BF16)
        self.now = flip_by_core(part, Y_OF, X_OF)

    def along_z(self):
        self.r2 = self.now
        parts = [
            up32(self.keep[0, 0, k], self.r[0, 0, k], self.r1[0, k], self.r2[k]) for k in range(4)
        ]
        self.own = parts[0]
        self.now = flips_z([t.astype(BF16) for t in parts])

    def back(self):
        self.own = up32(self.own, *self.now).astype(BF16)
        self.now = [flip(self.own, 0, j) for j in (1, 2, 3)]

    def done(self):
        return order_dp((self.own, *self.now))


def order_dp(parts):
    p = lax.axis_index("dp")
    low, high = (p & 1) == 1, (p >> 1) == 1
    a, b, c, d = parts
    a, b, c, d = (
        jnp.where(low, b, a),
        jnp.where(low, a, b),
        jnp.where(low, d, c),
        jnp.where(low, c, d),
    )
    return (
        jnp.where(high, c, a),
        jnp.where(high, d, b),
        jnp.where(high, a, c),
        jnp.where(high, b, d),
    )


def spread_dp(done):
    over = flip(done, 0, 2)
    return order_dp((done, flip(done, 0, 1), over, flip(over, 0, 1)))


def on_device(
    sizes,
    inputs,
    cotangent,
    timesteps,
    layouts,
    step_table,
    first_gain,
    first_shift,
    query_matrix,
    query_bias,
    key_matrix,
    value_matrix,
    value_bias,
    out_matrix,
    out_bias,
    second_gain,
    second_shift,
    up_matrix,
    up_bias,
    down_matrix,
    down_bias,
):
    n_fsdp, n_dp = sizes
    fast = (n_fsdp, n_dp) == (8, 4)
    f, p = lax.axis_index("fsdp"), lax.axis_index("dp")
    scal = jnp.stack([f, p]).astype(jnp.int32)
    row_count = inputs.shape[0]
    win = row_count // layouts.shape[0]
    ff = up_matrix.shape[1] * n_fsdp
    steps = step_table.shape[0]
    pairs = timesteps.reshape(-1, 2)
    first_steps = pairs[:, 0]
    second_steps = jnp.where(layouts == 1, first_steps, pairs[:, 1])
    slot_steps = jnp.stack([first_steps, second_steps], axis=1).reshape(-1)
    vecs = (
        first_gain,
        first_shift,
        query_bias,
        value_bias,
        out_bias,
        second_gain,
        second_shift,
        down_bias,
        up_bias,
    )
    mats = (query_matrix, key_matrix, value_matrix, out_matrix, up_matrix, down_matrix)
    r = D // 32
    if fast:
        return exchange_and_run(
            scal, inputs, cotangent, layouts, step_table, slot_steps, vecs, mats, win, ff, f
        )
    cot_low = cotangent.astype(BF16)
    low = [m.astype(BF16) for m in vecs + mats]
    full = [lax.all_gather(m, "fsdp", axis=0, tiled=True) for m in low[:9]]
    vec = jnp.concatenate(full).reshape(12, D).astype(F32)
    w_qkv = [lax.all_gather(m, "fsdp", axis=0, tiled=True) for m in low[9:12]]
    w_out = [lax.all_gather(low[12], "fsdp", axis=0, tiled=True)]
    w_up = [lax.all_gather(low[13], "fsdp", axis=1, tiled=True)]
    w_down = [lax.all_gather(low[14], "fsdp", axis=0, tiled=True)]
    table = lax.all_gather(step_table.astype(BF16), "fsdp", axis=1, tiled=True)
    rel = jnp.take(table, slot_steps, axis=0).astype(F32)
    count = layouts.shape[0]

    normed, q, k, v, slots, vec = qkv(scal, inputs, rel, w_qkv, vec, win)
    mixture = attend(scal, layouts, q, k, v)
    attended, second = mix(scal, mixture, inputs, slots, vec, w_out, win)
    hidden, pre, up_add = mlp(scal * 0, second, cot_low, vec, w_up, w_down, ff)
    grad, low, sums2 = second_back(scal, pre, attended, cotangent, vec, w_up, win)
    dq, dk, dv = attend_back(scal, layouts, low, q, k, v, w_out, 0, count)
    input_grad, slot_sums, sums1 = first_back(
        scal, dq, dk, dv, inputs, grad, slots, vec, w_qkv, win
    )
    block_output = down_out(scal, hidden, attended, vec, w_down, win, 0, count)

    total_of = lambda v, dim: lax.psum(
        lax.psum_scatter(v, "fsdp", scatter_dimension=dim, tiled=True), "dp"
    )
    down_grad = total_of(mm(hidden, cot_low, 0, 0), 0)
    up_grad = total_of(mm(second, pre, 0, 0), 1)
    out_grad = total_of(mm(mixture, low, 0, 0), 0)
    query_grad = total_of(mm(normed, dq, 0, 0), 0)
    key_grad = total_of(mm(normed, dk, 0, 0), 0)
    value_grad = total_of(mm(normed, dv, 0, 0), 0)
    small = lax.psum(vector_sums(sums1, sums2, up_add), BOTH)
    table_grad = total_of(jnp.zeros((steps, D), F32).at[slot_steps].add(slot_sums), 1)
    return results(
        block_output, input_grad, table_grad, small, f, n_fsdp, ff,
        query_grad, key_grad, value_grad, out_grad, up_grad, down_grad,
    )


def vector_sums(sums1, sums2, up_add):
    return jnp.concatenate(
        [sums1[:4], sums2[2:3], sums2[:2], sums2[3:4], up_add.reshape(-1, D)], axis=0
    )


def results(
    block_output, input_grad, table_grad, small, f, n_fsdp, ff,
    query_grad, key_grad, value_grad, out_grad, up_grad, down_grad,
):
    width = D // n_fsdp
    mine = lax.dynamic_slice(small[:8], (0, f * width), (8, width))
    up_mine = lax.dynamic_slice(small[8:].reshape(-1), (f * (ff // n_fsdp),), (ff // n_fsdp,))
    return named(
        block_output, input_grad, table_grad, mine, up_mine,
        query_grad, key_grad, value_grad, out_grad, up_grad, down_grad,
    )


def named(
    block_output, input_grad, table_grad, mine, up_mine,
    query_grad, key_grad, value_grad, out_grad, up_grad, down_grad,
):
    return (
        block_output,
        input_grad,
        table_grad,
        mine[0],
        mine[1],
        query_grad,
        mine[2],
        key_grad,
        value_grad,
        mine[3],
        out_grad,
        mine[4],
        mine[5],
        mine[6],
        up_grad,
        up_mine,
        down_grad,
        mine[7],
    )


def exchange_and_run(
    scal, inputs, cotangent, layouts, step_table, slot_steps, vecs, mats, win, ff, f
):
    r = D // 32
    at_up = dict(row=r, rows=D // 8)
    at_down = dict(rows=D // 8)
    one, two, three = Gather(), Gather(), Gather()

    pieces = prep(scal, vecs, mats)
    y_steps = jnp.stack([slot_steps, flip(slot_steps, 1)])
    pieces, y_steps = together(pieces, y_steps)

    one.along_z(pieces[0])
    z_steps = flips_z([y_steps] * 4)
    cot_low = cotangent.astype(BF16)
    one.now, z_steps, cot_low, pieces = together(one.now, z_steps, cot_low, pieces)

    one.along_xy()
    all_steps = jnp.stack([y_steps] + z_steps)
    asked = jnp.take(step_table, all_steps, axis=0).astype(BF16)
    back = jnp.stack([asked[0]] + flips_z(asked))
    two.along_z(pieces[1])
    one.now, back = together(one.now, back)

    one.along_rest()
    given = jnp.stack([back[:, 0], flip(back[:, 1], 1)], axis=1)
    one.now, given, pieces = together(one.now, given, pieces)

    one.along_core()
    rel = given.reshape(8, given.shape[2], given.shape[3]).astype(F32)
    one.now, rel, pieces, two.now = together(one.now, rel, pieces, two.now)

    two.along_xy()
    three.along_z(pieces[2])
    w_qkv = one.done()
    normed, q, k, v, slots, vec = qkv(scal, inputs, rel, w_qkv, None, win)
    q, k, v, two.now, three.now = together(q, k, v, two.now, three.now)

    two.along_rest()
    three.along_xy()
    mixture = attend(scal, layouts, q, k, v)
    mixture, two.now, three.now = together(mixture, two.now, three.now)

    two.along_core()
    three.along_rest()
    mixture, two.now = together(mixture, two.now)

    w_two = two.done()
    attended, second = mix(scal, mixture, inputs, slots, vec, w_two, win)
    attended, second, three.now = together(attended, second, three.now)

    three.along_core()
    second, three.now = together(second, three.now)

    w_down = three.done()
    hidden, pre, up_add = mlp(scal, second, cot_low, vec, w_two, w_down, ff, r, D // 8)
    down = Sum()
    kept = wide_grad(scal, hidden, cot_low, False)
    kept, pre = together(kept, pre)

    down.along_core(*kept)
    grad, low, sums2 = second_back(scal, pre, attended, cotangent, vec, w_two, win, **at_up)
    grad, low, pre, down.now = together(grad, low, pre, down.now)

    down.along_first()
    up = Sum()
    kept = wide_grad(scal, second, pre, True, (mixture, low))
    kept, low, down.now = together(kept, low, down.now)

    down.along_second()
    up.along_core(*kept)
    halves = layouts.shape[0] // 2
    back1 = attend_back(scal, layouts, low, q, k, v, w_two, 0, halves)
    back1, down.now, up.now = together(back1, down.now, up.now)

    down.along_z()
    up.along_first()
    dq, dk, dv = attend_back(scal, layouts, low, q, k, v, w_two, halves, halves, back1)
    dq, dk, dv, down.now, up.now = together(dq, dk, dv, down.now, up.now)

    down.back()
    up.along_second()
    square = Sum()
    kept = square_grads(scal, normed, dq, dk, dv)
    kept, dq, dk, dv, down.now, up.now, hidden = together(
        kept, dq, dk, dv, down.now, up.now, hidden
    )

    square.along_core(*kept)
    up.along_z()
    part = down_out(scal, hidden, attended, vec, w_down, win, 0, halves, **at_down)
    square.now, part, dq = together(square.now, part, dq)

    square.along_first()
    input_grad, slot_sums, sums1 = first_back(
        scal, dq, dk, dv, inputs, grad, slots, vec, w_qkv, win
    )
    small = vector_sums(sums1, sums2, up_add)
    small, slot_sums, square.now, up.now, part = together(
        small, slot_sums, square.now, up.now, part
    )

    width = D // 8
    count = slot_sums.shape[0]
    own = jnp.concatenate([slot_sums, small[:8]]).reshape(-1, 8, width).swapaxes(0, 1)
    own = jnp.concatenate([own, small[8:].reshape(8, -1, width)], axis=1)
    own = jnp.stack([lax.dynamic_index_in_dim(own, f ^ j, 0, False) for j in range(8)])
    tag = jnp.zeros((8, 1, width), F32).at[:, 0, :count].set(slot_steps.astype(F32))
    own = jnp.concatenate([own, tag], axis=1)
    own = own.reshape(4, 2, *own.shape[1:])
    up.back()
    square.along_second()
    own_y = flip(own[:, 1], 1)
    block_output = down_out(
        scal, hidden, attended, vec, w_down, win, halves, halves, so_far=(part,), **at_down
    )
    block_output, own_y, up.now, square.now = together(block_output, own_y, up.now, square.now)

    square.along_z()
    own = jnp.stack([own[:, 0], own_y], axis=1)
    own_z = flips_z(own)
    half = D // 2
    down_grad = jnp.concatenate(down.done(), axis=0).astype(F32)
    square.now, own_z, down_grad = together(square.now, own_z, down_grad)

    square.back()
    own = jnp.stack([own[0]] + own_z).reshape(8, *own.shape[2:])
    parts = [own] + [flip(own, 0, j) for j in (1, 2, 3)]
    got = up.done()
    u = D // 8
    up_grad = jnp.concatenate(
        [t for m in got for t in (m[:u, :half], m[:u, half:])], axis=0
    ).astype(F32)
    out_grad = jnp.concatenate([m[u:] for m in got], axis=0).astype(F32)
    square.now, parts, up_grad, out_grad = together(square.now, parts, up_grad, out_grad)

    query_grad, key_grad, value_grad = (
        jnp.concatenate([m[j * r : (j + 1) * r] for m in square.done()], axis=0).astype(F32)
        for j in range(3)
    )
    every = jnp.stack(order_dp(parts)).reshape(-1, *own.shape[1:])
    steps = every[:, -1, :count].astype(jnp.int32).reshape(-1)
    table_grad = (
        jnp.zeros((step_table.shape[0], width), F32)
        .at[steps]
        .add(every[:, :count].reshape(-1, width))
    )
    mine = jnp.sum(every[:, count:-1], axis=0)
    return named(
        block_output, input_grad, table_grad, mine, mine[8:].reshape(-1),
        query_grad, key_grad, value_grad, out_grad, up_grad, down_grad,
    )


def solution(mesh):
    rows = P(("fsdp", "dp"), None)
    slots = P(("fsdp", "dp"))
    vector = P("fsdp")
    matrix = P("fsdp", None)
    wide = P(None, "fsdp")
    placed = (
        rows, rows, slots, slots, wide, vector, vector, matrix, vector, matrix,
        matrix, vector, matrix, vector, vector, vector, wide, vector, matrix, vector,
    )
    returned = (
        rows, rows, wide, vector, vector, matrix, vector, matrix, matrix, vector,
        matrix, vector, vector, vector, wide, vector, matrix, vector,
    )
    return jax.shard_map(
        functools.partial(on_device, (mesh.shape["fsdp"], mesh.shape["dp"])),
        mesh=mesh,
        in_specs=placed,
        out_specs=returned,
        check_vma=False,
    )
```

```python
import functools
import math

import jax
import jax.numpy as jnp
from jax import lax
from jax.experimental import pallas as pl
from jax.experimental.pallas import tpu as pltpu
from jax.sharding import PartitionSpec as P

HEADS = 12
HEAD = 64
D = HEADS * HEAD
F32 = jnp.float32
BF16 = jnp.bfloat16
ANY = pl.BlockSpec(memory_space=pl.ANY)
SMEM = pl.BlockSpec(memory_space=pltpu.SMEM)
PARAMS = pltpu.CompilerParams(vmem_limit_bytes=60 * 1024 * 1024)

TAIL_P = 0.3
TAIL = (
    0.11962929811062077,
    0.12075396817215742,
    0.0999134093206875,
    0.12856192203768363,
    -0.053684240767073,
    0.20635418971029199,
    -0.15720349531083133,
    0.0356748757872949,
)

GAIN1, SHIFT1, QADD, VADD, OADD, GAIN2, SHIFT2, DADD, UADD = range(9)


def whole(shape):
    return pl.BlockSpec(shape, lambda *_: (0,) * len(shape))


def sds(shape, dtype):
    return jax.ShapeDtypeStruct(shape, dtype)


def mm(a, b, ca=1, cb=0):
    return lax.dot_general(a, b, (((ca,), (cb,)), ((), ())), preferred_element_type=F32)


def place(scal, buf, other, k):
    f, p = scal[0], scal[1]
    y, z, c, x = f & 1, f >> 1, p & 1, p >> 1
    core = c ^ other
    by_y = 1 - core if buf == 1 else core if buf == 2 else buf // 3
    by_x = core if buf == 1 else 1 - core if buf == 2 else buf // 3
    return ((z ^ k) << 1) | (y ^ by_y), ((x ^ by_x) << 1) | core


def fetch(scal, refs, dst, sem, row=0, rows=0, columns=False, parts=range(4)):
    if len(refs) == 1 and len(parts) == 4:
        pltpu.make_async_copy(refs[0], dst, sem).start()
        return
    if len(refs) == 1:
        size = dst.shape[columns] // 4
        at = pl.ds(pl.multiple_of((parts[0] ^ (scal[0] >> 1)) * size, size), size)
        at = (slice(None), at) if columns else (at, slice(None))
        pltpu.make_async_copy(refs[0].at[at], dst.at[at], sem).start()
        return
    for other in range(2):
        for buf in range(4):
            for k in parts:
                f, p = place(scal, buf, other, k)
                src = refs[other * 4 + buf].at[k]
                if columns:
                    half = D // 2
                    for part in range(2):
                        r = pl.multiple_of(p * 2 * rows + part * rows, 8)
                        pltpu.make_async_copy(
                            src.at[pl.ds(row, rows), pl.ds(part * half, half)],
                            dst.at[pl.ds(r, rows), pl.ds(pl.multiple_of(f * half, 128), half)],
                            sem,
                        ).start()
                else:
                    r = pl.multiple_of((f * 4 + p) * rows, 8)
                    pltpu.make_async_copy(
                        src.at[pl.ds(row, rows), :], dst.at[pl.ds(r, rows), :], sem
                    ).start()


def arrive(dst, sem):
    pltpu.make_async_copy(dst, dst, sem).wait()


def prep_body(scal, *refs):
    vecs, (q, k, v, o, up, down), (one, two, three) = refs[:9], refs[9:15], refs[15:]
    up_add = vecs[8][...]
    left = jnp.concatenate([r[...] for r in vecs[:8]], axis=0)
    left = jnp.concatenate([left, jnp.zeros((8, D // 2 - left.shape[1]), F32)], axis=1)
    right = jnp.concatenate([up_add, jnp.zeros((7, D // 2), F32)], axis=0)
    one[0:8, :] = jnp.concatenate([left, right], axis=1).astype(BF16)
    r = q.shape[0]
    for i, m in enumerate((q, k, v)):
        one[8 + i * r : 8 + (i + 1) * r, :] = m[...].astype(BF16)
    two[0:r, :] = o[...].astype(BF16)
    u = up.shape[0] // 2
    two[r : r + u, 0 : D // 2] = up[0:u, :].astype(BF16)
    two[r : r + u, D // 2 : D] = up[u : 2 * u, :].astype(BF16)
    three[...] = down[...].astype(BF16)


def prep(scal, vecs, mats):
    q, up, down = mats[0], mats[4], mats[5]
    r, u, d = q.shape[0] // 4, up.shape[0] // 4, down.shape[0] // 4
    half = up.shape[1]
    mine = lambda rows, cols: pl.BlockSpec((rows, cols), lambda i, s: (s[1], 0))
    vecs = [v.reshape(1, -1) for v in vecs]
    return pl.pallas_call(
        prep_body,
        grid_spec=pltpu.PrefetchScalarGridSpec(
            num_scalar_prefetch=1,
            grid=(1,),
            in_specs=[pl.BlockSpec(v.shape, lambda i, s: (0, 0)) for v in vecs]
            + [mine(r, D)] * 4
            + [mine(u, half), mine(d, D)],
            out_specs=[
                pl.BlockSpec(s, lambda i, s_: (0, 0))
                for s in ((8 + 3 * r, D), (r + u // 2, D), (d, D))
            ],
        ),
        out_shape=(sds((8 + 3 * r, D), BF16), sds((r + u // 2, D), BF16), sds((d, D), BF16)),
        compiler_params=PARAMS,
    )(scal, *vecs, *mats)


def normal_rows(v):
    c = v - jnp.mean(v, axis=-1, keepdims=True)
    r = lax.rsqrt(jnp.mean(c * c, axis=-1, keepdims=True) + 1e-05)
    return c * r, r


def stamp(x, slots, i):
    half = x.shape[0] // 2
    return jnp.concatenate(
        [x[:half] + slots[pl.ds(2 * i, 1), :], x[half:] + slots[pl.ds(2 * i + 1, 1), :]], axis=0
    )


def qkv_body(n, shape, scal, x, rel, *refs):
    weights, refs = refs[:n], refs[n:]
    if n != 8:
        vec_in, refs = refs[0], refs[1:]
    normed, q, k, v, slots_out, vec_out, wq, wk, wv, small, sems = refs
    i = pl.program_id(0)

    @pl.when(i == 0)
    def _():
        if n == 8:
            rows = shape
            for j, w in enumerate((wq, wk, wv)):
                fetch(scal, weights, w, sems.at[j], 8 + j * rows, rows)
            for buf in range(4):
                for z in range(4):
                    f, _ = place(scal, buf, 0, z)
                    if buf in (0, 1, 2):
                        pass
                    pltpu.make_async_copy(
                        weights[buf].at[z, pl.ds(0, 8), :], small.at[buf * 4 + z], sems.at[3]
                    ).start()
            f0 = scal[0]
            slots_out[...] = jnp.concatenate([rel[f0 ^ f] for f in range(8)], axis=1)
            arrive(small, sems.at[3])
            core = scal[1] & 1
            flip = jnp.where(core == 0, 1, 2)
            parts = []
            for f in range(8):
                zz = (f >> 1) ^ (f0 >> 1)
                yy = (f & 1) ^ (f0 & 1)
                parts.append(small[yy * flip * 4 + zz].astype(F32))
            vec_out[0:8, :] = jnp.concatenate([t[:, : D // 8] for t in parts], axis=1)
            for j in range(4):
                vec_out[8 + j : 9 + j, :] = jnp.concatenate(
                    [parts[2 * j][0:1, D // 2 :], parts[2 * j + 1][0:1, D // 2 :]], axis=1
                )
        else:
            for j, w in enumerate((wq, wk, wv)):
                fetch(scal, weights[j : j + 1], w, sems.at[j])
            slots_out[...] = rel[...]
            vec_out[...] = vec_in[...]
        for j, w in enumerate((wq, wk, wv)):
            arrive(w, sems.at[j])

    n1, _ = normal_rows(stamp(x[...], slots_out, i))
    low = (n1 * vec_out[GAIN1 : GAIN1 + 1, :] + vec_out[SHIFT1 : SHIFT1 + 1, :]).astype(BF16)
    normed[...] = low
    q[...] = (mm(low, wq[...]) + vec_out[QADD : QADD + 1, :]).astype(BF16)
    k[...] = mm(low, wk[...]).astype(BF16)
    v[...] = (mm(low, wv[...]) + vec_out[VADD : VADD + 1, :]).astype(BF16)


def qkv(scal, x, rel, weights, vec, win):
    rows = x.shape[0]
    slots = 2 * (rows // win)
    n = len(weights)
    blk = pl.BlockSpec((win, D), lambda i: (i, 0))
    ins = [SMEM, blk, whole(rel.shape)] + [ANY] * n
    args = [scal, x, rel, *weights]
    if n != 8:
        ins.append(whole(vec.shape))
        args.append(vec)
    return pl.pallas_call(
        functools.partial(qkv_body, n, D // 32),
        grid=(rows // win,),
        in_specs=ins,
        out_specs=[blk] * 4 + [whole((slots, D)), whole((12, D))],
        out_shape=[sds((rows, D), BF16)] * 4 + [sds((slots, D), F32), sds((12, D), F32)],
        scratch_shapes=[pltpu.VMEM((D, D), BF16)] * 3
        + [pltpu.VMEM((16, 8, D), BF16), pltpu.SemaphoreType.DMA((4,))],
        compiler_params=PARAMS,
    )(*args)


def lane_mask(half):
    lane = lax.broadcasted_iota(jnp.int32, (1, 2 * HEAD), 1)
    return (lane >= HEAD) if half else (lane < HEAD)


def permitted(win, layout):
    a = lax.broadcasted_iota(jnp.int32, (win, win), 0) // (win // 2)
    b = lax.broadcasted_iota(jnp.int32, (win, win), 1) // (win // 2)
    return (a == b) | (layout == 1)


def attend_body(scal, lay, q, k, v, mixture):
    allowed = permitted(q.shape[0], lay[pl.program_id(0)])

    def pair(j, _):
        at = pl.ds(pl.multiple_of(j * 2 * HEAD, 2 * HEAD), 2 * HEAD)
        qp, kp, vp = q[:, at] * 0.125, k[:, at], v[:, at]
        got = []
        for half in range(2):
            s = mm(jnp.where(lane_mask(half), qp, 0), kp, 1, 1)
            s = jnp.where(allowed, s, -1e30)
            e = jnp.exp(s - jnp.max(s, axis=-1, keepdims=True))
            a = e * (1.0 / jnp.sum(e, axis=-1, keepdims=True))
            got.append(mm(a.astype(BF16), vp))
        mixture[:, at] = jnp.where(lane_mask(0), got[0], got[1]).astype(BF16)
        return 0

    lax.fori_loop(0, HEADS // 2, pair, 0, unroll=True)


def attend(scal, lay, q, k, v):
    rows = q.shape[0]
    win = rows // lay.shape[0]
    blk = pl.BlockSpec((win, D), lambda i: (i, 0))
    return pl.pallas_call(
        attend_body,
        grid=(rows // win,),
        in_specs=[SMEM, SMEM] + [blk] * 3,
        out_specs=blk,
        out_shape=sds((rows, D), BF16),
        compiler_params=PARAMS,
    )(scal, lay, q, k, v)


def mix_body(n, rows, scal, mixture, x, slots, vec, *refs):
    weights, refs = refs[:n], refs[n:]
    attended, second, wo, sems = refs
    i = pl.program_id(0)

    @pl.when(i == 0)
    def _():
        fetch(scal, weights, wo, sems, 0, rows)
        arrive(wo, sems)

    att = stamp(x[...], slots, i) + mm(mixture[...], wo[...]) + vec[OADD : OADD + 1, :]
    attended[...] = att
    n2, _ = normal_rows(att)
    second[...] = (n2 * vec[GAIN2 : GAIN2 + 1, :] + vec[SHIFT2 : SHIFT2 + 1, :]).astype(BF16)


def mix(scal, mixture, x, slots, vec, weights, win):
    rows = x.shape[0]
    n = len(weights)
    blk = pl.BlockSpec((win, D), lambda i: (i, 0))
    return pl.pallas_call(
        functools.partial(mix_body, n, D // 32),
        grid=(rows // win,),
        in_specs=[SMEM, blk, blk, whole(slots.shape), whole(vec.shape)] + [ANY] * n,
        out_specs=[blk] * 2,
        out_shape=[sds((rows, D), F32), sds((rows, D), BF16)],
        scratch_shapes=[pltpu.VMEM((D, D), BF16), pltpu.SemaphoreType.DMA],
        compiler_params=PARAMS,
    )(scal, mixture, x, slots, vec, *weights)


TILE = 256


def mlp_body(n, row_up, rows, scal, second, cot, vec, *refs):
    w_up, w_down, refs = refs[:n], refs[n : 2 * n], refs[2 * n :]
    hidden, low, add, wu, wd, pre_a, pre_b, grad_a, grad_b, sems = refs
    i = pl.program_id(0)
    last = pl.num_programs(0) - 1
    across = D // TILE
    units = (second.shape[0] // TILE) * across
    own = scal[0] >> 1

    def wait(g):
        arrive(wu.at[:, pl.ds(0, D)], sems.at[0, g])
        arrive(wd.at[pl.ds(0, D), :], sems.at[1, g])

    def tile(u):
        r = pl.multiple_of((u // across) * TILE, TILE)
        return pl.ds(r, TILE), (u % across) * TILE

    def multiply(step, u, pre, grad):
        at, col = tile(u)
        cols = pl.ds(pl.multiple_of((step ^ own) * D + col, TILE), TILE)
        pre[...] = mm(second[at, :], wu[:, cols])
        grad[...] = mm(cot[at, :], wd[cols, :], 1, 1)

    def finish(n, pre, grad):
        at, col = tile(n)
        cols = pl.ds(pl.multiple_of(col, TILE), TILE)
        bias = vec[pl.ds(8 + (i ^ own), 1), cols]
        u = pre[...] + bias
        a = jnp.abs(u)
        t = 1.0 / (1.0 + TAIL_P * a)
        e = jnp.exp2((-0.5 * math.log2(math.e)) * (u * u))
        acc = jnp.full_like(t, TAIL[-1])
        for c in TAIL[-2::-1]:
            acc = acc * t + c
        tail = e * (t * acc)
        cdf = jnp.where(u >= 0, 1.0 - tail, tail)
        hidden[at, cols] = (u * cdf).astype(BF16)
        slope = cdf + u * (e * (1.0 / math.sqrt(2.0 * math.pi)))
        low[at, cols] = (grad[...] * slope).astype(BF16)
        new = mm(jnp.ones((8, TILE), BF16), low[at, cols])[:1]
        add[:, cols] = jnp.where(n < across, 0.0, add[:, cols]) + new

    @pl.when(i == 0)
    def _():
        for g in range(4):
            fetch(scal, w_up, wu, sems.at[0, g], row_up, rows, True, [g])
            fetch(scal, w_down, wd, sems.at[1, g], 0, rows, False, [g])
        wait(0)
        multiply(0, 0, pre_a, grad_a)

    @pl.when(i != last)
    def _():
        wait(i + 1)

    def two(p, _):
        n = 2 * p
        multiply(i, n + 1, pre_b, grad_b)
        finish(n, pre_a, grad_a)
        over = n + 2 == units
        multiply(jnp.where(over, jnp.minimum(i + 1, last), i), jnp.where(over, 0, n + 2), pre_a, grad_a)
        finish(n + 1, pre_b, grad_b)
        return 0

    lax.fori_loop(0, units // 2, two, 0)


def mlp(scal, second, cot, vec, w_up, w_down, ff, row_up=0, rows=0):
    n = len(w_up)
    m = second.shape[0]
    blk = lambda rows: pl.BlockSpec((rows, D), lambda i, s: (0, i ^ (s[0] >> 1)))
    tile = pltpu.VMEM((TILE, TILE), F32)
    return pl.pallas_call(
        functools.partial(mlp_body, n, row_up, rows),
        grid_spec=pltpu.PrefetchScalarGridSpec(
            num_scalar_prefetch=1,
            grid=(ff // D,),
            in_specs=[whole(second.shape), whole(cot.shape), whole(vec.shape)] + [ANY] * (2 * n),
            out_specs=[blk(m), blk(m), blk(1)],
            scratch_shapes=[pltpu.VMEM((D, ff), BF16), pltpu.VMEM((ff, D), BF16)]
            + [tile] * 4
            + [pltpu.SemaphoreType.DMA((2, 4))],
        ),
        out_shape=[sds((m, ff), BF16), sds((m, ff), BF16), sds((1, ff), F32)],
        compiler_params=PARAMS,
    )(scal, second, cot, vec, *w_up, *w_down)


def norm_back(e, n, r, gain):
    f = e * gain
    return r * (f - jnp.mean(f, -1, keepdims=True) - n * jnp.mean(f * n, -1, keepdims=True))


def total(v):
    return jnp.sum(v, axis=0, keepdims=True)


def accumulate(ref, i, rows):
    new = jnp.concatenate(rows + [jnp.zeros((8 - len(rows), D), F32)], axis=0)

    @pl.when(i == 0)
    def _():
        ref[...] = new

    @pl.when(i != 0)
    def _():
        ref[...] += new


def second_body(n, row, rows, scal, pre, attended, cot, vec, *refs):
    weights, refs = refs[:n], refs[n:]
    grad, low, sums, wu, sems = refs
    i = pl.program_id(0)

    @pl.when(i == 0)
    def _():
        fetch(scal, weights, wu, sems, row, rows, True)
        arrive(wu, sems)

    e = mm(pre[...], wu[...], 1, 1)
    n2, r = normal_rows(attended[...])
    c = cot[...]
    g = c + norm_back(e, n2, r, vec[GAIN2 : GAIN2 + 1, :])
    grad[...] = g
    low[...] = g.astype(BF16)
    accumulate(sums, i, [total(e * n2), total(e), total(g), total(c)])


def second_back(scal, pre, attended, cot, vec, weights, win, row=0, rows=0):
    n = len(weights)
    m, ff = pre.shape
    blk = pl.BlockSpec((win, D), lambda i: (i, 0))
    return pl.pallas_call(
        functools.partial(second_body, n, row, rows),
        grid=(m // win,),
        in_specs=[SMEM, pl.BlockSpec((win, ff), lambda i: (i, 0)), blk, blk, whole(vec.shape)]
        + [ANY] * n,
        out_specs=[blk, blk, whole((8, D))],
        out_shape=[sds((m, D), F32), sds((m, D), BF16), sds((8, D), F32)],
        scratch_shapes=[pltpu.VMEM((D, ff), BF16), pltpu.SemaphoreType.DMA],
        compiler_params=PARAMS,
    )(scal, pre, attended, cot, vec, *weights)


def attend_back_body(n, rows, start, filled, scal, lay, low, q, k, v, *refs):
    weights, refs = refs[:n], refs[n + filled :]
    dq, dk, dv, wo, mix, sems = refs
    i = pl.program_id(0)

    @pl.when(i == 0)
    def _():
        fetch(scal, weights, wo, sems, 0, rows)
        arrive(wo, sems)

    mix[...] = mm(low[...], wo[...], 1, 1).astype(BF16)
    win = q.shape[0]
    allowed = permitted(win, lay[i + start])

    def pair(j, _):
        at = pl.ds(pl.multiple_of(j * 2 * HEAD, 2 * HEAD), 2 * HEAD)
        qp, kp, vp, gp = q[:, at] * 0.125, k[:, at], v[:, at], mix[:, at]
        ks = kp * 0.125
        got = []
        for half in range(2):
            mask = lane_mask(half)
            s = mm(jnp.where(mask, kp, 0), qp, 1, 1)
            s = jnp.where(allowed, s, -1e30)
            e = jnp.exp(s - jnp.max(s, axis=0, keepdims=True))
            a = e * (1.0 / jnp.sum(e, axis=0, keepdims=True))
            t = a * mm(jnp.where(mask, vp, 0), gp, 1, 1)
            ds = (t - a * jnp.sum(t, axis=0, keepdims=True)).astype(BF16)
            got.append((mm(ds, ks, 0, 0), mm(ds, qp), mm(a.astype(BF16), gp)))
        for ref, first, last in zip((dq, dk, dv), got[0], got[1]):
            ref[:, at] = jnp.where(lane_mask(0), first, last).astype(BF16)
        return 0

    lax.fori_loop(0, HEADS // 2, pair, 0, unroll=3)


def attend_back(scal, lay, low, q, k, v, weights, start, count, so_far=()):
    n = len(weights)
    m = q.shape[0]
    win = m // lay.shape[0]
    blk = pl.BlockSpec((win, D), lambda i: (i + start, 0))
    return pl.pallas_call(
        functools.partial(attend_back_body, n, D // 32, start, len(so_far)),
        grid=(count,),
        in_specs=[SMEM, SMEM] + [blk] * 4 + [ANY] * (n + len(so_far)),
        out_specs=[blk] * 3,
        out_shape=[sds((m, D), BF16)] * 3,
        scratch_shapes=[
            pltpu.VMEM((D, D), BF16),
            pltpu.VMEM((win, D), BF16),
            pltpu.SemaphoreType.DMA,
        ],
        input_output_aliases={6 + n + j: j for j in range(len(so_far))},
        compiler_params=PARAMS,
    )(scal, lay, low, q, k, v, *weights, *so_far)


def first_body(n, rows, scal, dq, dk, dv, x, upper, slots, vec, *refs):
    weights, refs = refs[:n], refs[n:]
    out, slot_sums, sums, wq, wk, wv, sems = refs
    i = pl.program_id(0)

    @pl.when(i == 0)
    def _():
        for j, w in enumerate((wq, wk, wv)):
            src = weights if n == 8 else weights[j : j + 1]
            fetch(scal, src, w, sems.at[j], 8 + j * rows, rows)
        for j, w in enumerate((wq, wk, wv)):
            arrive(w, sems.at[j])

    e = mm(dq[...], wq[...], 1, 1) + mm(dk[...], wk[...], 1, 1) + mm(dv[...], wv[...], 1, 1)
    n1, r = normal_rows(stamp(x[...], slots, i))
    g = upper[...] + norm_back(e, n1, r, vec[GAIN1 : GAIN1 + 1, :])
    out[...] = g
    half = g.shape[0] // 2
    slot_sums[pl.ds(2 * i, 1), :] = total(g[:half])
    slot_sums[pl.ds(2 * i + 1, 1), :] = total(g[half:])
    accumulate(
        sums,
        i,
        [total(e * n1), total(e), total(dq[...].astype(F32)), total(dv[...].astype(F32))],
    )


def first_back(scal, dq, dk, dv, x, upper, slots, vec, weights, win):
    n = len(weights)
    m = x.shape[0]
    blk = pl.BlockSpec((win, D), lambda i: (i, 0))
    return pl.pallas_call(
        functools.partial(first_body, n, D // 32),
        grid=(m // win,),
        in_specs=[SMEM] + [blk] * 5 + [whole(slots.shape), whole(vec.shape)] + [ANY] * n,
        out_specs=[blk, whole(slots.shape), whole((8, D))],
        out_shape=[sds((m, D), F32), sds(slots.shape, F32), sds((8, D), F32)],
        scratch_shapes=[pltpu.VMEM((D, D), BF16)] * 3 + [pltpu.SemaphoreType.DMA((3,))],
        compiler_params=PARAMS,
    )(scal, dq, dk, dv, x, upper, slots, vec, *weights)


def down_body(n, rows, filled, scal, hidden, attended, vec, *refs):
    weights, refs = refs[:n], refs[n + filled :]
    out, wd, sems = refs
    i = pl.program_id(0)

    @pl.when(i == 0)
    def _():
        fetch(scal, weights, wd, sems, 0, rows)
        arrive(wd, sems)

    out[...] = attended[...] + mm(hidden[...], wd[...]) + vec[DADD : DADD + 1, :]


def down_out(scal, hidden, attended, vec, weights, win, start, count, rows=0, so_far=()):
    n = len(weights)
    m, ff = hidden.shape
    blk = pl.BlockSpec((win, D), lambda i: (i + start, 0))
    return pl.pallas_call(
        functools.partial(down_body, n, rows, len(so_far)),
        grid=(count,),
        in_specs=[SMEM, pl.BlockSpec((win, ff), lambda i: (i + start, 0)), blk, whole(vec.shape)]
        + [ANY] * (n + len(so_far)),
        out_specs=blk,
        out_shape=sds((m, D), F32),
        scratch_shapes=[pltpu.VMEM((ff, D), BF16), pltpu.SemaphoreType.DMA],
        input_output_aliases={4 + n: 0} if so_far else {},
        compiler_params=PARAMS,
    )(scal, hidden, attended, vec, *weights, *so_far)


def scatter_tile(scal, stage, keep, send, sem, blocks, rows, row, columns=False, across=None):
    f0, p0 = scal[0], scal[1]
    y, z, c, x = f0 & 1, f0 >> 1, p0 & 1, p0 >> 1
    for at, f in enumerate(blocks):
        dy, k = (f & 1) ^ y, (f >> 1) ^ z
        for px in range(2):
            dx = px ^ x
            for other, out in enumerate((keep, send)):
                core = c ^ other
                one = jnp.where(core == 0, dx, dy)
                two = jnp.where(core == 0, dy, dx)
                dst = out.at[one, two, k]
                piece = px * 2 + core
                if columns:
                    half = D // 2
                    for part in range(2):
                        pltpu.make_async_copy(
                            stage.at[pl.ds(pl.multiple_of((piece * 2 + part) * rows, 8), rows), :],
                            dst.at[pl.ds(row, rows), pl.ds(part * half, half)],
                            sem,
                        ).start()
                else:
                    src = pl.multiple_of((at * 4 + piece) * rows, 8)
                    cols = slice(None) if across is None else pl.ds(across * (D // 2), D // 2)
                    pltpu.make_async_copy(
                        stage.at[pl.ds(src, rows), :], dst.at[pl.ds(row, rows), cols], sem
                    ).start()


def wide_body(columns, scal, a, b, *refs):
    i = pl.program_id(0)
    last = pl.num_programs(0) - 1
    slot = i & 1
    rows, half = D // 8, D // 2
    if columns:
        mixture, low, keep, send, stage, sems = refs
    else:
        keep, send, stage, sems = refs

    @pl.when(i >= 2)
    def _():
        arrive(stage.at[slot], sems.at[slot])

    if columns:

        @pl.when(i < 8)
        def _():
            stage[slot] = mm(a[...], b[...], 0, 0).astype(BF16)
            scatter_tile(scal, stage.at[slot], keep, send, sems.at[slot], [i], rows, 0, True)

        @pl.when(i >= 8)
        def _():
            part = i - 8
            left = mixture[:, pl.ds(pl.multiple_of(part * half, 128), half)]
            blocks = [part * 4 + n for n in range(4)]
            tile = mm(left, low[...], 0, 0).astype(BF16)
            for n in range(2):
                at = slice(n * half, (n + 1) * half)
                stage[slot, at, :] = tile[:, at]
                scatter_tile(
                    scal, stage.at[slot, pl.ds(n * half, half)], keep, send, sems.at[slot],
                    blocks, rows // 4, rows, across=n,
                )

    else:
        stage[slot] = mm(a[...], b[...], 0, 0).astype(BF16)
        scatter_tile(scal, stage.at[slot], keep, send, sems.at[slot], [i], rows, 0)

    @pl.when(i == last)
    def _():
        arrive(stage.at[1 - slot], sems.at[1 - slot])
        arrive(stage.at[slot], sems.at[slot])


def wide_grad(scal, a, b, columns, square=()):
    m = a.shape[0]
    half = D // 2
    full = pl.BlockSpec((m, D), lambda i: (0, 0))
    part = pl.BlockSpec((m, half), lambda i: (0, jnp.minimum(i, 7)))
    shape = sds((2, 2, 4, D // 8 + (D // 32 if columns else 0), D), BF16)
    return pl.pallas_call(
        functools.partial(wide_body, columns),
        grid=(10 if columns else 8,),
        in_specs=[SMEM] + ([full, part, full, full] if columns else [part, full]),
        out_specs=[ANY, ANY],
        out_shape=[shape, shape],
        scratch_shapes=[
            pltpu.VMEM((2, D, half) if columns else (2, half, D), BF16),
            pltpu.SemaphoreType.DMA((2,)),
        ],
        compiler_params=PARAMS,
    )(scal, a, b, *square)


def square_body(count, scal, left, *refs):
    rights, (keep, send, stage, sems) = refs[:count], refs[count:]
    rows = D // 32
    half = D // 2
    for m in range(count):

        def piece(part, _):
            if m:
                arrive(stage.at[part], sems.at[part])
            at = pl.ds(pl.multiple_of(part * half, 128), half)
            stage[part] = mm(left[:, at], rights[m][...], 0, 0).astype(BF16)
            blocks = [part * 4 + n for n in range(4)]
            scatter_tile(scal, stage.at[part], keep, send, sems.at[part], blocks, rows, m * rows)
            return 0

        lax.fori_loop(0, 2, piece, 0)
    for slot in range(2):
        arrive(stage.at[slot], sems.at[slot])


def square_grads(scal, left, *rights):
    shape = sds((2, 2, 4, len(rights) * D // 32, D), BF16)
    return pl.pallas_call(
        functools.partial(square_body, len(rights)),
        in_specs=[SMEM] + [pl.BlockSpec(memory_space=pltpu.VMEM)] * (1 + len(rights)),
        out_specs=[ANY, ANY],
        out_shape=[shape, shape],
        scratch_shapes=[pltpu.VMEM((2, D // 2, D), BF16), pltpu.SemaphoreType.DMA((2,))],
        compiler_params=PARAMS,
    )(scal, left, *rights)


BOTH = ("fsdp", "dp")


def flip(v, f_of=0, p_of=0):
    pairs = [
        (f * 4 + p, (f ^ f_of) * 4 + (p ^ p_of)) for f in range(8) for p in range(4)
    ]
    return lax.ppermute(v, BOTH, pairs)


def flip_by_core(v, first, second):
    pairs = []
    for f in range(8):
        for p in range(4):
            df, dp = second if p & 1 else first
            pairs.append((f * 4 + p, (f ^ df) * 4 + (p ^ dp)))
    return lax.ppermute(v, BOTH, pairs)


Y_OF, X_OF = (1, 0), (0, 2)


def up32(*vs):
    out = vs[0].astype(F32)
    for v in vs[1:]:
        out = out + v.astype(F32)
    return out


def together(*groups):
    flat, tree = jax.tree.flatten(groups)
    return jax.tree.unflatten(tree, lax.optimization_barrier(tuple(flat)))


def flips_z(v):
    return [flip(v[k], 2 * k) for k in (1, 2, 3)]


class Gather:
    def along_z(self, piece):
        self.now = [piece] + flips_z([piece] * 4)

    def along_xy(self):
        self.held = jnp.stack(self.now)
        self.now = [flip_by_core(self.held, Y_OF, X_OF), flip_by_core(self.held, X_OF, Y_OF)]

    def along_rest(self):
        one, two = self.now
        self.mine = [self.held, one, two]
        self.now = [flip_by_core(one, X_OF, Y_OF)] + [flip(v, 0, 1) for v in self.mine]

    def along_core(self):
        three, *others = self.now
        self.all = self.mine + [three] + others
        self.now = flip(three, 0, 1)

    def done(self):
        return self.all + [self.now]


class Sum:
    def along_core(self, keep, send):
        self.keep = keep
        self.now = flip(send, 0, 1)

    def along_first(self):
        self.r = self.now
        part = up32(self.keep[1], self.r[1]).astype(BF16)
        self.now = flip_by_core(part, X_OF, Y_OF)

    def along_second(self):
        self.r1 = self.now
        part = up32(self.keep[0, 1], self.r[0, 1], self.r1[1]).astype(BF16)
        self.now = flip_by_core(part, Y_OF, X_OF)

    def along_z(self):
        self.r2 = self.now
        parts = [
            up32(self.keep[0, 0, k], self.r[0, 0, k], self.r1[0, k], self.r2[k]) for k in range(4)
        ]
        self.own = parts[0]
        self.now = flips_z([t.astype(BF16) for t in parts])

    def back(self):
        self.own = up32(self.own, *self.now).astype(BF16)
        self.now = [flip(self.own, 0, j) for j in (1, 2, 3)]

    def done(self):
        return order_dp((self.own, *self.now))


def order_dp(parts):
    p = lax.axis_index("dp")
    low, high = (p & 1) == 1, (p >> 1) == 1
    a, b, c, d = parts
    a, b, c, d = (
        jnp.where(low, b, a),
        jnp.where(low, a, b),
        jnp.where(low, d, c),
        jnp.where(low, c, d),
    )
    return (
        jnp.where(high, c, a),
        jnp.where(high, d, b),
        jnp.where(high, a, c),
        jnp.where(high, b, d),
    )


def spread_dp(done):
    over = flip(done, 0, 2)
    return order_dp((done, flip(done, 0, 1), over, flip(over, 0, 1)))


def on_device(
    sizes,
    inputs,
    cotangent,
    timesteps,
    layouts,
    step_table,
    first_gain,
    first_shift,
    query_matrix,
    query_bias,
    key_matrix,
    value_matrix,
    value_bias,
    out_matrix,
    out_bias,
    second_gain,
    second_shift,
    up_matrix,
    up_bias,
    down_matrix,
    down_bias,
):
    n_fsdp, n_dp = sizes
    fast = (n_fsdp, n_dp) == (8, 4)
    f, p = lax.axis_index("fsdp"), lax.axis_index("dp")
    scal = jnp.stack([f, p]).astype(jnp.int32)
    row_count = inputs.shape[0]
    win = row_count // layouts.shape[0]
    ff = up_matrix.shape[1] * n_fsdp
    steps = step_table.shape[0]
    pairs = timesteps.reshape(-1, 2)
    first_steps = pairs[:, 0]
    second_steps = jnp.where(layouts == 1, first_steps, pairs[:, 1])
    slot_steps = jnp.stack([first_steps, second_steps], axis=1).reshape(-1)
    vecs = (
        first_gain,
        first_shift,
        query_bias,
        value_bias,
        out_bias,
        second_gain,
        second_shift,
        down_bias,
        up_bias,
    )
    mats = (query_matrix, key_matrix, value_matrix, out_matrix, up_matrix, down_matrix)
    r = D // 32
    if fast:
        return exchange_and_run(
            scal, inputs, cotangent, layouts, step_table, slot_steps, vecs, mats, win, ff, f
        )
    cot_low = cotangent.astype(BF16)
    low = [m.astype(BF16) for m in vecs + mats]
    full = [lax.all_gather(m, "fsdp", axis=0, tiled=True) for m in low[:9]]
    vec = jnp.concatenate(full).reshape(12, D).astype(F32)
    w_qkv = [lax.all_gather(m, "fsdp", axis=0, tiled=True) for m in low[9:12]]
    w_out = [lax.all_gather(low[12], "fsdp", axis=0, tiled=True)]
    w_up = [lax.all_gather(low[13], "fsdp", axis=1, tiled=True)]
    w_down = [lax.all_gather(low[14], "fsdp", axis=0, tiled=True)]
    table = lax.all_gather(step_table.astype(BF16), "fsdp", axis=1, tiled=True)
    rel = jnp.take(table, slot_steps, axis=0).astype(F32)
    count = layouts.shape[0]

    normed, q, k, v, slots, vec = qkv(scal, inputs, rel, w_qkv, vec, win)
    mixture = attend(scal, layouts, q, k, v)
    attended, second = mix(scal, mixture, inputs, slots, vec, w_out, win)
    hidden, pre, up_add = mlp(scal * 0, second, cot_low, vec, w_up, w_down, ff)
    grad, low, sums2 = second_back(scal, pre, attended, cotangent, vec, w_up, win)
    dq, dk, dv = attend_back(scal, layouts, low, q, k, v, w_out, 0, count)
    input_grad, slot_sums, sums1 = first_back(
        scal, dq, dk, dv, inputs, grad, slots, vec, w_qkv, win
    )
    block_output = down_out(scal, hidden, attended, vec, w_down, win, 0, count)

    total_of = lambda v, dim: lax.psum(
        lax.psum_scatter(v, "fsdp", scatter_dimension=dim, tiled=True), "dp"
    )
    down_grad = total_of(mm(hidden, cot_low, 0, 0), 0)
    up_grad = total_of(mm(second, pre, 0, 0), 1)
    out_grad = total_of(mm(mixture, low, 0, 0), 0)
    query_grad = total_of(mm(normed, dq, 0, 0), 0)
    key_grad = total_of(mm(normed, dk, 0, 0), 0)
    value_grad = total_of(mm(normed, dv, 0, 0), 0)
    small = lax.psum(vector_sums(sums1, sums2, up_add), BOTH)
    table_grad = total_of(jnp.zeros((steps, D), F32).at[slot_steps].add(slot_sums), 1)
    return results(
        block_output, input_grad, table_grad, small, f, n_fsdp, ff,
        query_grad, key_grad, value_grad, out_grad, up_grad, down_grad,
    )


def vector_sums(sums1, sums2, up_add):
    return jnp.concatenate(
        [sums1[:4], sums2[2:3], sums2[:2], sums2[3:4], up_add.reshape(-1, D)], axis=0
    )


def results(
    block_output, input_grad, table_grad, small, f, n_fsdp, ff,
    query_grad, key_grad, value_grad, out_grad, up_grad, down_grad,
):
    width = D // n_fsdp
    mine = lax.dynamic_slice(small[:8], (0, f * width), (8, width))
    up_mine = lax.dynamic_slice(small[8:].reshape(-1), (f * (ff // n_fsdp),), (ff // n_fsdp,))
    return named(
        block_output, input_grad, table_grad, mine, up_mine,
        query_grad, key_grad, value_grad, out_grad, up_grad, down_grad,
    )


def named(
    block_output, input_grad, table_grad, mine, up_mine,
    query_grad, key_grad, value_grad, out_grad, up_grad, down_grad,
):
    return (
        block_output,
        input_grad,
        table_grad,
        mine[0],
        mine[1],
        query_grad,
        mine[2],
        key_grad,
        value_grad,
        mine[3],
        out_grad,
        mine[4],
        mine[5],
        mine[6],
        up_grad,
        up_mine,
        down_grad,
        mine[7],
    )


def exchange_and_run(
    scal, inputs, cotangent, layouts, step_table, slot_steps, vecs, mats, win, ff, f
):
    r = D // 32
    at_up = dict(row=r, rows=D // 8)
    at_down = dict(rows=D // 8)
    one, two, three = Gather(), Gather(), Gather()

    pieces = prep(scal, vecs, mats)
    y_steps = jnp.stack([slot_steps, flip(slot_steps, 1)])
    pieces, y_steps = together(pieces, y_steps)

    one.along_z(pieces[0])
    z_steps = flips_z([y_steps] * 4)
    cot_low = cotangent.astype(BF16)
    one.now, z_steps, cot_low, pieces = together(one.now, z_steps, cot_low, pieces)

    one.along_xy()
    all_steps = jnp.stack([y_steps] + z_steps)
    asked = jnp.take(step_table, all_steps, axis=0).astype(BF16)
    back = jnp.stack([asked[0]] + flips_z(asked))
    two.along_z(pieces[1])
    one.now, back = together(one.now, back)

    one.along_rest()
    given = jnp.stack([back[:, 0], flip(back[:, 1], 1)], axis=1)
    one.now, given, pieces = together(one.now, given, pieces)

    one.along_core()
    rel = given.reshape(8, given.shape[2], given.shape[3]).astype(F32)
    one.now, rel, pieces, two.now = together(one.now, rel, pieces, two.now)

    two.along_xy()
    three.along_z(pieces[2])
    w_qkv = one.done()
    normed, q, k, v, slots, vec = qkv(scal, inputs, rel, w_qkv, None, win)
    q, k, v, two.now, three.now = together(q, k, v, two.now, three.now)

    two.along_rest()
    three.along_xy()
    mixture = attend(scal, layouts, q, k, v)
    mixture, two.now, three.now = together(mixture, two.now, three.now)

    two.along_core()
    three.along_rest()
    mixture, two.now = together(mixture, two.now)

    w_two = two.done()
    attended, second = mix(scal, mixture, inputs, slots, vec, w_two, win)
    attended, second, three.now = together(attended, second, three.now)

    three.along_core()
    second, three.now = together(second, three.now)

    w_down = three.done()
    hidden, pre, up_add = mlp(scal, second, cot_low, vec, w_two, w_down, ff, r, D // 8)
    down = Sum()
    kept = wide_grad(scal, hidden, cot_low, False)
    kept, pre = together(kept, pre)

    down.along_core(*kept)
    grad, low, sums2 = second_back(scal, pre, attended, cotangent, vec, w_two, win, **at_up)
    grad, low, pre, down.now = together(grad, low, pre, down.now)

    down.along_first()
    up = Sum()
    kept = wide_grad(scal, second, pre, True, (mixture, low))
    kept, low, down.now = together(kept, low, down.now)

    down.along_second()
    up.along_core(*kept)
    halves = layouts.shape[0] // 2
    back1 = attend_back(scal, layouts, low, q, k, v, w_two, 0, halves)
    back1, down.now, up.now = together(back1, down.now, up.now)

    down.along_z()
    up.along_first()
    dq, dk, dv = attend_back(scal, layouts, low, q, k, v, w_two, halves, halves, back1)
    dq, dk, dv, down.now, up.now = together(dq, dk, dv, down.now, up.now)

    down.back()
    up.along_second()
    square = Sum()
    kept = square_grads(scal, normed, dq, dk, dv)
    kept, dq, dk, dv, down.now, up.now, hidden = together(
        kept, dq, dk, dv, down.now, up.now, hidden
    )

    square.along_core(*kept)
    up.along_z()
    part = down_out(scal, hidden, attended, vec, w_down, win, 0, halves, **at_down)
    square.now, part, dq = together(square.now, part, dq)

    square.along_first()
    input_grad, slot_sums, sums1 = first_back(
        scal, dq, dk, dv, inputs, grad, slots, vec, w_qkv, win
    )
    small = vector_sums(sums1, sums2, up_add)
    small, slot_sums, square.now, up.now, part = together(
        small, slot_sums, square.now, up.now, part
    )

    width = D // 8
    count = slot_sums.shape[0]
    own = jnp.concatenate([slot_sums, small[:8]]).reshape(-1, 8, width).swapaxes(0, 1)
    own = jnp.concatenate([own, small[8:].reshape(8, -1, width)], axis=1)
    own = jnp.stack([lax.dynamic_index_in_dim(own, f ^ j, 0, False) for j in range(8)])
    tag = jnp.zeros((8, 1, width), F32).at[:, 0, :count].set(slot_steps.astype(F32))
    own = jnp.concatenate([own, tag], axis=1)
    own = own.reshape(4, 2, *own.shape[1:])
    up.back()
    square.along_second()
    own_y = flip(own[:, 1], 1)
    block_output = down_out(
        scal, hidden, attended, vec, w_down, win, halves, halves, so_far=(part,), **at_down
    )
    block_output, own_y, up.now, square.now = together(block_output, own_y, up.now, square.now)

    square.along_z()
    own = jnp.stack([own[:, 0], own_y], axis=1)
    own_z = flips_z(own)
    half = D // 2
    down_grad = jnp.concatenate(down.done(), axis=0).astype(F32)
    square.now, own_z, down_grad = together(square.now, own_z, down_grad)

    square.back()
    own = jnp.stack([own[0]] + own_z).reshape(8, *own.shape[2:])
    parts = [own] + [flip(own, 0, j) for j in (1, 2, 3)]
    got = up.done()
    u = D // 8
    up_grad = jnp.concatenate(
        [t for m in got for t in (m[:u, :half], m[:u, half:])], axis=0
    ).astype(F32)
    out_grad = jnp.concatenate([m[u:] for m in got], axis=0).astype(F32)
    square.now, parts, up_grad, out_grad = together(square.now, parts, up_grad, out_grad)

    query_grad, key_grad, value_grad = (
        jnp.concatenate([m[j * r : (j + 1) * r] for m in square.done()], axis=0).astype(F32)
        for j in range(3)
    )
    every = jnp.stack(order_dp(parts)).reshape(-1, *own.shape[1:])
    steps = every[:, -1, :count].astype(jnp.int32).reshape(-1)
    table_grad = (
        jnp.zeros((step_table.shape[0], width), F32)
        .at[steps]
        .add(every[:, :count].reshape(-1, width))
    )
    mine = jnp.sum(every[:, count:-1], axis=0)
    return named(
        block_output, input_grad, table_grad, mine, mine[8:].reshape(-1),
        query_grad, key_grad, value_grad, out_grad, up_grad, down_grad,
    )


def solution(mesh):
    rows = P(("fsdp", "dp"), None)
    slots = P(("fsdp", "dp"))
    vector = P("fsdp")
    matrix = P("fsdp", None)
    wide = P(None, "fsdp")
    placed = (
        rows, rows, slots, slots, wide, vector, vector, matrix, vector, matrix,
        matrix, vector, matrix, vector, vector, vector, wide, vector, matrix, vector,
    )
    returned = (
        rows, rows, wide, vector, vector, matrix, vector, matrix, matrix, vector,
        matrix, vector, vector, vector, wide, vector, matrix, vector,
    )
    return jax.shard_map(
        functools.partial(on_device, (mesh.shape["fsdp"], mesh.shape["dp"])),
        mesh=mesh,
        in_specs=placed,
        out_specs=returned,
        check_vma=False,
    )
```

```python
import functools
import math

import jax
import jax.numpy as jnp
from jax import lax
from jax.experimental import pallas as pl
from jax.experimental.pallas import tpu as pltpu
from jax.sharding import PartitionSpec as P

HEADS = 12
HEAD = 64
D = HEADS * HEAD
F32 = jnp.float32
BF16 = jnp.bfloat16
ANY = pl.BlockSpec(memory_space=pl.ANY)
SMEM = pl.BlockSpec(memory_space=pltpu.SMEM)
PARAMS = pltpu.CompilerParams(vmem_limit_bytes=60 * 1024 * 1024)

TAIL_P = 0.3
TAIL = (
    0.11962929811062077,
    0.12075396817215742,
    0.0999134093206875,
    0.12856192203768363,
    -0.053684240767073,
    0.20635418971029199,
    -0.15720349531083133,
    0.0356748757872949,
)

GAIN1, SHIFT1, QADD, VADD, OADD, GAIN2, SHIFT2, DADD, UADD = range(9)


def whole(shape):
    return pl.BlockSpec(shape, lambda *_: (0,) * len(shape))


def sds(shape, dtype):
    return jax.ShapeDtypeStruct(shape, dtype)


def mm(a, b, ca=1, cb=0):
    return lax.dot_general(a, b, (((ca,), (cb,)), ((), ())), preferred_element_type=F32)


def place(scal, buf, other, k):
    f, p = scal[0], scal[1]
    y, z, c, x = f & 1, f >> 1, p & 1, p >> 1
    core = c ^ other
    by_y = 1 - core if buf == 1 else core if buf == 2 else buf // 3
    by_x = core if buf == 1 else 1 - core if buf == 2 else buf // 3
    return ((z ^ k) << 1) | (y ^ by_y), ((x ^ by_x) << 1) | core


def fetch(scal, refs, dst, sem, row=0, rows=0, columns=False, parts=range(4)):
    if len(refs) == 1 and len(parts) == 4:
        pltpu.make_async_copy(refs[0], dst, sem).start()
        return
    if len(refs) == 1:
        size = dst.shape[columns] // 4
        at = pl.ds(pl.multiple_of((parts[0] ^ (scal[0] >> 1)) * size, size), size)
        at = (slice(None), at) if columns else (at, slice(None))
        pltpu.make_async_copy(refs[0].at[at], dst.at[at], sem).start()
        return
    for other in range(2):
        for buf in range(4):
            for k in parts:
                f, p = place(scal, buf, other, k)
                src = refs[other * 4 + buf].at[k]
                if columns:
                    half = D // 2
                    for part in range(2):
                        r = pl.multiple_of(p * 2 * rows + part * rows, 8)
                        pltpu.make_async_copy(
                            src.at[pl.ds(row, rows), pl.ds(part * half, half)],
                            dst.at[pl.ds(r, rows), pl.ds(pl.multiple_of(f * half, 128), half)],
                            sem,
                        ).start()
                else:
                    r = pl.multiple_of((f * 4 + p) * rows, 8)
                    pltpu.make_async_copy(
                        src.at[pl.ds(row, rows), :], dst.at[pl.ds(r, rows), :], sem
                    ).start()


def arrive(dst, sem):
    pltpu.make_async_copy(dst, dst, sem).wait()


def prep_body(scal, *refs):
    vecs, (q, k, v, o, up, down), (one, two, three) = refs[:9], refs[9:15], refs[15:]
    up_add = vecs[8][...]
    left = jnp.concatenate([r[...] for r in vecs[:8]], axis=0)
    left = jnp.concatenate([left, jnp.zeros((8, D // 2 - left.shape[1]), F32)], axis=1)
    right = jnp.concatenate([up_add, jnp.zeros((7, D // 2), F32)], axis=0)
    one[0:8, :] = jnp.concatenate([left, right], axis=1).astype(BF16)
    r = q.shape[0]
    for i, m in enumerate((q, k, v)):
        one[8 + i * r : 8 + (i + 1) * r, :] = m[...].astype(BF16)
    two[0:r, :] = o[...].astype(BF16)
    u = up.shape[0] // 2
    two[r : r + u, 0 : D // 2] = up[0:u, :].astype(BF16)
    two[r : r + u, D // 2 : D] = up[u : 2 * u, :].astype(BF16)
    three[...] = down[...].astype(BF16)


def prep(scal, vecs, mats):
    q, up, down = mats[0], mats[4], mats[5]
    r, u, d = q.shape[0] // 4, up.shape[0] // 4, down.shape[0] // 4
    half = up.shape[1]
    mine = lambda rows, cols: pl.BlockSpec((rows, cols), lambda i, s: (s[1], 0))
    vecs = [v.reshape(1, -1) for v in vecs]
    return pl.pallas_call(
        prep_body,
        grid_spec=pltpu.PrefetchScalarGridSpec(
            num_scalar_prefetch=1,
            grid=(1,),
            in_specs=[pl.BlockSpec(v.shape, lambda i, s: (0, 0)) for v in vecs]
            + [mine(r, D)] * 4
            + [mine(u, half), mine(d, D)],
            out_specs=[
                pl.BlockSpec(s, lambda i, s_: (0, 0))
                for s in ((8 + 3 * r, D), (r + u // 2, D), (d, D))
            ],
        ),
        out_shape=(sds((8 + 3 * r, D), BF16), sds((r + u // 2, D), BF16), sds((d, D), BF16)),
        compiler_params=PARAMS,
    )(scal, *vecs, *mats)


def normal_rows(v):
    c = v - jnp.mean(v, axis=-1, keepdims=True)
    r = lax.rsqrt(jnp.mean(c * c, axis=-1, keepdims=True) + 1e-05)
    return c * r, r


def stamp(x, slots, i):
    half = x.shape[0] // 2
    return jnp.concatenate(
        [x[:half] + slots[pl.ds(2 * i, 1), :], x[half:] + slots[pl.ds(2 * i + 1, 1), :]], axis=0
    )


def qkv_body(n, shape, scal, x, rel, *refs):
    weights, refs = refs[:n], refs[n:]
    if n != 8:
        vec_in, refs = refs[0], refs[1:]
    normed, q, k, v, slots_out, vec_out, wq, wk, wv, small, sems = refs
    i = pl.program_id(0)

    @pl.when(i == 0)
    def _():
        if n == 8:
            rows = shape
            for j, w in enumerate((wq, wk, wv)):
                fetch(scal, weights, w, sems.at[j], 8 + j * rows, rows)
            for buf in range(4):
                for z in range(4):
                    f, _ = place(scal, buf, 0, z)
                    if buf in (0, 1, 2):
                        pass
                    pltpu.make_async_copy(
                        weights[buf].at[z, pl.ds(0, 8), :], small.at[buf * 4 + z], sems.at[3]
                    ).start()
            f0 = scal[0]
            slots_out[...] = jnp.concatenate([rel[f0 ^ f] for f in range(8)], axis=1)
            arrive(small, sems.at[3])
            core = scal[1] & 1
            flip = jnp.where(core == 0, 1, 2)
            parts = []
            for f in range(8):
                zz = (f >> 1) ^ (f0 >> 1)
                yy = (f & 1) ^ (f0 & 1)
                parts.append(small[yy * flip * 4 + zz].astype(F32))
            vec_out[0:8, :] = jnp.concatenate([t[:, : D // 8] for t in parts], axis=1)
            for j in range(4):
                vec_out[8 + j : 9 + j, :] = jnp.concatenate(
                    [parts[2 * j][0:1, D // 2 :], parts[2 * j + 1][0:1, D // 2 :]], axis=1
                )
        else:
            for j, w in enumerate((wq, wk, wv)):
                fetch(scal, weights[j : j + 1], w, sems.at[j])
            slots_out[...] = rel[...]
            vec_out[...] = vec_in[...]
        for j, w in enumerate((wq, wk, wv)):
            arrive(w, sems.at[j])

    n1, _ = normal_rows(stamp(x[...], slots_out, i))
    low = (n1 * vec_out[GAIN1 : GAIN1 + 1, :] + vec_out[SHIFT1 : SHIFT1 + 1, :]).astype(BF16)
    normed[...] = low
    q[...] = (mm(low, wq[...]) + vec_out[QADD : QADD + 1, :]).astype(BF16)
    k[...] = mm(low, wk[...]).astype(BF16)
    v[...] = (mm(low, wv[...]) + vec_out[VADD : VADD + 1, :]).astype(BF16)


def qkv(scal, x, rel, weights, vec, win):
    rows = x.shape[0]
    slots = 2 * (rows // win)
    n = len(weights)
    blk = pl.BlockSpec((win, D), lambda i: (i, 0))
    ins = [SMEM, blk, whole(rel.shape)] + [ANY] * n
    args = [scal, x, rel, *weights]
    if n != 8:
        ins.append(whole(vec.shape))
        args.append(vec)
    return pl.pallas_call(
        functools.partial(qkv_body, n, D // 32),
        grid=(rows // win,),
        in_specs=ins,
        out_specs=[blk] * 4 + [whole((slots, D)), whole((12, D))],
        out_shape=[sds((rows, D), BF16)] * 4 + [sds((slots, D), F32), sds((12, D), F32)],
        scratch_shapes=[pltpu.VMEM((D, D), BF16)] * 3
        + [pltpu.VMEM((16, 8, D), BF16), pltpu.SemaphoreType.DMA((4,))],
        compiler_params=PARAMS,
    )(*args)


def lane_mask(half):
    lane = lax.broadcasted_iota(jnp.int32, (1, 2 * HEAD), 1)
    return (lane >= HEAD) if half else (lane < HEAD)


def permitted(win, layout):
    a = lax.broadcasted_iota(jnp.int32, (win, win), 0) // (win // 2)
    b = lax.broadcasted_iota(jnp.int32, (win, win), 1) // (win // 2)
    return (a == b) | (layout == 1)


def attend_body(scal, lay, q, k, v, mixture):
    allowed = permitted(q.shape[0], lay[pl.program_id(0)])

    def pair(j, _):
        at = pl.ds(pl.multiple_of(j * 2 * HEAD, 2 * HEAD), 2 * HEAD)
        qp, kp, vp = q[:, at] * 0.125, k[:, at], v[:, at]
        got = []
        for half in range(2):
            s = mm(jnp.where(lane_mask(half), qp, 0), kp, 1, 1)
            s = jnp.where(allowed, s, -1e30)
            e = jnp.exp(s - jnp.max(s, axis=-1, keepdims=True))
            a = e * (1.0 / jnp.sum(e, axis=-1, keepdims=True))
            got.append(mm(a.astype(BF16), vp))
        mixture[:, at] = jnp.where(lane_mask(0), got[0], got[1]).astype(BF16)
        return 0

    lax.fori_loop(0, HEADS // 2, pair, 0, unroll=True)


def attend(scal, lay, q, k, v):
    rows = q.shape[0]
    win = rows // lay.shape[0]
    blk = pl.BlockSpec((win, D), lambda i: (i, 0))
    return pl.pallas_call(
        attend_body,
        grid=(rows // win,),
        in_specs=[SMEM, SMEM] + [blk] * 3,
        out_specs=blk,
        out_shape=sds((rows, D), BF16),
        compiler_params=PARAMS,
    )(scal, lay, q, k, v)


def mix_body(n, rows, scal, mixture, x, slots, vec, *refs):
    weights, refs = refs[:n], refs[n:]
    attended, second, wo, sems = refs
    i = pl.program_id(0)

    @pl.when(i == 0)
    def _():
        fetch(scal, weights, wo, sems, 0, rows)
        arrive(wo, sems)

    att = stamp(x[...], slots, i) + mm(mixture[...], wo[...]) + vec[OADD : OADD + 1, :]
    attended[...] = att
    n2, _ = normal_rows(att)
    second[...] = (n2 * vec[GAIN2 : GAIN2 + 1, :] + vec[SHIFT2 : SHIFT2 + 1, :]).astype(BF16)


def mix(scal, mixture, x, slots, vec, weights, win):
    rows = x.shape[0]
    n = len(weights)
    blk = pl.BlockSpec((win, D), lambda i: (i, 0))
    return pl.pallas_call(
        functools.partial(mix_body, n, D // 32),
        grid=(rows // win,),
        in_specs=[SMEM, blk, blk, whole(slots.shape), whole(vec.shape)] + [ANY] * n,
        out_specs=[blk] * 2,
        out_shape=[sds((rows, D), F32), sds((rows, D), BF16)],
        scratch_shapes=[pltpu.VMEM((D, D), BF16), pltpu.SemaphoreType.DMA],
        compiler_params=PARAMS,
    )(scal, mixture, x, slots, vec, *weights)


TILE = 256


def mlp_body(n, row_up, rows, scal, second, cot, vec, *refs):
    w_up, w_down, refs = refs[:n], refs[n : 2 * n], refs[2 * n :]
    hidden, low, add, wu, wd, pre_a, pre_b, grad_a, grad_b, sems = refs
    i = pl.program_id(0)
    last = pl.num_programs(0) - 1
    across = D // TILE
    units = (second.shape[0] // TILE) * across
    own = scal[0] >> 1

    def wait(g):
        arrive(wu.at[:, pl.ds(0, D)], sems.at[0, g])
        arrive(wd.at[pl.ds(0, D), :], sems.at[1, g])

    def tile(u):
        r = pl.multiple_of((u // across) * TILE, TILE)
        return pl.ds(r, TILE), (u % across) * TILE

    def multiply(step, u, pre, grad):
        at, col = tile(u)
        cols = pl.ds(pl.multiple_of((step ^ own) * D + col, TILE), TILE)
        pre[...] = mm(second[at, :], wu[:, cols])
        grad[...] = mm(cot[at, :], wd[cols, :], 1, 1)

    def finish(n, pre, grad):
        at, col = tile(n)
        cols = pl.ds(pl.multiple_of(col, TILE), TILE)
        bias = vec[pl.ds(8 + (i ^ own), 1), cols]
        u = pre[...] + bias
        a = jnp.abs(u)
        t = 1.0 / (1.0 + TAIL_P * a)
        e = jnp.exp2((-0.5 * math.log2(math.e)) * (u * u))
        acc = jnp.full_like(t, TAIL[-1])
        for c in TAIL[-2::-1]:
            acc = acc * t + c
        tail = e * (t * acc)
        cdf = jnp.where(u >= 0, 1.0 - tail, tail)
        hidden[at, cols] = (u * cdf).astype(BF16)
        slope = cdf + u * (e * (1.0 / math.sqrt(2.0 * math.pi)))
        low[at, cols] = (grad[...] * slope).astype(BF16)
        new = mm(jnp.ones((8, TILE), BF16), low[at, cols])[:1]
        add[:, cols] = jnp.where(n < across, 0.0, add[:, cols]) + new

    @pl.when(i == 0)
    def _():
        for g in range(4):
            fetch(scal, w_up, wu, sems.at[0, g], row_up, rows, True, [g])
            fetch(scal, w_down, wd, sems.at[1, g], 0, rows, False, [g])
        wait(0)
        multiply(0, 0, pre_a, grad_a)

    @pl.when(i != last)
    def _():
        wait(i + 1)

    def two(p, _):
        n = 2 * p
        multiply(i, n + 1, pre_b, grad_b)
        finish(n, pre_a, grad_a)
        over = n + 2 == units
        multiply(jnp.where(over, jnp.minimum(i + 1, last), i), jnp.where(over, 0, n + 2), pre_a, grad_a)
        finish(n + 1, pre_b, grad_b)
        return 0

    lax.fori_loop(0, units // 2, two, 0)


def mlp(scal, second, cot, vec, w_up, w_down, ff, row_up=0, rows=0):
    n = len(w_up)
    m = second.shape[0]
    blk = lambda rows: pl.BlockSpec((rows, D), lambda i, s: (0, i ^ (s[0] >> 1)))
    tile = pltpu.VMEM((TILE, TILE), F32)
    return pl.pallas_call(
        functools.partial(mlp_body, n, row_up, rows),
        grid_spec=pltpu.PrefetchScalarGridSpec(
            num_scalar_prefetch=1,
            grid=(ff // D,),
            in_specs=[whole(second.shape), whole(cot.shape), whole(vec.shape)] + [ANY] * (2 * n),
            out_specs=[blk(m), blk(m), blk(1)],
            scratch_shapes=[pltpu.VMEM((D, ff), BF16), pltpu.VMEM((ff, D), BF16)]
            + [tile] * 4
            + [pltpu.SemaphoreType.DMA((2, 4))],
        ),
        out_shape=[sds((m, ff), BF16), sds((m, ff), BF16), sds((1, ff), F32)],
        compiler_params=PARAMS,
    )(scal, second, cot, vec, *w_up, *w_down)


def norm_back(e, n, r, gain):
    f = e * gain
    return r * (f - jnp.mean(f, -1, keepdims=True) - n * jnp.mean(f * n, -1, keepdims=True))


def total(v):
    return jnp.sum(v, axis=0, keepdims=True)


def accumulate(ref, i, rows):
    new = jnp.concatenate(rows + [jnp.zeros((8 - len(rows), D), F32)], axis=0)

    @pl.when(i == 0)
    def _():
        ref[...] = new

    @pl.when(i != 0)
    def _():
        ref[...] += new


def second_body(n, row, rows, scal, pre, attended, cot, vec, *refs):
    weights, refs = refs[:n], refs[n:]
    grad, low, sums, wu, sems = refs
    i = pl.program_id(0)

    @pl.when(i == 0)
    def _():
        fetch(scal, weights, wu, sems, row, rows, True)
        arrive(wu, sems)

    e = mm(pre[...], wu[...], 1, 1)
    n2, r = normal_rows(attended[...])
    c = cot[...]
    g = c + norm_back(e, n2, r, vec[GAIN2 : GAIN2 + 1, :])
    grad[...] = g
    low[...] = g.astype(BF16)
    accumulate(sums, i, [total(e * n2), total(e), total(g), total(c)])


def second_back(scal, pre, attended, cot, vec, weights, win, row=0, rows=0):
    n = len(weights)
    m, ff = pre.shape
    blk = pl.BlockSpec((win, D), lambda i: (i, 0))
    return pl.pallas_call(
        functools.partial(second_body, n, row, rows),
        grid=(m // win,),
        in_specs=[SMEM, pl.BlockSpec((win, ff), lambda i: (i, 0)), blk, blk, whole(vec.shape)]
        + [ANY] * n,
        out_specs=[blk, blk, whole((8, D))],
        out_shape=[sds((m, D), F32), sds((m, D), BF16), sds((8, D), F32)],
        scratch_shapes=[pltpu.VMEM((D, ff), BF16), pltpu.SemaphoreType.DMA],
        compiler_params=PARAMS,
    )(scal, pre, attended, cot, vec, *weights)


def attend_back_body(n, rows, start, filled, scal, lay, low, q, k, v, *refs):
    weights, refs = refs[:n], refs[n + filled :]
    dq, dk, dv, wo, mix, sems = refs
    i = pl.program_id(0)

    @pl.when(i == 0)
    def _():
        fetch(scal, weights, wo, sems, 0, rows)
        arrive(wo, sems)

    mix[...] = mm(low[...], wo[...], 1, 1).astype(BF16)
    win = q.shape[0]
    allowed = permitted(win, lay[i + start])

    def pair(j, _):
        at = pl.ds(pl.multiple_of(j * 2 * HEAD, 2 * HEAD), 2 * HEAD)
        qp, kp, vp, gp = q[:, at] * 0.125, k[:, at], v[:, at], mix[:, at]
        ks = kp * 0.125
        got = []
        for half in range(2):
            mask = lane_mask(half)
            s = mm(jnp.where(mask, kp, 0), qp, 1, 1)
            s = jnp.where(allowed, s, -1e30)
            e = jnp.exp(s - jnp.max(s, axis=0, keepdims=True))
            a = e * (1.0 / jnp.sum(e, axis=0, keepdims=True))
            t = a * mm(jnp.where(mask, vp, 0), gp, 1, 1)
            ds = (t - a * jnp.sum(t, axis=0, keepdims=True)).astype(BF16)
            got.append((mm(ds, ks, 0, 0), mm(ds, qp), mm(a.astype(BF16), gp)))
        for ref, first, last in zip((dq, dk, dv), got[0], got[1]):
            ref[:, at] = jnp.where(lane_mask(0), first, last).astype(BF16)
        return 0

    lax.fori_loop(0, HEADS // 2, pair, 0, unroll=3)


def attend_back(scal, lay, low, q, k, v, weights, start, count, so_far=()):
    n = len(weights)
    m = q.shape[0]
    win = m // lay.shape[0]
    blk = pl.BlockSpec((win, D), lambda i: (i + start, 0))
    return pl.pallas_call(
        functools.partial(attend_back_body, n, D // 32, start, len(so_far)),
        grid=(count,),
        in_specs=[SMEM, SMEM] + [blk] * 4 + [ANY] * (n + len(so_far)),
        out_specs=[blk] * 3,
        out_shape=[sds((m, D), BF16)] * 3,
        scratch_shapes=[
            pltpu.VMEM((D, D), BF16),
            pltpu.VMEM((win, D), BF16),
            pltpu.SemaphoreType.DMA,
        ],
        input_output_aliases={6 + n + j: j for j in range(len(so_far))},
        compiler_params=PARAMS,
    )(scal, lay, low, q, k, v, *weights, *so_far)


def first_body(n, rows, scal, dq, dk, dv, x, upper, slots, vec, *refs):
    weights, refs = refs[:n], refs[n:]
    out, slot_sums, sums, wq, wk, wv, sems = refs
    i = pl.program_id(0)

    @pl.when(i == 0)
    def _():
        for j, w in enumerate((wq, wk, wv)):
            src = weights if n == 8 else weights[j : j + 1]
            fetch(scal, src, w, sems.at[j], 8 + j * rows, rows)
        for j, w in enumerate((wq, wk, wv)):
            arrive(w, sems.at[j])

    e = mm(dq[...], wq[...], 1, 1) + mm(dk[...], wk[...], 1, 1) + mm(dv[...], wv[...], 1, 1)
    n1, r = normal_rows(stamp(x[...], slots, i))
    g = upper[...] + norm_back(e, n1, r, vec[GAIN1 : GAIN1 + 1, :])
    out[...] = g
    half = g.shape[0] // 2
    slot_sums[pl.ds(2 * i, 1), :] = total(g[:half])
    slot_sums[pl.ds(2 * i + 1, 1), :] = total(g[half:])
    accumulate(
        sums,
        i,
        [total(e * n1), total(e), total(dq[...].astype(F32)), total(dv[...].astype(F32))],
    )


def first_back(scal, dq, dk, dv, x, upper, slots, vec, weights, win):
    n = len(weights)
    m = x.shape[0]
    blk = pl.BlockSpec((win, D), lambda i: (i, 0))
    return pl.pallas_call(
        functools.partial(first_body, n, D // 32),
        grid=(m // win,),
        in_specs=[SMEM] + [blk] * 5 + [whole(slots.shape), whole(vec.shape)] + [ANY] * n,
        out_specs=[blk, whole(slots.shape), whole((8, D))],
        out_shape=[sds((m, D), F32), sds(slots.shape, F32), sds((8, D), F32)],
        scratch_shapes=[pltpu.VMEM((D, D), BF16)] * 3 + [pltpu.SemaphoreType.DMA((3,))],
        compiler_params=PARAMS,
    )(scal, dq, dk, dv, x, upper, slots, vec, *weights)


def down_body(n, rows, filled, scal, hidden, attended, vec, *refs):
    weights, refs = refs[:n], refs[n + filled :]
    out, wd, sems = refs
    i = pl.program_id(0)

    @pl.when(i == 0)
    def _():
        fetch(scal, weights, wd, sems, 0, rows)
        arrive(wd, sems)

    out[...] = attended[...] + mm(hidden[...], wd[...]) + vec[DADD : DADD + 1, :]


def down_out(scal, hidden, attended, vec, weights, win, start, count, rows=0, so_far=()):
    n = len(weights)
    m, ff = hidden.shape
    blk = pl.BlockSpec((win, D), lambda i: (i + start, 0))
    return pl.pallas_call(
        functools.partial(down_body, n, rows, len(so_far)),
        grid=(count,),
        in_specs=[SMEM, pl.BlockSpec((win, ff), lambda i: (i + start, 0)), blk, whole(vec.shape)]
        + [ANY] * (n + len(so_far)),
        out_specs=blk,
        out_shape=sds((m, D), F32),
        scratch_shapes=[pltpu.VMEM((ff, D), BF16), pltpu.SemaphoreType.DMA],
        input_output_aliases={4 + n: 0} if so_far else {},
        compiler_params=PARAMS,
    )(scal, hidden, attended, vec, *weights, *so_far)


def scatter_tile(scal, stage, keep, send, sem, blocks, rows, row, columns=False, across=None):
    f0, p0 = scal[0], scal[1]
    y, z, c, x = f0 & 1, f0 >> 1, p0 & 1, p0 >> 1
    for at, f in enumerate(blocks):
        dy, k = (f & 1) ^ y, (f >> 1) ^ z
        for px in range(2):
            dx = px ^ x
            for other, out in enumerate((keep, send)):
                core = c ^ other
                one = jnp.where(core == 0, dx, dy)
                two = jnp.where(core == 0, dy, dx)
                dst = out.at[one, two, k]
                piece = px * 2 + core
                if columns:
                    half = D // 2
                    for part in range(2):
                        pltpu.make_async_copy(
                            stage.at[pl.ds(pl.multiple_of((piece * 2 + part) * rows, 8), rows), :],
                            dst.at[pl.ds(row, rows), pl.ds(part * half, half)],
                            sem,
                        ).start()
                else:
                    src = pl.multiple_of((at * 4 + piece) * rows, 8)
                    cols = slice(None) if across is None else pl.ds(across * (D // 2), D // 2)
                    pltpu.make_async_copy(
                        stage.at[pl.ds(src, rows), :], dst.at[pl.ds(row, rows), cols], sem
                    ).start()


def wide_body(columns, scal, a, b, *refs):
    i = pl.program_id(0)
    last = pl.num_programs(0) - 1
    slot = i & 1
    rows, half = D // 8, D // 2
    if columns:
        mixture, low, keep, send, stage, sems = refs
    else:
        keep, send, stage, sems = refs

    @pl.when(i >= 2)
    def _():
        arrive(stage.at[slot], sems.at[slot])

    if columns:

        @pl.when(i < 8)
        def _():
            stage[slot] = mm(a[...], b[...], 0, 0).astype(BF16)
            scatter_tile(scal, stage.at[slot], keep, send, sems.at[slot], [i], rows, 0, True)

        @pl.when(i >= 8)
        def _():
            part = i - 8
            left = mixture[:, pl.ds(pl.multiple_of(part * half, 128), half)]
            blocks = [part * 4 + n for n in range(4)]
            tile = mm(left, low[...], 0, 0).astype(BF16)
            for n in range(2):
                at = slice(n * half, (n + 1) * half)
                stage[slot, at, :] = tile[:, at]
                scatter_tile(
                    scal, stage.at[slot, pl.ds(n * half, half)], keep, send, sems.at[slot],
                    blocks, rows // 4, rows, across=n,
                )

    else:
        stage[slot] = mm(a[...], b[...], 0, 0).astype(BF16)
        scatter_tile(scal, stage.at[slot], keep, send, sems.at[slot], [i], rows, 0)

    @pl.when(i == last)
    def _():
        arrive(stage.at[1 - slot], sems.at[1 - slot])
        arrive(stage.at[slot], sems.at[slot])


def wide_grad(scal, a, b, columns, square=()):
    m = a.shape[0]
    half = D // 2
    full = pl.BlockSpec((m, D), lambda i: (0, 0))
    part = pl.BlockSpec((m, half), lambda i: (0, jnp.minimum(i, 7)))
    shape = sds((2, 2, 4, D // 8 + (D // 32 if columns else 0), D), BF16)
    return pl.pallas_call(
        functools.partial(wide_body, columns),
        grid=(10 if columns else 8,),
        in_specs=[SMEM] + ([full, part, full, full] if columns else [part, full]),
        out_specs=[ANY, ANY],
        out_shape=[shape, shape],
        scratch_shapes=[
            pltpu.VMEM((2, D, half) if columns else (2, half, D), BF16),
            pltpu.SemaphoreType.DMA((2,)),
        ],
        compiler_params=PARAMS,
    )(scal, a, b, *square)


def square_body(count, scal, left, *refs):
    rights, (keep, send, stage, sems) = refs[:count], refs[count:]
    rows = D // 32
    half = D // 2
    for m in range(count):

        def piece(part, _):
            if m:
                arrive(stage.at[part], sems.at[part])
            at = pl.ds(pl.multiple_of(part * half, 128), half)
            stage[part] = mm(left[:, at], rights[m][...], 0, 0).astype(BF16)
            blocks = [part * 4 + n for n in range(4)]
            scatter_tile(scal, stage.at[part], keep, send, sems.at[part], blocks, rows, m * rows)
            return 0

        lax.fori_loop(0, 2, piece, 0)
    for slot in range(2):
        arrive(stage.at[slot], sems.at[slot])


def square_grads(scal, left, *rights):
    shape = sds((2, 2, 4, len(rights) * D // 32, D), BF16)
    return pl.pallas_call(
        functools.partial(square_body, len(rights)),
        in_specs=[SMEM] + [pl.BlockSpec(memory_space=pltpu.VMEM)] * (1 + len(rights)),
        out_specs=[ANY, ANY],
        out_shape=[shape, shape],
        scratch_shapes=[pltpu.VMEM((2, D // 2, D), BF16), pltpu.SemaphoreType.DMA((2,))],
        compiler_params=PARAMS,
    )(scal, left, *rights)


BOTH = ("fsdp", "dp")


def flip(v, f_of=0, p_of=0):
    pairs = [
        (f * 4 + p, (f ^ f_of) * 4 + (p ^ p_of)) for f in range(8) for p in range(4)
    ]
    return lax.ppermute(v, BOTH, pairs)


def flip_by_core(v, first, second):
    pairs = []
    for f in range(8):
        for p in range(4):
            df, dp = second if p & 1 else first
            pairs.append((f * 4 + p, (f ^ df) * 4 + (p ^ dp)))
    return lax.ppermute(v, BOTH, pairs)


Y_OF, X_OF = (1, 0), (0, 2)


def up32(*vs):
    out = vs[0].astype(F32)
    for v in vs[1:]:
        out = out + v.astype(F32)
    return out


def together(*groups):
    flat, tree = jax.tree.flatten(groups)
    return jax.tree.unflatten(tree, lax.optimization_barrier(tuple(flat)))


def flips_z(v):
    return [flip(v[k], 2 * k) for k in (1, 2, 3)]


class Gather:
    def along_z(self, piece):
        self.now = [piece] + flips_z([piece] * 4)

    def along_xy(self):
        self.held = jnp.stack(self.now)
        self.now = [flip_by_core(self.held, Y_OF, X_OF), flip_by_core(self.held, X_OF, Y_OF)]

    def along_rest(self):
        one, two = self.now
        self.mine = [self.held, one, two]
        self.now = [flip_by_core(one, X_OF, Y_OF)] + [flip(v, 0, 1) for v in self.mine]

    def along_core(self):
        three, *others = self.now
        self.all = self.mine + [three] + others
        self.now = flip(three, 0, 1)

    def done(self):
        return self.all + [self.now]


class Sum:
    def along_core(self, keep, send):
        self.keep = keep
        self.now = flip(send, 0, 1)

    def along_first(self):
        self.r = self.now
        part = up32(self.keep[1], self.r[1]).astype(BF16)
        self.now = flip_by_core(part, X_OF, Y_OF)

    def along_second(self):
        self.r1 = self.now
        part = up32(self.keep[0, 1], self.r[0, 1], self.r1[1]).astype(BF16)
        self.now = flip_by_core(part, Y_OF, X_OF)

    def along_z(self):
        self.r2 = self.now
        parts = [
            up32(self.keep[0, 0, k], self.r[0, 0, k], self.r1[0, k], self.r2[k]) for k in range(4)
        ]
        self.own = parts[0]
        self.now = flips_z([t.astype(BF16) for t in parts])

    def back(self):
        self.own = up32(self.own, *self.now).astype(BF16)
        self.now = [flip(self.own, 0, j) for j in (1, 2, 3)]

    def done(self):
        return order_dp((self.own, *self.now))


def order_dp(parts):
    p = lax.axis_index("dp")
    low, high = (p & 1) == 1, (p >> 1) == 1
    a, b, c, d = parts
    a, b, c, d = (
        jnp.where(low, b, a),
        jnp.where(low, a, b),
        jnp.where(low, d, c),
        jnp.where(low, c, d),
    )
    return (
        jnp.where(high, c, a),
        jnp.where(high, d, b),
        jnp.where(high, a, c),
        jnp.where(high, b, d),
    )


def spread_dp(done):
    over = flip(done, 0, 2)
    return order_dp((done, flip(done, 0, 1), over, flip(over, 0, 1)))


def on_device(
    sizes,
    inputs,
    cotangent,
    timesteps,
    layouts,
    step_table,
    first_gain,
    first_shift,
    query_matrix,
    query_bias,
    key_matrix,
    value_matrix,
    value_bias,
    out_matrix,
    out_bias,
    second_gain,
    second_shift,
    up_matrix,
    up_bias,
    down_matrix,
    down_bias,
):
    n_fsdp, n_dp = sizes
    fast = (n_fsdp, n_dp) == (8, 4)
    f, p = lax.axis_index("fsdp"), lax.axis_index("dp")
    scal = jnp.stack([f, p]).astype(jnp.int32)
    row_count = inputs.shape[0]
    win = row_count // layouts.shape[0]
    ff = up_matrix.shape[1] * n_fsdp
    steps = step_table.shape[0]
    pairs = timesteps.reshape(-1, 2)
    first_steps = pairs[:, 0]
    second_steps = jnp.where(layouts == 1, first_steps, pairs[:, 1])
    slot_steps = jnp.stack([first_steps, second_steps], axis=1).reshape(-1)
    vecs = (
        first_gain,
        first_shift,
        query_bias,
        value_bias,
        out_bias,
        second_gain,
        second_shift,
        down_bias,
        up_bias,
    )
    mats = (query_matrix, key_matrix, value_matrix, out_matrix, up_matrix, down_matrix)
    r = D // 32
    if fast:
        return exchange_and_run(
            scal, inputs, cotangent, layouts, step_table, slot_steps, vecs, mats, win, ff, f
        )
    cot_low = cotangent.astype(BF16)
    low = [m.astype(BF16) for m in vecs + mats]
    full = [lax.all_gather(m, "fsdp", axis=0, tiled=True) for m in low[:9]]
    vec = jnp.concatenate(full).reshape(12, D).astype(F32)
    w_qkv = [lax.all_gather(m, "fsdp", axis=0, tiled=True) for m in low[9:12]]
    w_out = [lax.all_gather(low[12], "fsdp", axis=0, tiled=True)]
    w_up = [lax.all_gather(low[13], "fsdp", axis=1, tiled=True)]
    w_down = [lax.all_gather(low[14], "fsdp", axis=0, tiled=True)]
    table = lax.all_gather(step_table.astype(BF16), "fsdp", axis=1, tiled=True)
    rel = jnp.take(table, slot_steps, axis=0).astype(F32)
    count = layouts.shape[0]

    normed, q, k, v, slots, vec = qkv(scal, inputs, rel, w_qkv, vec, win)
    mixture = attend(scal, layouts, q, k, v)
    attended, second = mix(scal, mixture, inputs, slots, vec, w_out, win)
    hidden, pre, up_add = mlp(scal * 0, second, cot_low, vec, w_up, w_down, ff)
    grad, low, sums2 = second_back(scal, pre, attended, cotangent, vec, w_up, win)
    dq, dk, dv = attend_back(scal, layouts, low, q, k, v, w_out, 0, count)
    input_grad, slot_sums, sums1 = first_back(
        scal, dq, dk, dv, inputs, grad, slots, vec, w_qkv, win
    )
    block_output = down_out(scal, hidden, attended, vec, w_down, win, 0, count)

    total_of = lambda v, dim: lax.psum(
        lax.psum_scatter(v, "fsdp", scatter_dimension=dim, tiled=True), "dp"
    )
    down_grad = total_of(mm(hidden, cot_low, 0, 0), 0)
    up_grad = total_of(mm(second, pre, 0, 0), 1)
    out_grad = total_of(mm(mixture, low, 0, 0), 0)
    query_grad = total_of(mm(normed, dq, 0, 0), 0)
    key_grad = total_of(mm(normed, dk, 0, 0), 0)
    value_grad = total_of(mm(normed, dv, 0, 0), 0)
    small = lax.psum(vector_sums(sums1, sums2, up_add), BOTH)
    table_grad = total_of(jnp.zeros((steps, D), F32).at[slot_steps].add(slot_sums), 1)
    return results(
        block_output, input_grad, table_grad, small, f, n_fsdp, ff,
        query_grad, key_grad, value_grad, out_grad, up_grad, down_grad,
    )


def vector_sums(sums1, sums2, up_add):
    return jnp.concatenate(
        [sums1[:4], sums2[2:3], sums2[:2], sums2[3:4], up_add.reshape(-1, D)], axis=0
    )


def results(
    block_output, input_grad, table_grad, small, f, n_fsdp, ff,
    query_grad, key_grad, value_grad, out_grad, up_grad, down_grad,
):
    width = D // n_fsdp
    mine = lax.dynamic_slice(small[:8], (0, f * width), (8, width))
    up_mine = lax.dynamic_slice(small[8:].reshape(-1), (f * (ff // n_fsdp),), (ff // n_fsdp,))
    return named(
        block_output, input_grad, table_grad, mine, up_mine,
        query_grad, key_grad, value_grad, out_grad, up_grad, down_grad,
    )


def named(
    block_output, input_grad, table_grad, mine, up_mine,
    query_grad, key_grad, value_grad, out_grad, up_grad, down_grad,
):
    return (
        block_output,
        input_grad,
        table_grad,
        mine[0],
        mine[1],
        query_grad,
        mine[2],
        key_grad,
        value_grad,
        mine[3],
        out_grad,
        mine[4],
        mine[5],
        mine[6],
        up_grad,
        up_mine,
        down_grad,
        mine[7],
    )


def exchange_and_run(
    scal, inputs, cotangent, layouts, step_table, slot_steps, vecs, mats, win, ff, f
):
    r = D // 32
    at_up = dict(row=r, rows=D // 8)
    at_down = dict(rows=D // 8)
    one, two, three = Gather(), Gather(), Gather()

    pieces = prep(scal, vecs, mats)
    y_steps = jnp.stack([slot_steps, flip(slot_steps, 1)])
    pieces, y_steps = together(pieces, y_steps)

    one.along_z(pieces[0])
    z_steps = flips_z([y_steps] * 4)
    cot_low = cotangent.astype(BF16)
    one.now, z_steps, cot_low, pieces = together(one.now, z_steps, cot_low, pieces)

    one.along_xy()
    all_steps = jnp.stack([y_steps] + z_steps)
    asked = jnp.take(step_table, all_steps, axis=0).astype(BF16)
    back = jnp.stack([asked[0]] + flips_z(asked))
    two.along_z(pieces[1])
    one.now, back = together(one.now, back)

    one.along_rest()
    given = jnp.stack([back[:, 0], flip(back[:, 1], 1)], axis=1)
    one.now, given, pieces = together(one.now, given, pieces)

    one.along_core()
    rel = given.reshape(8, given.shape[2], given.shape[3]).astype(F32)
    one.now, rel, pieces, two.now = together(one.now, rel, pieces, two.now)

    two.along_xy()
    three.along_z(pieces[2])
    w_qkv = one.done()
    normed, q, k, v, slots, vec = qkv(scal, inputs, rel, w_qkv, None, win)
    q, k, v, two.now, three.now = together(q, k, v, two.now, three.now)

    two.along_rest()
    three.along_xy()
    mixture = attend(scal, layouts, q, k, v)
    mixture, two.now, three.now = together(mixture, two.now, three.now)

    two.along_core()
    three.along_rest()
    mixture, two.now = together(mixture, two.now)

    w_two = two.done()
    attended, second = mix(scal, mixture, inputs, slots, vec, w_two, win)
    attended, second, three.now = together(attended, second, three.now)

    three.along_core()
    second, three.now = together(second, three.now)

    w_down = three.done()
    hidden, pre, up_add = mlp(scal, second, cot_low, vec, w_two, w_down, ff, r, D // 8)
    down = Sum()
    kept = wide_grad(scal, hidden, cot_low, False)
    kept, pre = together(kept, pre)

    down.along_core(*kept)
    grad, low, sums2 = second_back(scal, pre, attended, cotangent, vec, w_two, win, **at_up)
    grad, low, pre, down.now = together(grad, low, pre, down.now)

    down.along_first()
    up = Sum()
    kept = wide_grad(scal, second, pre, True, (mixture, low))
    kept, low, down.now = together(kept, low, down.now)

    down.along_second()
    up.along_core(*kept)
    halves = layouts.shape[0] // 2
    back1 = attend_back(scal, layouts, low, q, k, v, w_two, 0, halves)
    back1, down.now, up.now = together(back1, down.now, up.now)

    down.along_z()
    up.along_first()
    dq, dk, dv = attend_back(scal, layouts, low, q, k, v, w_two, halves, halves, back1)
    dq, dk, dv, down.now, up.now = together(dq, dk, dv, down.now, up.now)

    down.back()
    up.along_second()
    square = Sum()
    kept = square_grads(scal, normed, dq, dk, dv)
    kept, dq, dk, dv, down.now, up.now, hidden = together(
        kept, dq, dk, dv, down.now, up.now, hidden
    )

    square.along_core(*kept)
    up.along_z()
    part = down_out(scal, hidden, attended, vec, w_down, win, 0, halves, **at_down)
    square.now, part, dq = together(square.now, part, dq)

    square.along_first()
    input_grad, slot_sums, sums1 = first_back(
        scal, dq, dk, dv, inputs, grad, slots, vec, w_qkv, win
    )
    small = vector_sums(sums1, sums2, up_add)
    small, slot_sums, square.now, up.now, part = together(
        small, slot_sums, square.now, up.now, part
    )

    width = D // 8
    count = slot_sums.shape[0]
    own = jnp.concatenate([slot_sums, small[:8]]).reshape(-1, 8, width).swapaxes(0, 1)
    own = jnp.concatenate([own, small[8:].reshape(8, -1, width)], axis=1)
    own = jnp.stack([lax.dynamic_index_in_dim(own, f ^ j, 0, False) for j in range(8)])
    tag = jnp.zeros((8, 1, width), F32).at[:, 0, :count].set(slot_steps.astype(F32))
    own = jnp.concatenate([own, tag], axis=1)
    own = own.reshape(4, 2, *own.shape[1:])
    up.back()
    square.along_second()
    own_y = flip(own[:, 1], 1)
    part, own_y, up.now, square.now = together(part, own_y, up.now, square.now)

    square.along_z()
    block_output = down_out(
        scal, hidden, attended, vec, w_down, win, halves, halves, so_far=(part,), **at_down
    )
    own = jnp.stack([own[:, 0], own_y], axis=1)
    own_z = flips_z(own)
    half = D // 2
    down_grad = jnp.concatenate(down.done(), axis=0).astype(F32)
    square.now, own_z, down_grad, block_output = together(
        square.now, own_z, down_grad, block_output
    )

    square.back()
    own = jnp.stack([own[0]] + own_z).reshape(8, *own.shape[2:])
    parts = [own] + [flip(own, 0, j) for j in (1, 2, 3)]
    got = up.done()
    u = D // 8
    up_grad = jnp.concatenate(
        [t for m in got for t in (m[:u, :half], m[:u, half:])], axis=0
    ).astype(F32)
    out_grad = jnp.concatenate([m[u:] for m in got], axis=0).astype(F32)
    square.now, parts, up_grad, out_grad = together(square.now, parts, up_grad, out_grad)

    query_grad, key_grad, value_grad = (
        jnp.concatenate([m[j * r : (j + 1) * r] for m in square.done()], axis=0).astype(F32)
        for j in range(3)
    )
    every = jnp.stack(order_dp(parts)).reshape(-1, *own.shape[1:])
    steps = every[:, -1, :count].astype(jnp.int32).reshape(-1)
    table_grad = (
        jnp.zeros((step_table.shape[0], width), F32)
        .at[steps]
        .add(every[:, :count].reshape(-1, width))
    )
    mine = jnp.sum(every[:, count:-1], axis=0)
    return named(
        block_output, input_grad, table_grad, mine, mine[8:].reshape(-1),
        query_grad, key_grad, value_grad, out_grad, up_grad, down_grad,
    )


def solution(mesh):
    rows = P(("fsdp", "dp"), None)
    slots = P(("fsdp", "dp"))
    vector = P("fsdp")
    matrix = P("fsdp", None)
    wide = P(None, "fsdp")
    placed = (
        rows, rows, slots, slots, wide, vector, vector, matrix, vector, matrix,
        matrix, vector, matrix, vector, vector, vector, wide, vector, matrix, vector,
    )
    returned = (
        rows, rows, wide, vector, vector, matrix, vector, matrix, matrix, vector,
        matrix, vector, vector, vector, wide, vector, matrix, vector,
    )
    return jax.shard_map(
        functools.partial(on_device, (mesh.shape["fsdp"], mesh.shape["dp"])),
        mesh=mesh,
        in_specs=placed,
        out_specs=returned,
        check_vma=False,
    )
```
